32 devices in a mesh: dp: 4 (over y, x), expert: 8 (over z, core).
Axes of the slice: x: 2, y: 2, z: 4, core: 2. Of those that a mesh axis runs over, the one named last changes fastest.
Arguments:
- block_input: bfloat16 [20480, 1024], P(('dp', 'expert')), may hold values from -6 to 6
- routes: int32 [20480, 2], P(('dp', 'expert')), may hold values from 0 to 7, all different within a row; in each aligned block of 640 rows (0 to 639, 640 to 1279, ...) at most 200 rows name the same one
- item_lengths: int32 [32, 2], P(('dp', 'expert')), may hold values from 64 to 512, as said below
- w_qkv: bfloat16 [1024, 3072], replicated, may hold values from -0.1875 to 0.1875
- w_attn_out: bfloat16 [1024, 1024], replicated, may hold values from -1 to 1
- rel_table: float32 [32, 16], replicated, may hold values from -4 to 4
- gain_attn: float32 [1024], replicated, may hold values from 0.25 to 1.75
- gain_moe: float32 [1024], replicated, may hold values from 0.25 to 1.75
- w_router: bfloat16 [1024, 8], replicated, may hold values from -0.125 to 0.125
- w_gate: bfloat16 [8, 1024, 2816], P('expert'), may hold values from -0.1875 to 0.1875
- w_up: bfloat16 [8, 1024, 2816], P('expert'), may hold values from -0.1875 to 0.1875
- w_down: bfloat16 [8, 2816, 1024], P('expert'), may hold values from -0.15625 to 0.15625
- cotangent: bfloat16 [20480, 1024], P(('dp', 'expert')), may hold values from -6 to 6
Outputs:
- output: bfloat16 [20480, 1024], P(('dp', 'expert'))
- grad_input: float32 [20480, 1024], P(('dp', 'expert'))
- grad_qkv: float32 [1024, 3072], P(('dp', 'expert'))
- grad_attn_out: float32 [1024, 1024], P(('dp', 'expert'))
- grad_rel_table: float32 [512], P(('dp', 'expert'))
- grad_gain_attn: float32 [1024], P(('dp', 'expert'))
- grad_gain_moe: float32 [1024], P(('dp', 'expert'))
- grad_router: float32 [1024, 8], P(('dp', 'expert'))
- grad_gate: float32 [8, 1024, 2816], P('expert', None, 'dp')
- grad_up: float32 [8, 1024, 2816], P('expert', None, 'dp')
- grad_down: float32 [8, 2816, 1024], P('expert', None, 'dp')
The draws below stay inside these ranges and needn't reach their ends.
Inputs may be any that keep to these rules, and one draw needn't show every extreme that they name: `routes`: A row names two different experts. In each aligned block of 640 rows no expert is named by more than 200 rows, a bound that some block reaches. `item_lengths`: columns 0 to 0 lie between 256 and 512, the others between 64 and 128; both upper ends are reached.
All inputs are finite; a program needn't handle non-finite values.
Results may differ from the reference program's by a relative error of at most 0.019.
Values may be sent and summed in bfloat16 or wider, within the bound.
No kernel may reach another device: no remote copies, remote signals or barrier semaphores. Data moves between devices by JAX's collectives and lax.ppermute only.
A program may use at most 320 MiB of HBM per device.

```python
import math
from functools import partial
import jax
import jax.numpy as jnp
import numpy as np
from jax import lax

D = 1024
H = 16
DH = 64
FF = 2816
TOP = 2
BUCKETS = 32
LONG_LEN = 512
SHORT_LEN = 128
LONG_DEV = 1
SHORT_DEV = 1
TOK_DEV = 640
EXPERTS = 8
CAP = 200
TOKENS = 20480


def draw_item_lengths(key, part):
    blocks = TOKENS // TOK_DEV
    long_key, short_key = jax.random.split(jax.random.fold_in(key, 11))
    longs = jax.random.randint(long_key, (blocks, LONG_DEV), LONG_LEN // 2, LONG_LEN + 1, dtype=jnp.int32)
    shorts = jax.random.randint(short_key, (blocks, SHORT_DEV), SHORT_LEN // 2, SHORT_LEN + 1, dtype=jnp.int32)
    longs = longs.at[0, 0].set(LONG_LEN)
    shorts = shorts.at[0, 0].set(SHORT_LEN)
    return jnp.concatenate([longs, shorts], axis=1)


def strengthened(values, own_key, source, target, shards_of, factor):
    owner, partner = [(jnp.arange(values.shape[dim]) // (values.shape[dim] // shards_of)).reshape([-1 if axis == dim else 1 for axis in range(values.ndim)]) for dim in (source, target)]
    chosen = jax.random.permutation(own_key, shards_of)[partner]
    strong = (owner == chosen) | (owner == (partner + shards_of // 2) % shards_of)
    return jnp.where(strong, factor * values, values)


def levels(rng, shape, cuts, least, high):
    def one(dim, parts):
        heights = jax.random.uniform(jax.random.fold_in(jax.random.fold_in(rng, 6), dim), (parts,), jnp.float32, least / len(cuts), high / len(cuts))
        return jnp.repeat(jnp.exp(heights), shape[dim] // parts).reshape((-1,) + (1,) * (len(shape) - dim - 1))

    level = one(*cuts[0])
    for cut in cuts[1:]:
        level = level * one(*cut)
    return level


def assign_block(rng, own, number, rows, number_of, top, limit, lean):
    sequence = jax.random.permutation(rng, number_of)
    crowded, common = portions_of(number_of, rows * top, limit, lean, True), portions_of(number_of, rows * top, limit, lean, False)
    places = jnp.arange(number_of)

    def named(sizes, offset_by):
        used = int((sizes > 0).sum())
        fixed = max(1, used // 4)
        shifted = fixed + (places - fixed + offset_by * (used - fixed)) % max(1, number_of - fixed)
        return jnp.zeros((number_of,), jnp.int32).at[sequence[jnp.where(places < fixed, places, shifted)]].set(jnp.asarray(sizes, jnp.int32))

    sizes = jnp.where(number % 4 == 0, named(crowded, number // 4), named(common, number - number // 4 - 1))
    mixed = jax.random.permutation(jax.random.fold_in(own, 3), number_of)
    giver, taker = mixed[0:number_of // 2 * 2:2], mixed[1:number_of // 2 * 2:2]
    slack = jnp.minimum(sizes[giver] - 1, limit - sizes[taker]) // 2
    slack = jnp.where((giver == sequence[0]) | (taker == sequence[0]) | (sizes[taker] == 0), 0, jnp.maximum(slack, 0))
    shifted = jax.random.randint(jax.random.fold_in(own, 4), (number_of // 2,), 0, 1 << 20) % (slack + 1)
    sizes = sizes.at[giver].add(-shifted).at[taker].add(shifted)
    members = jnp.searchsorted(jnp.cumsum(sizes), jnp.arange(rows * top), side="right").astype(jnp.int32)
    listing = members.reshape(top, rows).T
    listing = listing[jax.random.permutation(jax.random.fold_in(own, 1), rows)]
    offset_by = jax.random.randint(jax.random.fold_in(own, 2), (rows, 1), 0, top)
    return jnp.take_along_axis(listing, (jnp.arange(top)[None, :] + offset_by) % top, axis=1)


def portions_of(amount, total, reach, lean, full):
    loads = [(1 << 20) // math.isqrt(standing ** lean) + 1 for standing in range(1, amount + 1)]
    largest = reach if full else min(reach, max(-(-total // amount), total * loads[0] // sum(loads)))
    least = 1 if total - largest >= amount - 1 else 0
    given, rest = [largest] + [least] * (amount - 1), total - largest - least * (amount - 1)
    while rest > 0:
        free = [i for i in range(1, amount) if given[i] < largest] or [i for i in range(1, amount) if given[i] < reach]
        pool, budget = sum([loads[i] for i in free]), rest
        for i in free:
            extra = min(reach - given[i], max(1, budget * loads[i] // pool), rest)
            given[i] = given[i] + extra
            rest = rest - extra
    return np.array(given)


def centred(own_key, dims, scale, most, cuts=(), kind=jnp.bfloat16):
    drawn = jax.random.normal(own_key, dims, jnp.float32) * scale
    if len(cuts) > 0:
        drawn = levels(own_key, dims, cuts, -0.22, 0.18) * drawn
    return jnp.clip(drawn, min=-most, max=most).astype(kind)


def bell_draw_with(own_key, dims, scale, reach, cuts, heavy, kind=jnp.bfloat16):
    values = scale * jax.random.normal(own_key, dims, jnp.float32)
    if cuts:
        values = values * levels(own_key, dims, cuts, -0.22, 0.18)
    return jnp.clip(strengthened(values, jax.random.fold_in(own_key, 3), *heavy), -reach, reach).astype(kind)


def setup_inputs(seed: int = 0) -> dict:
    arg_keys = jax.random.split(jax.random.key(seed), 14)
    block_input = bell_draw_with(arg_keys[0], (TOKENS, D), 1.0, 6.0, ((0, 32),), (0, 1, 32, 2.75))
    routes_keys = jax.random.split(jax.random.fold_in(arg_keys[1], 1), TOKENS // TOK_DEV)
    routes_turns = jax.random.permutation(jax.random.fold_in(arg_keys[1], 3), TOKENS // TOK_DEV)
    routes = jax.vmap(lambda own, number: assign_block(jax.random.fold_in(arg_keys[1], 2), own, number, TOK_DEV, EXPERTS, TOP, CAP, 2))(routes_keys, routes_turns).reshape((TOKENS, TOP))
    item_lengths = draw_item_lengths(jax.random.fold_in(arg_keys[13], 71), 0)
    w_qkv = centred(arg_keys[3], (D, 3 * H * DH), D ** -0.5, 0.1875)
    w_attn_out = centred(arg_keys[4], (H * DH, D), (D // 32) ** -0.5, 1.0)
    rel_table = centred(arg_keys[5], (BUCKETS, H), 1.0, 4.0, (), jnp.float32)
    gain_attn = jnp.clip(1.0 + 0.15 * jax.random.normal(arg_keys[6], (D,), jnp.float32), 0.25, 1.75)
    gain_moe = jnp.clip(1.0 + 0.15 * jax.random.normal(arg_keys[7], (D,), jnp.float32), 0.25, 1.75)
    w_router = centred(arg_keys[8], (D, EXPERTS), (2 * D) ** -0.5, 0.125)
    w_gate = centred(arg_keys[9], (EXPERTS, D, FF), D ** -0.5, 0.1875, ((0, 8),))
    w_up = centred(arg_keys[10], (EXPERTS, D, FF), D ** -0.5, 0.1875, ((0, 8),))
    w_down = centred(arg_keys[11], (EXPERTS, FF, D), (FF // 2) ** -0.5, 0.15625, ((0, 8),))
    cotangent = centred(arg_keys[12], (TOKENS, D), 1.0, 6.0, ((0, 32),))
    return {"block_input": block_input, "routes": routes, "item_lengths": item_lengths, "w_qkv": w_qkv, "w_attn_out": w_attn_out, "rel_table": rel_table, "gain_attn": gain_attn, "gain_moe": gain_moe, "w_router": w_router, "w_gate": w_gate, "w_up": w_up, "w_down": w_down, "cotangent": cotangent}


@jax.custom_vjp
def low(v):
    return lax.optimization_barrier(v.astype(jnp.bfloat16)).astype(jnp.float32)

@jax.custom_vjp
def low_back(v):
    return v

def low_keep(v):
    return (low(v), None)

def low_pass(kept, grad):
    return (grad,)

def back_keep(v):
    return (v, None)

def back_low(kept, grad):
    return (low(grad),)
low.defvjp(low_keep, low_pass)
low_back.defvjp(back_keep, back_low)
BOUNDS = (12, 16, 23, 32, 46, 64, 91)
EPSILON = 1e-06
HIGHEST = lax.Precision.HIGHEST

def bucket_table(length):
    places = jnp.arange(length, dtype=jnp.int32)
    offset = places[None, :] - places[:, None]
    distance = jnp.abs(offset)
    far = 8 + sum(((distance >= bound).astype(jnp.int32) for bound in BOUNDS))
    return jnp.where(distance < 8, distance, far) + 16 * (offset > 0).astype(jnp.int32)

def bucket_onehot(length, buckets):
    table = bucket_table(length)
    labels = jnp.arange(buckets, dtype=jnp.int32)
    return (table[:, :, None] == labels[None, None, :]).astype(jnp.float32)

def gaussian_unit(value):
    return 0.5 * value * (1.0 + jnp.tanh(0.7978845608028654 * (value + 0.044715 * value * value * value)))

def normalize(value, gain):
    scale = lax.rsqrt(lax.optimization_barrier(jnp.mean(value * value, axis=-1, keepdims=True)) + EPSILON)
    return value * scale * gain

def attention_core(items, lengths, w_qkv, w_attn_out, bias):
    count, length, width = items.shape
    heads = bias.shape[0]
    size = w_qkv.shape[1] // (3 * heads)
    proj = low_back(low(jnp.einsum('nld,de->nle', items, w_qkv, precision=HIGHEST)))
    proj = proj.reshape(count, length, 3, heads, size)
    query = proj[:, :, 0]
    keys = proj[:, :, 1]
    values = proj[:, :, 2]
    scores = jnp.einsum('nqhd,nkhd->nhqk', query, keys, precision=HIGHEST) * 0.125 + bias[None]
    scores = low_back(scores)
    valid = jnp.arange(length, dtype=jnp.int32)[None, :] < lengths[:, None]
    masked = jnp.where(valid[:, None, None, :], scores, -1e+30)
    highest = lax.optimization_barrier(jnp.max(masked, axis=-1, keepdims=True))
    exps = jnp.exp(masked - highest)
    probs = exps / lax.optimization_barrier(jnp.sum(exps, axis=-1, keepdims=True))
    weights = low(probs)
    mixed = jnp.einsum('nhqk,nkhd->nqhd', weights, values, precision=HIGHEST).reshape(count, length, heads * size)
    mixed = low_back(low(mixed))
    return low_back(jnp.einsum('nle,ed->nld', mixed, w_attn_out, precision=HIGHEST))

def bucket_attention(group, lengths, w_qkv, w_attn_out, rel_table):
    onehot = bucket_onehot(group.shape[2], rel_table.shape[0])
    bias = jnp.einsum('qkb,bh->hqk', onehot, rel_table, precision=HIGHEST)

    def inner(operands):
        return attention_core(operands[0], operands[1], w_qkv, w_attn_out, bias)
    return lax.map(jax.checkpoint(inner), (group, lengths))

def expert_step(operands):
    rows, gate_weight, up_weight, down_weight = operands
    gate_pre = low_back(jnp.dot(rows, gate_weight, precision=HIGHEST))
    up_pre = low_back(jnp.dot(rows, up_weight, precision=HIGHEST))
    hidden = low(gaussian_unit(gate_pre) * up_pre)
    return low_back(low(jnp.dot(hidden, down_weight, precision=HIGHEST)))

def forward(routes, item_lengths, block_input, w_qkv, w_attn_out, rel_table, gain_attn, gain_moe, w_router, w_gate, w_up, w_down):
    width = block_input.shape[1]
    blocks = block_input.shape[0] // TOK_DEV
    split_at = LONG_DEV * LONG_LEN
    attn_in = low(normalize(block_input, gain_attn))
    grouped = attn_in.reshape(blocks, TOK_DEV, width)
    long_part = grouped[:, :split_at].reshape(blocks, LONG_DEV, LONG_LEN, width)
    short_part = grouped[:, split_at:].reshape(blocks, SHORT_DEV, SHORT_LEN, width)
    long_out = bucket_attention(long_part, item_lengths[:, :LONG_DEV], w_qkv, w_attn_out, rel_table)
    short_out = bucket_attention(short_part, item_lengths[:, LONG_DEV:], w_qkv, w_attn_out, rel_table)
    attn = jnp.concatenate([long_out.reshape(blocks, split_at, width), short_out.reshape(blocks, TOK_DEV - split_at, width)], axis=1).reshape(-1, width)
    resid = block_input + attn
    moe_in = low(normalize(resid, gain_moe))
    logits = low_back(jnp.dot(moe_in, w_router, precision=HIGHEST))
    chosen = jnp.take_along_axis(logits, routes, axis=1)
    highest = lax.optimization_barrier(jnp.max(chosen, axis=1, keepdims=True))
    exps = jnp.exp(chosen - highest)
    gates = exps / lax.optimization_barrier(jnp.sum(exps, axis=1, keepdims=True))
    experts = w_router.shape[1]
    entries = routes.reshape(blocks, TOK_DEV * TOP)
    labels = jnp.arange(experts, dtype=jnp.int32)
    member = (entries[:, :, None] == labels[None, None, :]).astype(jnp.int32)
    before = jnp.cumsum(member, axis=1, dtype=jnp.int32) - member
    position = lax.optimization_barrier(jnp.sum(before * member, axis=2)).astype(jnp.int32)
    block_ids = jnp.broadcast_to(jnp.arange(blocks, dtype=jnp.int32)[:, None], entries.shape)
    token_ids = block_ids * TOK_DEV + jnp.arange(TOK_DEV * TOP, dtype=jnp.int32)[None, :] // TOP
    table = jnp.zeros((blocks, experts, CAP), jnp.int32).at[block_ids, entries, position].set(token_ids + 1)
    padded = jnp.concatenate([jnp.zeros((1, width), jnp.float32), moe_in], axis=0)
    sent = low_back(padded[table])
    by_expert = jnp.transpose(sent, (1, 0, 2, 3)).reshape(experts, blocks * CAP, width)
    results = lax.map(jax.checkpoint(expert_step), (by_expert, w_gate, w_up, w_down))
    returned = jnp.transpose(results.reshape(experts, blocks, CAP, width), (1, 0, 2, 3))
    picked = returned[block_ids, entries, position].reshape(-1, TOP, width)
    mixture = lax.optimization_barrier(jnp.sum(gates[:, :, None] * picked, axis=1))
    return resid + mixture

def reference(block_input, routes, item_lengths, w_qkv, w_attn_out, rel_table, gain_attn, gain_moe, w_router, w_gate, w_up, w_down, cotangent):
    floats = (block_input.astype(jnp.float32), w_qkv.astype(jnp.float32), w_attn_out.astype(jnp.float32), rel_table, gain_attn, gain_moe, w_router.astype(jnp.float32), w_gate.astype(jnp.float32), w_up.astype(jnp.float32), w_down.astype(jnp.float32))
    result, pullback = jax.vjp(partial(forward, routes, item_lengths), *floats)
    grads = pullback(cotangent.astype(jnp.float32))
    return (result.astype(jnp.bfloat16), grads[0], grads[1], grads[2], grads[3].reshape(-1), grads[4], grads[5], grads[6], grads[7], grads[8], grads[9])
```

```python
import jax
import jax.numpy as jnp
from jax import lax
from jax.experimental import pallas as pl
from jax.experimental.pallas import tpu as pltpu
from jax.sharding import PartitionSpec as P

TOP = 2
LONG_LEN = 512
SHORT_LEN = 128
TOK_DEV = 640
BOUNDS = (12, 16, 23, 32, 46, 64, 91)
EPSILON = 1e-06
HIGHEST = lax.Precision.HIGHEST
TILE = 128
FT = 256
NEG = -1e30
NN = (((1,), (0,)), ((), ()))
NT = (((1,), (1,)), ((), ()))
TN = (((0,), (0,)), ((), ()))
CURVE = 0.7978845608028654
CUBE = 0.044715


def dot(a, b, dims=NN):
    return lax.dot_general(a, b, dims, preferred_element_type=jnp.float32)


def normalize_forward(value, gain):
    scale = lax.rsqrt(jnp.mean(value * value, axis=-1, keepdims=True) + EPSILON)
    unit = value * scale
    return (unit * gain, unit, scale)


def normalize_backward(grad, unit, scale, gain):
    gain_grad = jnp.sum(grad * unit, axis=0)
    along = grad * gain
    inner = jnp.mean(along * unit, axis=-1, keepdims=True)
    return (scale * (along - unit * inner), gain_grad)


def bias_strip(bias_row):
    wide = jnp.broadcast_to(bias_row, (TILE, bias_row.shape[1]))
    return pltpu.roll(wide, 0, 1, stride=1, stride_axis=0)


def bias_tile(strip, bias_row, step):
    if abs(step) <= 1:
        start = 2 * TILE - step * TILE
        return strip[:, start : start + TILE]
    last = bias_row.shape[1] - 1
    return bias_row[:, 0:1] if step > 0 else bias_row[:, last : last + 1]


def items_of(tokens, lengths_ref):
    return ((0, LONG_LEN, lengths_ref[0, 0], LONG_LEN // 2), (LONG_LEN, tokens, lengths_ref[0, 1], SHORT_LEN // 2))


def attention_forward_kernel(lengths_ref, bias_ref, q_ref, k_ref, v_ref, mixed_ref, stat_ref, score_ref, exp_ref):
    tokens, lanes = q_ref.shape
    size = lanes // 2
    lane = lax.broadcasted_iota(jnp.int32, (1, lanes), 1)
    values_t = v_ref[...].T
    for start, stop, visible, sure in items_of(tokens, lengths_ref):
        length = stop - start
        count = length // TILE
        outs = []
        for head in range(2):
            bias_row = bias_ref[0, head : head + 1, :]
            strip = bias_strip(bias_row)
            own = (lane >= head * size) & (lane < (head + 1) * size)
            query = jnp.where(own, q_ref[start:stop, :] * 0.125, 0.0).astype(jnp.bfloat16)
            score_ref[0:length, 0:length] = dot(k_ref[start:stop, :], query, NT)
            totals = []
            for col in range(count):
                cols = slice(col * TILE, (col + 1) * TILE)
                top = None
                for row in range(count):
                    rows = slice(row * TILE, (row + 1) * TILE)
                    tile = score_ref[rows, cols] + bias_tile(strip, bias_row, row - col)
                    if (row + 1) * TILE > sure:
                        place = lax.broadcasted_iota(jnp.int32, (TILE, 1), 0) + row * TILE
                        tile = jnp.where(place < visible, tile, NEG)
                    score_ref[rows, cols] = tile
                    peak = jnp.max(tile, axis=0, keepdims=True)
                    top = peak if top is None else jnp.maximum(top, peak)
                total = jnp.zeros((1, TILE), jnp.float32)
                for row in range(count):
                    rows = slice(row * TILE, (row + 1) * TILE)
                    tile = jnp.exp(score_ref[rows, cols] - top)
                    total = total + jnp.sum(tile, axis=0, keepdims=True)
                    exp_ref[rows, cols] = tile.astype(jnp.bfloat16)
                totals.append(total)
                stat_ref[0, head : head + 1, start + col * TILE : start + (col + 1) * TILE] = top + jnp.log(total)
            total = jnp.concatenate(totals, axis=1)
            out = dot(values_t[head * size : (head + 1) * size, start:stop], exp_ref[0:length, 0:length])
            outs.append(out / total)
        mixed_ref[start:stop, :] = jnp.concatenate(outs, axis=0).T.astype(jnp.bfloat16)


def attention_forward(lengths, bias, proj):
    tokens, width = proj.shape[0], proj.shape[1] // 3
    lanes = TILE
    pairs = width // lanes
    return pl.pallas_call(
        attention_forward_kernel,
        grid=(pairs,),
        in_specs=[
            pl.BlockSpec(memory_space=pltpu.SMEM),
            pl.BlockSpec((1, 2, bias.shape[2]), lambda p: (p, 0, 0)),
            pl.BlockSpec((tokens, lanes), lambda p: (0, p)),
            pl.BlockSpec((tokens, lanes), lambda p: (0, pairs + p)),
            pl.BlockSpec((tokens, lanes), lambda p: (0, 2 * pairs + p)),
        ],
        out_specs=[
            pl.BlockSpec((tokens, lanes), lambda p: (0, p)),
            pl.BlockSpec((1, 2, tokens), lambda p: (p, 0, 0)),
        ],
        out_shape=[
            jax.ShapeDtypeStruct((tokens, width), jnp.bfloat16),
            jax.ShapeDtypeStruct((pairs, 2, tokens), jnp.float32),
        ],
        scratch_shapes=[pltpu.VMEM((LONG_LEN, LONG_LEN), jnp.float32), pltpu.VMEM((LONG_LEN, LONG_LEN), jnp.bfloat16)],
        name="attention_forward",
    )(lengths, bias, proj, proj, proj)


def attention_backward_kernel(
    lengths_ref, bias_ref, stat_ref, q_ref, k_ref, v_ref, mixed_ref, grad_ref, proj_ref, table_ref,
    score_ref, slope_ref, weight_ref, change_ref,
):
    tokens, lanes = q_ref.shape
    size = lanes // 2
    lane = lax.broadcasted_iota(jnp.int32, (1, lanes), 1)
    keys_t = k_ref[...].T
    product = (grad_ref[...].astype(jnp.float32) * mixed_ref[...].astype(jnp.float32)).T
    table_ref[...] = jnp.zeros_like(table_ref)
    for start, stop, visible, sure in items_of(tokens, lengths_ref):
        length = stop - start
        count = length // TILE
        query_grads, key_grads, value_grads = [], [], []
        for head in range(2):
            bias_row = bias_ref[0, head : head + 1, :]
            strip = bias_strip(bias_row)
            own = (lane >= head * size) & (lane < (head + 1) * size)
            query = jnp.where(own, q_ref[start:stop, :] * 0.125, 0.0).astype(jnp.bfloat16)
            grad = jnp.where(own, grad_ref[start:stop, :], 0.0).astype(jnp.bfloat16)
            score_ref[0:length, 0:length] = dot(k_ref[start:stop, :], query, NT)
            slope_ref[0:length, 0:length] = dot(v_ref[start:stop, :], grad, NT)
            inner = jnp.sum(product[head * size : (head + 1) * size, start:stop], axis=0, keepdims=True)
            sums = {-1: None, 0: None, 1: None}
            far = {-1: None, 1: None}
            for col in range(count):
                cols = slice(col * TILE, (col + 1) * TILE)
                base = stat_ref[0, head : head + 1, start + col * TILE : start + (col + 1) * TILE]
                middle = inner[:, cols]
                for row in range(count):
                    rows = slice(row * TILE, (row + 1) * TILE)
                    step = row - col
                    tile = score_ref[rows, cols] + (bias_tile(strip, bias_row, step) - base)
                    if (row + 1) * TILE > sure:
                        place = lax.broadcasted_iota(jnp.int32, (TILE, 1), 0) + row * TILE
                        tile = jnp.where(place < visible, tile, NEG)
                    tile = jnp.exp(tile)
                    weight_ref[rows, cols] = tile.astype(jnp.bfloat16)
                    tile = tile * (slope_ref[rows, cols] - middle)
                    change_ref[rows, cols] = tile.astype(jnp.bfloat16)
                    if abs(step) <= 1:
                        sums[step] = tile if sums[step] is None else sums[step] + tile
                    else:
                        side = 1 if step > 0 else -1
                        part = jnp.sum(tile, axis=0, keepdims=True)
                        far[side] = part if far[side] is None else far[side] + part
            for step, value in sums.items():
                if value is not None:
                    at = TILE - step * TILE
                    table_ref[0, head, 0:TILE, at : at + TILE] += value
            for side, value in far.items():
                if value is not None:
                    at = TILE - side * TILE
                    table_ref[0, head, TILE : TILE + 1, at : at + TILE] = value
            value_grads.append(dot(weight_ref[0:length, 0:length], grad))
            key_grads.append(dot(change_ref[0:length, 0:length], query))
            query_grads.append(dot(keys_t[head * size : (head + 1) * size, start:stop], change_ref[0:length, 0:length]))
        proj_ref[0, start:stop, :] = (jnp.concatenate(query_grads, axis=0).T * 0.125).astype(jnp.bfloat16)
        proj_ref[1, start:stop, :] = (key_grads[0] + key_grads[1]).astype(jnp.bfloat16)
        proj_ref[2, start:stop, :] = (value_grads[0] + value_grads[1]).astype(jnp.bfloat16)


def attention_backward(lengths, bias, stat, proj, mixed, grad):
    tokens, width = mixed.shape
    lanes = TILE
    pairs = width // lanes
    return pl.pallas_call(
        attention_backward_kernel,
        grid=(pairs,),
        in_specs=[
            pl.BlockSpec(memory_space=pltpu.SMEM),
            pl.BlockSpec((1, 2, bias.shape[2]), lambda p: (p, 0, 0)),
            pl.BlockSpec((1, 2, tokens), lambda p: (p, 0, 0)),
            pl.BlockSpec((tokens, lanes), lambda p: (0, p)),
            pl.BlockSpec((tokens, lanes), lambda p: (0, pairs + p)),
            pl.BlockSpec((tokens, lanes), lambda p: (0, 2 * pairs + p)),
            pl.BlockSpec((tokens, lanes), lambda p: (0, p)),
            pl.BlockSpec((tokens, lanes), lambda p: (0, p)),
        ],
        out_specs=[
            pl.BlockSpec((3, tokens, lanes), lambda p: (0, 0, p)),
            pl.BlockSpec((1, 2, TILE + 8, 3 * TILE), lambda p: (p, 0, 0, 0)),
        ],
        out_shape=[
            jax.ShapeDtypeStruct((3, tokens, width), jnp.bfloat16),
            jax.ShapeDtypeStruct((pairs, 2, TILE + 8, 3 * TILE), jnp.float32),
        ],
        scratch_shapes=[
            pltpu.VMEM((LONG_LEN, LONG_LEN), jnp.float32),
            pltpu.VMEM((LONG_LEN, LONG_LEN), jnp.float32),
            pltpu.VMEM((LONG_LEN, LONG_LEN), jnp.bfloat16),
            pltpu.VMEM((LONG_LEN, LONG_LEN), jnp.bfloat16),
        ],
        name="attention_backward",
    )(lengths, bias, stat, proj, proj, proj, mixed, grad)


def bucket_of(offset):
    distance = jnp.abs(offset)
    far = 8 + sum(((distance >= bound).astype(jnp.int32) for bound in BOUNDS))
    return jnp.where(distance < 8, distance, far) + 16 * (offset > 0).astype(jnp.int32)


def bias_rows(rel_table):
    bucket = bucket_of(2 * TILE - jnp.arange(4 * TILE, dtype=jnp.int32))
    onehot = (bucket[:, None] == jnp.arange(rel_table.shape[0], dtype=jnp.int32)[None, :]).astype(jnp.float32)
    return jnp.einsum("xb,bh->hx", onehot, rel_table, precision=HIGHEST).reshape(-1, 2, 4 * TILE)


def table_sums(tiles, buckets):
    row = jnp.arange(TILE + 8, dtype=jnp.int32)[:, None]
    col = jnp.arange(3 * TILE, dtype=jnp.int32)[None, :]
    near = bucket_of(row - col + TILE)
    far = jnp.where(col < TILE, buckets - 1, buckets // 2 - 1)
    bucket = jnp.where(row < TILE, near, far)
    onehot = (bucket[:, :, None] == jnp.arange(buckets, dtype=jnp.int32)).astype(jnp.float32)
    return jnp.einsum("ghrc,rcb->bgh", tiles, onehot, precision=HIGHEST).reshape(buckets, -1)


def expert_kernel(x_ref, slope_ref, wg_ref, wu_ref, hidden_ref, gate_ref, up_ref, pair_ref, dots_ref, acc_ref, *, parts):
    step = pl.program_id(0)
    rows = x_ref.shape[0] // parts

    @pl.when(step == 0)
    def _():
        acc_ref[...] = jnp.zeros_like(acc_ref)
        dots_ref[...] = jnp.zeros_like(dots_ref)

    for part in range(parts):
        span = slice(part * rows, (part + 1) * rows)
        x = x_ref[span, :]
        gate = dot(x, wg_ref[...])
        up = dot(x, wu_ref[...])
        slope = slope_ref[span, :].astype(jnp.float32)
        square = gate * gate
        turn = jnp.tanh(gate * (CURVE + (CURVE * CUBE) * square))
        rise = 0.5 + 0.5 * turn
        unit = gate * rise
        bend = rise + (0.5 * gate) * (1.0 - turn * turn) * (CURVE + (3 * CURVE * CUBE) * square)
        hidden = (unit * up).astype(jnp.bfloat16)
        hidden_ref[span, :] = hidden
        both = hidden.astype(jnp.float32) * slope
        dots_ref[span, :] += both[:, 0:TILE] + both[:, TILE : 2 * TILE]
        gate_grad = (slope * up * bend).astype(jnp.bfloat16)
        up_grad = (slope * unit).astype(jnp.bfloat16)
        gate_ref[span, :] = gate_grad
        up_ref[span, :] = up_grad
        acc_ref[span, :] += dot(gate_grad, wg_ref[...], NT) + dot(up_grad, wu_ref[...], NT)

    @pl.when(step == pl.num_programs(0) - 1)
    def _():
        pair_ref[...] = acc_ref[...].astype(jnp.bfloat16)


def expert_rows(x, slope, wg, wu, parts=4):
    n, d = x.shape
    f = wg.shape[1]
    tile = pl.BlockSpec((n, FT), lambda i: (0, i))
    weight = pl.BlockSpec((d, FT), lambda i: (0, i))
    whole = pl.BlockSpec((n, d), lambda i: (0, 0))
    return pl.pallas_call(
        lambda *refs: expert_kernel(*refs, parts=parts),
        grid=(f // FT,),
        in_specs=[whole, tile, weight, weight],
        out_specs=[tile, tile, tile, whole, pl.BlockSpec((n, TILE), lambda i: (0, 0))],
        out_shape=[jax.ShapeDtypeStruct((n, f), jnp.bfloat16)] * 3
        + [jax.ShapeDtypeStruct((n, d), jnp.bfloat16), jax.ShapeDtypeStruct((n, TILE), jnp.float32)],
        scratch_shapes=[pltpu.VMEM((n, d), jnp.float32)],
        name="expert_rows",
    )(x, slope, wg, wu)


def slope_kernel(u_ref, wd_ref, out_ref):
    out_ref[...] = dot(u_ref[...], wd_ref[...], NT).astype(jnp.bfloat16)


def slope_rows(u, wd):
    n, d = u.shape
    f = wd.shape[0]
    return pl.pallas_call(
        slope_kernel,
        grid=(f // FT,),
        in_specs=[pl.BlockSpec((n, d), lambda i: (0, 0)), pl.BlockSpec((FT, d), lambda i: (i, 0))],
        out_specs=pl.BlockSpec((n, FT), lambda i: (0, i)),
        out_shape=jax.ShapeDtypeStruct((n, f), jnp.bfloat16),
        name="slope_rows",
    )(u, wd)


def down_kernel(h_ref, u_ref, out_ref):
    out_ref[...] = dot(h_ref[...], u_ref[...], TN).astype(jnp.bfloat16)


def down_grads(h, u):
    n, f = h.shape
    d = u.shape[1]
    return pl.pallas_call(
        down_kernel,
        grid=(f // FT,),
        in_specs=[pl.BlockSpec((n, FT), lambda i: (0, i)), pl.BlockSpec((n, d), lambda i: (0, 0))],
        out_specs=pl.BlockSpec((FT, d), lambda i: (i, 0)),
        out_shape=jax.ShapeDtypeStruct((f, d), jnp.bfloat16),
        name="down_grads",
    )(h, u)


def gate_up_kernel(g_ref, p_ref, x_ref, out_ref):
    d = x_ref.shape[1]
    out_ref[:, 0:d] = dot(g_ref[...], x_ref[...], TN).astype(jnp.bfloat16)
    out_ref[:, d : 2 * d] = dot(p_ref[...], x_ref[...], TN).astype(jnp.bfloat16)


def gate_up_grads(g, p, x):
    n, f = g.shape
    d = x.shape[1]
    tile = pl.BlockSpec((n, FT), lambda i: (0, i))
    return pl.pallas_call(
        gate_up_kernel,
        grid=(f // FT,),
        in_specs=[tile, tile, pl.BlockSpec((n, d), lambda i: (0, 0))],
        out_specs=pl.BlockSpec((FT, 2 * d), lambda i: (i, 0)),
        out_shape=jax.ShapeDtypeStruct((f, 2 * d), jnp.bfloat16),
        name="gate_up_grads",
    )(g, p, x)


def on_device(
    block_input,
    routes,
    item_lengths,
    w_qkv,
    w_attn_out,
    rel_table,
    gain_attn,
    gain_moe,
    w_router,
    w_gate,
    w_up,
    w_down,
    cotangent,
):
    tokens, width = block_input.shape
    experts = w_router.shape[1]
    capacity = TOK_DEV * TOP * 5 // (4 * experts)
    buckets = rel_table.shape[0]
    slots = experts * capacity
    ways = lax.axis_size("expert")
    copies = lax.axis_size("dp")
    core = lax.axis_index("expert") % 2
    labels = jnp.arange(experts, dtype=jnp.int32)
    picks = [routes[:, rank : rank + 1] == labels[None, :] for rank in range(TOP)]
    named = (picks[0] | picks[1]).astype(jnp.bfloat16)
    ticks = jnp.arange(tokens, dtype=jnp.int32)
    earlier = (ticks[:, None] > ticks[None, :]).astype(jnp.bfloat16)
    count = dot(earlier, named)
    starts = (labels * capacity).astype(jnp.float32)
    target = [
        jnp.sum(jnp.where(pick, count + starts[None, :], 0.0), axis=1, keepdims=True).astype(jnp.int32)
        for pick in picks
    ]
    places = jnp.arange(slots, dtype=jnp.int32)
    routing = [(target[rank] == places[None, :]) for rank in range(TOP)]
    either = (routing[0] | routing[1]).astype(jnp.bfloat16)

    def pack(rows):
        return dot(either, rows, TN).astype(jnp.bfloat16)

    def exchange(rows):
        shape = rows.shape
        return lax.all_to_all(
            rows.reshape((experts, capacity) + shape[1:]), "expert", split_axis=0, concat_axis=0, tiled=True
        ).reshape(shape)

    packed = pack(cotangent)
    packed, block_input = lax.optimization_barrier((packed, block_input))
    raw = exchange(packed)
    inputs = block_input.astype(jnp.float32)
    normed, unit_one, scale_one = normalize_forward(inputs, gain_attn)
    attn_in = normed.astype(jnp.bfloat16)
    bias = bias_rows(rel_table)
    proj = dot(attn_in, w_qkv).astype(jnp.bfloat16)
    mixed, stat = attention_forward(item_lengths, bias, proj)
    attn = dot(mixed, w_attn_out)
    resid = inputs + attn
    second, unit_two, scale_two = normalize_forward(resid, gain_moe)
    moe_in = second.astype(jnp.bfloat16)
    packed = pack(moe_in)
    packed, raw = lax.optimization_barrier((packed, raw))
    rows = exchange(packed)
    logits = dot(moe_in, w_router)
    chosen = jnp.stack([jnp.sum(jnp.where(pick, logits, 0.0), axis=1) for pick in picks], axis=1)
    highest = jnp.max(chosen, axis=1, keepdims=True)
    exps = jnp.exp(chosen - highest)
    gates = exps / jnp.sum(exps, axis=1, keepdims=True)
    gated = jnp.where(routing[0], gates[:, 0:1], 0.0) + jnp.where(routing[1], gates[:, 1:2], 0.0)
    slot_gates = exchange(jnp.sum(gated, axis=0))[:, None]
    gated = gated.astype(jnp.bfloat16)
    gate_weight, up_weight, down_weight = w_gate[0], w_up[0], w_down[0]
    slope = slope_rows(raw, down_weight)
    hidden, gate_pre_grad, up_pre_grad, pair_grad, dots = expert_rows(rows, slope, gate_weight, up_weight)
    back = exchange(pair_grad)
    slot_dots = exchange(jnp.sum(dots, axis=1))[None, :]
    gated_raw = (raw.astype(jnp.float32) * slot_gates).astype(jnp.bfloat16)
    gated_rows = (rows.astype(jnp.float32) * slot_gates).astype(jnp.bfloat16)
    down_grad = down_grads(hidden, gated_raw)
    down_sum = lax.psum_scatter(down_grad, "dp", scatter_dimension=1, tiled=True)
    gate_up_grad = gate_up_grads(gate_pre_grad, up_pre_grad, gated_rows)
    gate_up_sum = lax.psum_scatter(gate_up_grad, "dp", scatter_dimension=0, tiled=True)
    result = dot(hidden, down_weight).astype(jnp.bfloat16)
    back, result, down_grad, gate_up_grad = lax.optimization_barrier((back, result, down_grad, gate_up_grad))
    returned = exchange(result)

    def halve(grad):
        parts = grad.reshape(copies, ways // 2, 2, -1, grad.shape[1])
        away = lax.dynamic_index_in_dim(parts, 1 - core, 2, keepdims=False).astype(jnp.bfloat16)
        mine = lax.dynamic_index_in_dim(parts, core, 2, keepdims=False)
        other = lax.ppermute(away, "expert", [(k, k ^ 1) for k in range(ways)])
        return (mine + other.astype(jnp.float32)).astype(jnp.bfloat16)

    def over_all(grad):
        half = halve(grad)
        half = lax.all_to_all(half, "dp", split_axis=0, concat_axis=0, tiled=True)
        part = jnp.sum(half.astype(jnp.float32), axis=0).astype(jnp.bfloat16)
        groups = [list(range(0, ways, 2)), list(range(1, ways, 2))]
        part = lax.all_to_all(
            part, "expert", split_axis=0, concat_axis=0, axis_index_groups=groups, tiled=True
        )
        return jnp.sum(part.astype(jnp.float32), axis=0)

    gate_grads = [jnp.sum(jnp.where(routing[rank], slot_dots, 0.0), axis=1) for rank in range(TOP)]
    average = gates[:, 0] * gate_grads[0] + gates[:, 1] * gate_grads[1]
    dlogits = jnp.zeros_like(logits)
    for rank in range(TOP):
        logit_grad = gates[:, rank] * (gate_grads[rank] - average)
        dlogits = dlogits + jnp.where(picks[rank], logit_grad[:, None], 0.0)
    dlogits = dlogits.astype(jnp.bfloat16)
    router_grad = dot(moe_in, dlogits, TN)
    moe_in_grad = dot(dlogits, w_router, NT) + dot(gated, back)
    upstream = cotangent.astype(jnp.float32)
    resid_norm_grad, gain_moe_grad = normalize_backward(moe_in_grad, unit_two, scale_two, gain_moe)
    resid_grad = upstream + resid_norm_grad
    attn_grad = resid_grad.astype(jnp.bfloat16)
    out_weight_sum = over_all(dot(mixed, attn_grad, TN))
    mixed_grad = dot(attn_grad, w_attn_out, NT).astype(jnp.bfloat16)
    proj_grad, tiles = attention_backward(item_lengths, bias, stat, proj, mixed, mixed_grad)
    table_grad = table_sums(tiles, buckets)
    qkv_grad = jnp.concatenate([dot(attn_in, proj_grad[k], TN) for k in range(3)], axis=1)
    qkv_sum = over_all(qkv_grad)
    attn_in_grad = sum(dot(proj_grad[k], w_qkv[:, k * width : (k + 1) * width], NT) for k in range(3))
    input_norm_grad, gain_attn_grad = normalize_backward(attn_in_grad, unit_one, scale_one, gain_attn)
    input_grad = resid_grad + input_norm_grad
    output = (resid + dot(gated, returned)).astype(jnp.bfloat16)
    devices = copies * ways
    small = (table_grad.reshape(-1), gain_attn_grad, gain_moe_grad, router_grad)
    sizes = [part.size // devices for part in small]
    together = jnp.concatenate([part.reshape(devices, -1) for part in small], axis=1)
    together = lax.all_to_all(together, ("dp", "expert"), split_axis=0, concat_axis=0, tiled=True)
    together = jnp.sum(together, axis=0)
    at = [sum(sizes[:k]) for k in range(5)]
    table_sum, attn_sum, moe_sum, router_sum = [together[at[k] : at[k + 1]] for k in range(4)]
    return (
        output,
        input_grad,
        qkv_sum,
        out_weight_sum,
        table_sum,
        attn_sum,
        moe_sum,
        router_sum.reshape(-1, experts),
        gate_up_sum[:, :width].astype(jnp.float32).T[None],
        gate_up_sum[:, width:].astype(jnp.float32).T[None],
        down_sum.astype(jnp.float32)[None],
    )


def solution(mesh):
    return jax.shard_map(
        on_device,
        mesh=mesh,
        in_specs=(
            P(("dp", "expert"), None),
            P(("dp", "expert"), None),
            P(("dp", "expert"), None),
            P(),
            P(),
            P(),
            P(),
            P(),
            P(),
            P("expert", None, None),
            P("expert", None, None),
            P("expert", None, None),
            P(("dp", "expert"), None),
        ),
        out_specs=(
            P(("dp", "expert"), None),
            P(("dp", "expert"), None),
            P(("dp", "expert"), None),
            P(("dp", "expert"), None),
            P(("dp", "expert")),
            P(("dp", "expert")),
            P(("dp", "expert")),
            P(("dp", "expert"), None),
            P("expert", None, "dp"),
            P("expert", None, "dp"),
            P("expert", None, "dp"),
        ),
        check_vma=False,
    )
```

```python
import jax
import jax.numpy as jnp
from jax import lax
from jax.experimental import pallas as pl
from jax.experimental.pallas import tpu as pltpu
from jax.sharding import PartitionSpec as P

TOP = 2
LONG_LEN = 512
SHORT_LEN = 128
TOK_DEV = 640
BOUNDS = (12, 16, 23, 32, 46, 64, 91)
EPSILON = 1e-06
HIGHEST = lax.Precision.HIGHEST
TILE = 128
FT = 256
NEG = -1e30
NN = (((1,), (0,)), ((), ()))
NT = (((1,), (1,)), ((), ()))
TN = (((0,), (0,)), ((), ()))
CURVE = 0.7978845608028654
CUBE = 0.044715
EXTRA = 8
SMALL = pl.CostEstimate(flops=1 << 20, bytes_accessed=1 << 16, transcendentals=0)
MEDIUM = pl.CostEstimate(flops=230 * 10**9, bytes_accessed=1 << 16, transcendentals=0)
LARGE = pl.CostEstimate(flops=1 << 38, bytes_accessed=1 << 28, transcendentals=0)


def dot(a, b, dims=NN):
    return lax.dot_general(a, b, dims, preferred_element_type=jnp.float32)


def normalize_forward(value, gain):
    scale = lax.rsqrt(jnp.mean(value * value, axis=-1, keepdims=True) + EPSILON)
    unit = value * scale
    return (unit * gain, unit, scale)


def normalize_backward(grad, unit, scale, gain):
    gain_grad = jnp.sum(grad * unit, axis=0)
    along = grad * gain
    inner = jnp.mean(along * unit, axis=-1, keepdims=True)
    return (scale * (along - unit * inner), gain_grad)


def bias_strip(bias_row):
    wide = jnp.broadcast_to(bias_row, (TILE, bias_row.shape[1]))
    return pltpu.roll(wide, 0, 1, stride=1, stride_axis=0)


def bias_tile(strip, bias_row, step):
    if abs(step) <= 1:
        start = 2 * TILE - step * TILE
        return strip[:, start : start + TILE]
    last = bias_row.shape[1] - 1
    return bias_row[:, 0:1] if step > 0 else bias_row[:, last : last + 1]


def items_of(tokens, lengths_ref):
    return ((0, LONG_LEN, lengths_ref[0, 0], LONG_LEN // 2), (LONG_LEN, tokens, lengths_ref[0, 1], SHORT_LEN // 2))


def attention_forward_kernel(lengths_ref, bias_ref, q_ref, k_ref, v_ref, mixed_ref, stat_ref, score_ref, exp_ref):
    tokens, lanes = q_ref.shape
    size = lanes // 2
    lane = lax.broadcasted_iota(jnp.int32, (1, lanes), 1)
    values_t = v_ref[...].T
    for start, stop, visible, sure in items_of(tokens, lengths_ref):
        length = stop - start
        count = length // TILE
        outs = []
        for head in range(2):
            bias_row = bias_ref[0, head : head + 1, :]
            strip = bias_strip(bias_row)
            own = (lane >= head * size) & (lane < (head + 1) * size)
            query = jnp.where(own, q_ref[start:stop, :] * 0.125, 0.0).astype(jnp.bfloat16)
            score_ref[0:length, 0:length] = dot(k_ref[start:stop, :], query, NT)
            totals = []
            for col in range(count):
                cols = slice(col * TILE, (col + 1) * TILE)
                top = None
                for row in range(count):
                    rows = slice(row * TILE, (row + 1) * TILE)
                    tile = score_ref[rows, cols] + bias_tile(strip, bias_row, row - col)
                    if (row + 1) * TILE > sure:
                        place = lax.broadcasted_iota(jnp.int32, (TILE, 1), 0) + row * TILE
                        tile = jnp.where(place < visible, tile, NEG)
                    score_ref[rows, cols] = tile
                    peak = jnp.max(tile, axis=0, keepdims=True)
                    top = peak if top is None else jnp.maximum(top, peak)
                total = jnp.zeros((1, TILE), jnp.float32)
                for row in range(count):
                    rows = slice(row * TILE, (row + 1) * TILE)
                    tile = jnp.exp(score_ref[rows, cols] - top)
                    total = total + jnp.sum(tile, axis=0, keepdims=True)
                    exp_ref[rows, cols] = tile.astype(jnp.bfloat16)
                totals.append(total)
                stat_ref[0, head : head + 1, start + col * TILE : start + (col + 1) * TILE] = top + jnp.log(total)
            total = jnp.concatenate(totals, axis=1)
            out = dot(values_t[head * size : (head + 1) * size, start:stop], exp_ref[0:length, 0:length])
            outs.append(out / total)
        mixed_ref[start:stop, :] = jnp.concatenate(outs, axis=0).T.astype(jnp.bfloat16)


def attention_forward(lengths, bias, proj):
    tokens, width = proj.shape[0], proj.shape[1] // 3
    lanes = TILE
    pairs = width // lanes
    return pl.pallas_call(
        attention_forward_kernel,
        grid=(pairs,),
        in_specs=[
            pl.BlockSpec(memory_space=pltpu.SMEM),
            pl.BlockSpec((1, 2, bias.shape[2]), lambda p: (p, 0, 0)),
            pl.BlockSpec((tokens, lanes), lambda p: (0, p)),
            pl.BlockSpec((tokens, lanes), lambda p: (0, pairs + p)),
            pl.BlockSpec((tokens, lanes), lambda p: (0, 2 * pairs + p)),
        ],
        out_specs=[
            pl.BlockSpec((tokens, lanes), lambda p: (0, p)),
            pl.BlockSpec((1, 2, tokens), lambda p: (p, 0, 0)),
        ],
        out_shape=[
            jax.ShapeDtypeStruct((tokens, width), jnp.bfloat16),
            jax.ShapeDtypeStruct((pairs, 2, tokens), jnp.float32),
        ],
        scratch_shapes=[pltpu.VMEM((LONG_LEN, LONG_LEN), jnp.float32), pltpu.VMEM((LONG_LEN, LONG_LEN), jnp.bfloat16)],
        cost_estimate=SMALL,
        name="attention_forward",
    )(lengths, bias, proj, proj, proj)


def attention_backward_kernel(
    lengths_ref, bias_ref, stat_ref, q_ref, k_ref, v_ref, mixed_ref, grad_ref, proj_ref, table_ref,
    score_ref, slope_ref, weight_ref, change_ref, stage_ref, done_ref,
):
    pair = pl.program_id(0)
    pairs = pl.num_programs(0)
    slot = pair % 2

    def copy(part, step):
        at = pl.multiple_of((part * pairs + step) * TILE, TILE)
        return pltpu.make_async_copy(
            stage_ref.at[step % 2, part], proj_ref.at[:, pl.ds(at, TILE)], done_ref.at[step % 2, part]
        )

    @pl.when(pair >= 2)
    def _():
        for part in range(3):
            copy(part, pair - 2).wait()

    tokens, lanes = q_ref.shape
    size = lanes // 2
    lane = lax.broadcasted_iota(jnp.int32, (1, lanes), 1)
    keys_t = k_ref[...].T
    product = (grad_ref[...].astype(jnp.float32) * mixed_ref[...].astype(jnp.float32)).T
    table_ref[...] = jnp.zeros_like(table_ref)
    for start, stop, visible, sure in items_of(tokens, lengths_ref):
        length = stop - start
        count = length // TILE
        query_grads, key_grads, value_grads = [], [], []
        for head in range(2):
            bias_row = bias_ref[0, head : head + 1, :]
            strip = bias_strip(bias_row)
            own = (lane >= head * size) & (lane < (head + 1) * size)
            query = jnp.where(own, q_ref[start:stop, :] * 0.125, 0.0).astype(jnp.bfloat16)
            grad = jnp.where(own, grad_ref[start:stop, :], 0.0).astype(jnp.bfloat16)
            score_ref[0:length, 0:length] = dot(k_ref[start:stop, :], query, NT)
            slope_ref[0:length, 0:length] = dot(v_ref[start:stop, :], grad, NT)
            inner = jnp.sum(product[head * size : (head + 1) * size, start:stop], axis=0, keepdims=True)
            sums = {-1: None, 0: None, 1: None}
            far = {-1: None, 1: None}
            for col in range(count):
                cols = slice(col * TILE, (col + 1) * TILE)
                base = stat_ref[0, head : head + 1, start + col * TILE : start + (col + 1) * TILE]
                middle = inner[:, cols]
                for row in range(count):
                    rows = slice(row * TILE, (row + 1) * TILE)
                    step = row - col
                    tile = score_ref[rows, cols] + (bias_tile(strip, bias_row, step) - base)
                    if (row + 1) * TILE > sure:
                        place = lax.broadcasted_iota(jnp.int32, (TILE, 1), 0) + row * TILE
                        tile = jnp.where(place < visible, tile, NEG)
                    tile = jnp.exp(tile)
                    weight_ref[rows, cols] = tile.astype(jnp.bfloat16)
                    tile = tile * (slope_ref[rows, cols] - middle)
                    change_ref[rows, cols] = tile.astype(jnp.bfloat16)
                    if abs(step) <= 1:
                        sums[step] = tile if sums[step] is None else sums[step] + tile
                    else:
                        side = 1 if step > 0 else -1
                        part = jnp.sum(tile, axis=0, keepdims=True)
                        far[side] = part if far[side] is None else far[side] + part
            for step, value in sums.items():
                if value is not None:
                    at = TILE - step * TILE
                    table_ref[0, head, 0:TILE, at : at + TILE] += value
            for side, value in far.items():
                if value is not None:
                    at = TILE - side * TILE
                    table_ref[0, head, TILE : TILE + 1, at : at + TILE] = value
            value_grads.append(dot(weight_ref[0:length, 0:length], grad))
            key_grads.append(dot(change_ref[0:length, 0:length], query))
            query_grads.append(dot(keys_t[head * size : (head + 1) * size, start:stop], change_ref[0:length, 0:length]))
        stage_ref[slot, 0, start:stop, :] = (jnp.concatenate(query_grads, axis=0).T * 0.125).astype(jnp.bfloat16)
        stage_ref[slot, 1, start:stop, :] = (key_grads[0] + key_grads[1]).astype(jnp.bfloat16)
        stage_ref[slot, 2, start:stop, :] = (value_grads[0] + value_grads[1]).astype(jnp.bfloat16)
    for part in range(3):
        copy(part, pair).start()

    @pl.when(pair == pairs - 1)
    def _():
        for part in range(3):
            copy(part, pair - 1).wait()
            copy(part, pair).wait()


def attention_backward(lengths, bias, stat, proj, mixed, grad):
    tokens, width = mixed.shape
    lanes = TILE
    pairs = width // lanes
    return pl.pallas_call(
        attention_backward_kernel,
        grid=(pairs,),
        in_specs=[
            pl.BlockSpec(memory_space=pltpu.SMEM),
            pl.BlockSpec((1, 2, bias.shape[2]), lambda p: (p, 0, 0)),
            pl.BlockSpec((1, 2, tokens), lambda p: (p, 0, 0)),
            pl.BlockSpec((tokens, lanes), lambda p: (0, p)),
            pl.BlockSpec((tokens, lanes), lambda p: (0, pairs + p)),
            pl.BlockSpec((tokens, lanes), lambda p: (0, 2 * pairs + p)),
            pl.BlockSpec((tokens, lanes), lambda p: (0, p)),
            pl.BlockSpec((tokens, lanes), lambda p: (0, p)),
        ],
        out_specs=[
            pl.BlockSpec(memory_space=pl.ANY),
            pl.BlockSpec((1, 2, TILE + 8, 3 * TILE), lambda p: (p, 0, 0, 0)),
        ],
        out_shape=[
            jax.ShapeDtypeStruct((tokens, 3 * width), jnp.bfloat16),
            jax.ShapeDtypeStruct((pairs, 2, TILE + 8, 3 * TILE), jnp.float32),
        ],
        scratch_shapes=[
            pltpu.VMEM((LONG_LEN, LONG_LEN), jnp.float32),
            pltpu.VMEM((LONG_LEN, LONG_LEN), jnp.float32),
            pltpu.VMEM((LONG_LEN, LONG_LEN), jnp.bfloat16),
            pltpu.VMEM((LONG_LEN, LONG_LEN), jnp.bfloat16),
            pltpu.VMEM((2, 3, tokens, lanes), jnp.bfloat16),
            pltpu.SemaphoreType.DMA((2, 3)),
        ],
        cost_estimate=SMALL,
        name="attention_backward",
    )(lengths, bias, stat, proj, proj, proj, mixed, grad)


def bucket_of(offset):
    distance = jnp.abs(offset)
    far = 8 + sum(((distance >= bound).astype(jnp.int32) for bound in BOUNDS))
    return jnp.where(distance < 8, distance, far) + 16 * (offset > 0).astype(jnp.int32)


def bias_rows(rel_table):
    bucket = bucket_of(2 * TILE - jnp.arange(4 * TILE, dtype=jnp.int32))
    onehot = (bucket[:, None] == jnp.arange(rel_table.shape[0], dtype=jnp.int32)[None, :]).astype(jnp.float32)
    return jnp.einsum("xb,bh->hx", onehot, rel_table, precision=HIGHEST).reshape(-1, 2, 4 * TILE)


def table_sums(tiles, buckets):
    row = jnp.arange(TILE + 8, dtype=jnp.int32)[:, None]
    col = jnp.arange(3 * TILE, dtype=jnp.int32)[None, :]
    near = bucket_of(row - col + TILE)
    far = jnp.where(col < TILE, buckets - 1, buckets // 2 - 1)
    bucket = jnp.where(row < TILE, near, far)
    onehot = (bucket[:, :, None] == jnp.arange(buckets, dtype=jnp.int32)).astype(jnp.float32)
    return jnp.einsum("ghrc,rcb->bgh", tiles, onehot, precision=HIGHEST).reshape(buckets, -1)


def pack_first_kernel(place_ref, routes_ref, rows_ref, *out_refs, experts, capacity):
    target_ref = out_refs[-1]
    tokens = routes_ref.shape[1]
    routes = [routes_ref[rank : rank + 1, :] for rank in range(TOP)]
    label = lax.broadcasted_iota(jnp.int32, (experts, 1), 0)
    picks = [label == route for route in routes]
    named = jnp.where(picks[0] | picks[1], 1.0, 0.0).astype(jnp.bfloat16)
    later = lax.broadcasted_iota(jnp.int32, (1, tokens), 1)
    earlier = lax.broadcasted_iota(jnp.int32, (tokens, 1), 0)
    count = dot(named, jnp.where(earlier < later, 1.0, 0.0).astype(jnp.bfloat16))
    for rank in range(TOP):
        position = jnp.sum(jnp.where(picks[rank], count, 0.0), axis=0, keepdims=True).astype(jnp.int32)
        apart = routes[rank] ^ place_ref[0]
        apart = jnp.where(apart < experts // 2, routes[rank] & (experts // 2 - 1), apart)
        target_ref[rank : rank + 1, :] = apart * capacity + position
    other = jnp.concatenate([routes[1], routes[0]], axis=0).astype(jnp.float32) + 1.0
    pack_kernel(target_ref, rows_ref, *out_refs[:-1], other=other, capacity=capacity)


def pack_kernel(target_ref, rows_ref, *out_refs, other=None, capacity):
    rows = rows_ref[...]
    base = 0
    for out_ref in out_refs:
        stride = capacity + (0 if other is None else EXTRA)
        for at in range(0, out_ref.shape[0], stride):
            slot = lax.broadcasted_iota(jnp.int32, (capacity, 1), 0) + base
            hits = [slot == target_ref[rank : rank + 1, :] for rank in range(TOP)]
            hit = jnp.where(hits[0] | hits[1], 1.0, 0.0).astype(jnp.bfloat16)
            out_ref[at : at + capacity, :] = dot(hit, rows).astype(jnp.bfloat16)
            if other is not None:
                named = sum(jnp.where(hits[rank], other[rank : rank + 1, :], 0.0) for rank in range(TOP))
                ones = jnp.ones((EXTRA, named.shape[1]), jnp.bfloat16)
                out_ref[at + capacity : at + stride, :] = jnp.zeros((EXTRA, out_ref.shape[1]), jnp.bfloat16)
                out_ref[at + capacity : at + stride, 0:capacity] = dot(ones, named.astype(jnp.bfloat16), NT).astype(jnp.bfloat16)
            base += capacity


def block_shapes(experts, rows, width):
    half = experts // 2
    return [jax.ShapeDtypeStruct((n * rows, width), jnp.bfloat16) for n in [half] + [1] * half]


def pack_first(place, routes, rows, experts, capacity):
    blocks = block_shapes(experts, capacity + EXTRA, rows.shape[1])
    *blocks, target = pl.pallas_call(
        lambda *refs: pack_first_kernel(*refs, experts=experts, capacity=capacity),
        in_specs=[pl.BlockSpec(memory_space=pltpu.SMEM), pl.BlockSpec(), pl.BlockSpec()],
        out_shape=blocks + [jax.ShapeDtypeStruct(routes.shape, jnp.int32)],
        cost_estimate=SMALL,
        name="pack_first",
    )(place, routes, rows)
    return blocks, target


def pack(target, rows, experts, capacity):
    return pl.pallas_call(
        lambda *refs: pack_kernel(*refs, capacity=capacity),
        out_shape=block_shapes(experts, capacity, rows.shape[1]),
        cost_estimate=SMALL,
        name="pack_rows",
    )(target, rows)


def gather_rows(target_ref, gates_ref, blocks):
    total = None
    base = 0
    for block in blocks:
        slot = lax.broadcasted_iota(jnp.int32, (1, block.shape[0]), 1) + base
        share = sum(
            jnp.where(target_ref[:, rank : rank + 1] == slot, gates_ref[:, rank : rank + 1], 0.0) for rank in range(TOP)
        )
        part = dot(share.astype(jnp.bfloat16), block[...])
        total = part if total is None else total + part
        base += block.shape[0]
    return total


def output_kernel(target_ref, gates_ref, resid_ref, *refs):
    refs[-1][...] = (resid_ref[...] + gather_rows(target_ref, gates_ref, refs[:-1])).astype(jnp.bfloat16)


def combine_output(target, gates, resid, blocks):
    return pl.pallas_call(
        output_kernel,
        out_shape=jax.ShapeDtypeStruct(resid.shape, jnp.bfloat16),
        cost_estimate=MEDIUM,
        name="combine_output",
    )(target, gates, resid, *blocks)


def combine_kernel(target_ref, gates_ref, resid_ref, scale_ref, gain_ref, upstream_ref, *refs):
    blocks, (grad_ref, low_ref, gain_grad_ref) = refs[:-3], refs[-3:]
    total = gather_rows(target_ref, gates_ref, blocks)
    scale = scale_ref[...]
    unit = resid_ref[...] * scale
    gain_grad_ref[...] = jnp.sum(total * unit, axis=0, keepdims=True)
    along = total * gain_ref[...]
    inner = jnp.mean(along * unit, axis=1, keepdims=True)
    grad = upstream_ref[...].astype(jnp.float32) + scale * (along - unit * inner)
    grad_ref[...] = grad
    low_ref[...] = grad.astype(jnp.bfloat16)


def combine(target, gates, resid, scale, gain, upstream, blocks):
    tokens, width = resid.shape
    return pl.pallas_call(
        combine_kernel,
        out_shape=[
            jax.ShapeDtypeStruct((tokens, width), jnp.float32),
            jax.ShapeDtypeStruct((tokens, width), jnp.bfloat16),
            jax.ShapeDtypeStruct((1, width), jnp.float32),
        ],
        cost_estimate=SMALL,
        name="combine_back",
    )(target, gates, resid, scale, gain, upstream, *blocks)


def spans(blocks, capacity, extra=0):
    base = 0
    for block in blocks:
        for at in range(0, block.shape[0], capacity + extra):
            yield block, at, base
            base += capacity


def expert_kernel(own_ref, slope_ref, wg_ref, wu_ref, wr_ref, other_ref, *refs, ways, parts):
    blocks, refs = refs[:ways], refs[-(8 + ways) :]
    hidden_ref, gate_ref, up_ref, share_ref, router_ref = refs[:5]
    pairs, (x_ref, acc_ref, dots_ref) = refs[5 : 5 + ways], refs[5 + ways :]
    step = pl.program_id(0)
    rows = x_ref.shape[0] // parts

    @pl.when(step == 0)
    def _():
        acc_ref[...] = jnp.zeros_like(acc_ref)
        dots_ref[...] = jnp.zeros_like(dots_ref)
        base = 0
        for block in blocks:
            x_ref[base : base + block.shape[0], :] = block[...]
            base += block.shape[0]

    for part in range(parts):
        span = slice(part * rows, (part + 1) * rows)
        x = x_ref[span, :]
        gate = dot(x, wg_ref[...])
        up = dot(x, wu_ref[...])
        slope = slope_ref[span, :].astype(jnp.float32)
        square = gate * gate
        turn = jnp.tanh(gate * (CURVE + (CURVE * CUBE) * square))
        rise = 0.5 + 0.5 * turn
        unit = gate * rise
        bend = rise + (0.5 * gate) * (1.0 - turn * turn) * (CURVE + (3 * CURVE * CUBE) * square)
        hidden = (unit * up).astype(jnp.bfloat16)
        hidden_ref[span, :] = hidden
        both = hidden.astype(jnp.float32) * slope
        dots_ref[span, :] += both[:, 0:TILE] + both[:, TILE : 2 * TILE]
        gate_grad = (slope * up * bend).astype(jnp.bfloat16)
        up_grad = (slope * unit).astype(jnp.bfloat16)
        gate_ref[span, :] = gate_grad
        up_ref[span, :] = up_grad
        acc_ref[span, :] += dot(gate_grad, wg_ref[...], NT) + dot(up_grad, wu_ref[...], NT)

    @pl.when(step == pl.num_programs(0) - 1)
    def _():
        logits = dot(x_ref[...], wr_ref[...], NT)
        label = lax.broadcasted_iota(jnp.int32, (1, TILE), 1)
        mine = label == own_ref[0]
        theirs = label == other_ref[...].astype(jnp.int32) - 1
        first = jnp.sum(jnp.where(mine, logits, 0.0), axis=1, keepdims=True)
        second = jnp.sum(jnp.where(theirs, logits, 0.0), axis=1, keepdims=True)
        top = jnp.maximum(first, second)
        first = jnp.exp(first - top)
        second = jnp.exp(second - top)
        total = first + second
        first = first / total
        second = second / total
        inner = jnp.sum(dots_ref[...], axis=1, keepdims=True)
        coef = inner * second * (jnp.where(mine, 1.0, 0.0) - jnp.where(theirs, 1.0, 0.0))
        share_ref[...] = jnp.broadcast_to(first, share_ref.shape)
        router_ref[...] = dot((first * coef).astype(jnp.bfloat16), x_ref[...], TN)
        acc_ref[...] += dot(coef.astype(jnp.bfloat16), wr_ref[...])
        base = 0
        for pair in pairs:
            pair[...] = acc_ref[base : base + pair.shape[0], :].astype(jnp.bfloat16)
            base += pair.shape[0]


def once(shape):
    return pl.BlockSpec(shape, lambda i: (0, 0), pipeline_mode=pl.Buffered(1))


def expert_rows(own, blocks, slope, wg, wu, wr, other, chunk, kept, parts=2):
    n = slope.shape[0] // 2
    d, f = wg.shape
    ways = len(blocks)
    tile = pl.BlockSpec((n, FT), lambda i: (chunk, i))
    weight = pl.BlockSpec((d, FT), lambda i: (0, i))
    fixed = lambda shape: pl.BlockSpec(shape, lambda i: (0, 0))
    hidden, gate, up, share, router, *pairs = pl.pallas_call(
        lambda *refs: expert_kernel(*refs, ways=ways, parts=parts),
        grid=(f // FT,),
        in_specs=[
            pl.BlockSpec(memory_space=pltpu.SMEM),
            tile,
            weight,
            weight,
            once((TILE, d)),
            pl.BlockSpec((n, 1), lambda i: (chunk, 0), pipeline_mode=pl.Buffered(1)),
        ]
        + [once(block.shape) for block in blocks]
        + [pl.BlockSpec(memory_space=pl.ANY) for _ in kept],
        out_specs=[tile, tile, tile, fixed((n, TILE)), fixed((TILE, d))] + [fixed(block.shape) for block in blocks],
        out_shape=[jax.ShapeDtypeStruct((2 * n, f), jnp.bfloat16)] * 3
        + [jax.ShapeDtypeStruct((n, TILE), jnp.float32), jax.ShapeDtypeStruct((TILE, d), jnp.float32)]
        + [jax.ShapeDtypeStruct(block.shape, jnp.bfloat16) for block in blocks],
        scratch_shapes=[
            pltpu.VMEM((n, d), jnp.bfloat16),
            pltpu.VMEM((n, d), jnp.float32),
            pltpu.VMEM((n, TILE), jnp.float32),
        ],
        input_output_aliases={6 + ways + k: k for k in range(len(kept))},
        cost_estimate=LARGE if chunk else SMALL,
        name="expert_rows",
    )(own, slope, wg, wu, wr, other, *blocks, *kept)
    return (hidden, gate, up), share, router, pairs


def slope_kernel(wd_ref, *refs, capacity):
    blocks, (out_ref, u_ref) = refs[:-2], refs[-2:]

    @pl.when(pl.program_id(0) == 0)
    def _():
        for block, at, base in spans(blocks, capacity, EXTRA):
            u_ref[base : base + capacity, :] = block[at : at + capacity, :]

    out_ref[...] = dot(u_ref[...], wd_ref[...], NT).astype(jnp.bfloat16)


def slope_rows(blocks, wd, experts, capacity):
    f, d = wd.shape
    n = experts * capacity
    return pl.pallas_call(
        lambda *refs: slope_kernel(*refs, capacity=capacity),
        grid=(f // FT,),
        in_specs=[pl.BlockSpec((FT, d), lambda i: (i, 0))] + [once(block.shape) for block in blocks],
        out_specs=pl.BlockSpec((n, FT), lambda i: (0, i)),
        out_shape=jax.ShapeDtypeStruct((n, f), jnp.bfloat16),
        scratch_shapes=[pltpu.VMEM((n, d), jnp.bfloat16)],
        cost_estimate=LARGE,
        name="slope_rows",
    )(wd, *blocks)


def weight_kernel(hidden, gate, up, wd_ref, near_ref, far_ref, *refs, ways, copies, capacity):
    rows, raw, refs = refs[:ways], refs[ways : 2 * ways], refs[2 * ways :]
    out_ref, results, refs = refs[0], refs[1 : 1 + ways], refs[1 + ways :]
    rows_ref, raw_ref, acc_ref, stage_ref, down_ref, done_ref, sent_ref = refs
    step = pl.program_id(0)
    steps = pl.num_programs(0)
    d = stage_ref.shape[2] // 2
    piece = d // copies
    part_of = out_ref.shape[0] // copies

    def whole(at):
        return pltpu.make_async_copy(
            stage_ref.at[at % 2], out_ref.at[pl.ds(pl.multiple_of(at * FT, FT), FT), 0 : 2 * d], done_ref.at[at % 2]
        )

    def small(at, part, copy):
        row = at * FT + part * 64
        column = pl.multiple_of(2 * d + row // part_of * piece, piece)
        return pltpu.make_async_copy(
            down_ref.at[at % 2, part * 64 : (part + 1) * 64, copy * piece : (copy + 1) * piece],
            out_ref.at[pl.ds(pl.multiple_of(copy * part_of + row % part_of, 64), 64), pl.ds(column, piece)],
            sent_ref.at[at % 2, part, copy],
        )

    def finish(at):
        whole(at).wait()
        for part in range(FT // 64):
            for copy in range(copies):
                small(at, part, copy).wait()

    @pl.when(step == 0)
    def _():
        acc_ref[...] = jnp.zeros_like(acc_ref)
        for target_ref, blocks, extra in ((rows_ref, rows, 0), (raw_ref, raw, EXTRA)):
            for block, at, base in spans(blocks, capacity, extra):
                share_ref, start = (near_ref, base) if base < near_ref.shape[0] else (far_ref, base - near_ref.shape[0])
                share = share_ref[start : start + capacity, 0:1]
                value = block[at : at + capacity, :].astype(jnp.float32) * share
                target_ref[base : base + capacity, :] = value.astype(jnp.bfloat16)

    @pl.when(step >= 2)
    def _():
        finish(step - 2)

    slot = step % 2
    stage_ref[slot, :, 0:d] = dot(gate[...], rows_ref[...], TN).astype(jnp.bfloat16)
    stage_ref[slot, :, d : 2 * d] = dot(up[...], rows_ref[...], TN).astype(jnp.bfloat16)
    down_ref[slot] = dot(hidden[...], raw_ref[...], TN).astype(jnp.bfloat16)
    acc_ref[...] += dot(hidden[...], wd_ref[...])
    whole(step).start()
    for part in range(FT // 64):
        for copy in range(copies):
            small(step, part, copy).start()

    @pl.when(step == steps - 1)
    def _():
        base = 0
        for result in results:
            result[...] = acc_ref[base : base + result.shape[0], :].astype(jnp.bfloat16)
            base += result.shape[0]
        finish(step - 1)
        finish(step)


def weight_grads(hidden, gate, up, wd, shares, rows, raw, copies, capacity):
    n, f = hidden.shape
    d = wd.shape[1]
    ways = len(rows)
    narrow = pl.BlockSpec((n, FT), lambda i: (0, i))
    grad, *results = pl.pallas_call(
        lambda *refs: weight_kernel(*refs, ways=ways, copies=copies, capacity=capacity),
        grid=(f // FT,),
        in_specs=[narrow] * 3
        + [pl.BlockSpec((FT, d), lambda i: (i, 0))]
        + [once(part.shape) for part in (*shares, *rows, *raw)],
        out_specs=[pl.BlockSpec(memory_space=pl.ANY)] + [pl.BlockSpec(part.shape, lambda i: (0, 0)) for part in rows],
        out_shape=[jax.ShapeDtypeStruct((f, 3 * d), jnp.bfloat16)]
        + [jax.ShapeDtypeStruct(part.shape, jnp.bfloat16) for part in rows],
        scratch_shapes=[
            pltpu.VMEM((n, d), jnp.bfloat16),
            pltpu.VMEM((n, d), jnp.bfloat16),
            pltpu.VMEM((n, d), jnp.float32),
            pltpu.VMEM((2, FT, 2 * d), jnp.bfloat16),
            pltpu.VMEM((2, FT, d), jnp.bfloat16),
            pltpu.SemaphoreType.DMA((2,)),
            pltpu.SemaphoreType.DMA((2, FT // 64, copies)),
        ],
        cost_estimate=SMALL,
        name="weight_grads",
    )(hidden, gate, up, wd, *shares, *rows, *raw)
    return grad, results


def shared_kernel(core_ref, first_ref, wide_ref, second_ref, narrow_ref, mine_ref, away_ref, *, steps, unit):
    step = pl.program_id(0)

    def store(value):
        own = core_ref[0] == 0
        for group in range(mine_ref.shape[0] // unit):
            low = value[2 * group * unit : (2 * group + 1) * unit, :]
            high = value[(2 * group + 1) * unit : (2 * group + 2) * unit, :]
            span = slice(group * unit, (group + 1) * unit)
            mine_ref[span, :] = jnp.where(own, low, high).astype(jnp.bfloat16)
            away_ref[span, :] = jnp.where(own, high, low).astype(jnp.bfloat16)

    @pl.when(step < steps)
    def _():
        store(dot(first_ref[...], wide_ref[...], TN))

    @pl.when(step >= steps)
    def _():
        store(dot(second_ref[...], narrow_ref[...], TN))


def shared_grads(core, first, wide, second, narrow, unit):
    tokens, rows = first.shape
    tile = 512
    steps, more = wide.shape[1] // tile, narrow.shape[1] // tile
    whole = once((tokens, rows))
    out = pl.BlockSpec((rows // 2, tile), lambda i: (0, i))
    shape = jax.ShapeDtypeStruct((rows // 2, wide.shape[1] + narrow.shape[1]), jnp.bfloat16)
    return pl.pallas_call(
        lambda *refs: shared_kernel(*refs, steps=steps, unit=unit),
        grid=(steps + more,),
        in_specs=[
            pl.BlockSpec(memory_space=pltpu.SMEM),
            whole,
            pl.BlockSpec((tokens, tile), lambda i: (0, jnp.minimum(i, steps - 1))),
            whole,
            pl.BlockSpec((tokens, tile), lambda i: (0, jnp.maximum(i - steps, 0))),
        ],
        out_specs=[out, out],
        out_shape=[shape, shape],
        cost_estimate=SMALL,
        name="shared_grads",
    )(core, first, wide, second, narrow)


def after(value, *before):
    return lax.optimization_barrier((value,) + before)[0]


def swap(value, axis, step):
    size = lax.axis_size(axis)
    return lax.ppermute(value, axis, [(k, k ^ step) for k in range(size)])


def direct_sum(pieces, axis, stride):
    total = pieces[0].astype(jnp.float32)
    for step, piece in enumerate(pieces[1:], 1):
        total = total + swap(piece, axis, step * stride).astype(jnp.float32)
    return total


def over_all(mine, away, unit, *wait):
    copies, chips = lax.axis_size("dp"), lax.axis_size("expert") // 2
    other = swap(after(away, *wait), "expert", 1)
    parts = [array.reshape(copies, chips * unit, -1) for array in (mine, other)]
    place = lax.axis_index("dp")
    pieces = []
    for step in range(copies):
        both = [lax.dynamic_index_in_dim(part, place ^ step, 0, keepdims=False) for part in parts]
        pieces.append((both[0].astype(jnp.float32) + both[1].astype(jnp.float32)).astype(jnp.bfloat16))
    half = direct_sum(pieces, "dp", 1).astype(jnp.bfloat16).reshape(chips, unit, -1)
    place = lax.axis_index("expert") // 2
    half = [lax.dynamic_index_in_dim(half, place ^ step, 0, keepdims=False) for step in range(chips)]
    return pieces, half, direct_sum(half, "expert", 2)


def on_device(
    block_input,
    routes,
    item_lengths,
    w_qkv,
    w_attn_out,
    rel_table,
    gain_attn,
    gain_moe,
    w_router,
    w_gate,
    w_up,
    w_down,
    cotangent,
):
    tokens, width = block_input.shape
    experts = w_router.shape[1]
    capacity = TOK_DEV * TOP * 5 // (4 * experts)
    slots = experts * capacity
    buckets = rel_table.shape[0]
    copies, ways = lax.axis_size("dp"), lax.axis_size("expert")
    place = lax.axis_index("expert").astype(jnp.int32)
    own = place.reshape(1)
    labels = jnp.arange(experts, dtype=jnp.int32)
    picks = [routes[:, rank : rank + 1] == labels[None, :] for rank in range(TOP)]
    places = jnp.arange(slots, dtype=jnp.int32)

    half = ways // 2
    groups = [list(range(k * half, (k + 1) * half)) for k in range(2)]

    def near(block):
        parts = block.reshape(half, -1, block.shape[1])
        parts = lax.all_to_all(parts, "expert", split_axis=0, concat_axis=0, axis_index_groups=groups, tiled=True)
        return parts.reshape(block.shape)

    def exchange(blocks):
        far = [swap(block, "expert", half + step) for step, block in enumerate(blocks[1:])]
        return [near(blocks[0])] + far

    packed, target_rows = pack_first(own, routes.T, cotangent, experts, capacity)
    target = target_rows.T
    raw = exchange(packed)
    block_input = after(block_input, *packed)
    other = [block[at + capacity, :capacity] for block, at, _ in spans(raw, capacity, EXTRA)]
    other = jnp.stack(other).astype(jnp.float32).reshape(slots, 1)
    inputs = block_input.astype(jnp.float32)
    normed, unit_one, scale_one = normalize_forward(inputs, gain_attn)
    attn_in = normed.astype(jnp.bfloat16)
    bias = bias_rows(rel_table)
    proj = dot(attn_in, w_qkv).astype(jnp.bfloat16)
    mixed, stat = attention_forward(item_lengths, bias, proj)
    attn = dot(mixed, w_attn_out)
    resid = inputs + attn
    second, unit_two, scale_two = normalize_forward(resid, gain_moe)
    moe_in = second.astype(jnp.bfloat16)
    rows = exchange(pack(target_rows, after(moe_in, *raw), experts, capacity))
    logits = dot(moe_in, w_router)
    chosen = jnp.stack([jnp.sum(jnp.where(pick, logits, 0.0), axis=1) for pick in picks], axis=1)
    highest = jnp.max(chosen, axis=1, keepdims=True)
    exps = jnp.exp(chosen - highest)
    gates = exps / jnp.sum(exps, axis=1, keepdims=True)
    gate_weight, up_weight, down_weight = w_gate[0], w_up[0], w_down[0]
    router_rows = jnp.pad(w_router.T, ((0, TILE - experts), (0, 0)))
    slope = slope_rows(raw, down_weight, experts, capacity)
    weights = (gate_weight, up_weight, router_rows, other)
    kept, near_share, near_router, near_pairs = expert_rows(own, rows[:1], slope, *weights, 0, ())
    back = [near(near_pairs[0])]
    rows[1:] = [after(block, near_pairs[0]) for block in rows[1:]]
    kept, far_share, far_router, far_pairs = expert_rows(own, rows[1:], slope, *weights, 1, kept)
    back += [swap(block, "expert", half + step) for step, block in enumerate(far_pairs)]
    hidden, gate_pre_grad, up_pre_grad = kept
    weight_grad, result = weight_grads(
        after(hidden, back[0]),
        gate_pre_grad,
        up_pre_grad,
        down_weight,
        (near_share, far_share),
        rows,
        raw,
        copies,
        capacity,
    )
    weight_sum = lax.psum_scatter(weight_grad, "dp", scatter_dimension=0, tiled=True)
    *back, held = lax.optimization_barrier((*back, result[0]))
    result = [after(block, *back) for block in (held, *result[1:])]
    returned = exchange(result)
    resid_grad, attn_grad, gain_moe_grad = combine(
        target, gates, resid, scale_two, gain_moe.reshape(1, width), cotangent, back
    )
    mixed_grad = dot(attn_grad, w_attn_out, NT).astype(jnp.bfloat16)
    proj_grad, tiles = attention_backward(item_lengths, bias, stat, proj, mixed, mixed_grad)
    unit = width // (copies * ways)
    mine, away = shared_grads(own % 2, attn_in, proj_grad, mixed, attn_grad, unit)
    mine, half_sums, sums = over_all(mine, away, unit, *returned)
    proj_grad = after(proj_grad, *mine)
    table_grad = table_sums(tiles, buckets)
    router_grad = (near_router + far_router)[:experts].T
    attn_in_grad = dot(proj_grad, w_qkv, NT)
    input_norm_grad, gain_attn_grad = normalize_backward(attn_in_grad, unit_one, scale_one, gain_attn)
    input_grad = resid_grad + input_norm_grad
    output = combine_output(target, gates, after(resid, *half_sums), returned)
    piece = width // copies
    down_sum = jnp.concatenate(
        [weight_sum[:, 2 * width + k * piece : 2 * width + (k + 1) * piece] for k in range(copies)], axis=0
    )
    small = (table_grad.reshape(-1), gain_attn_grad, gain_moe_grad, router_grad)
    sizes = [part.size // (copies * ways) for part in small]
    together = jnp.concatenate([part.reshape(copies * ways, -1) for part in small], axis=1)
    together = lax.all_to_all(together, ("dp", "expert"), split_axis=0, concat_axis=0, tiled=True)
    together = jnp.sum(together, axis=0)
    at = [sum(sizes[:k]) for k in range(5)]
    table_sum, attn_sum, moe_sum, router_sum = [together[at[k] : at[k + 1]] for k in range(4)]
    return (
        output,
        input_grad,
        sums[:, : 3 * width],
        sums[:, 3 * width :],
        table_sum,
        attn_sum,
        moe_sum,
        router_sum.reshape(-1, experts),
        weight_sum[:, :width].astype(jnp.float32).T[None],
        weight_sum[:, width : 2 * width].astype(jnp.float32).T[None],
        down_sum.astype(jnp.float32)[None],
    )


def solution(mesh):
    return jax.shard_map(
        on_device,
        mesh=mesh,
        in_specs=(
            P(("dp", "expert"), None),
            P(("dp", "expert"), None),
            P(("dp", "expert"), None),
            P(),
            P(),
            P(),
            P(),
            P(),
            P(),
            P("expert", None, None),
            P("expert", None, None),
            P("expert", None, None),
            P(("dp", "expert"), None),
        ),
        out_specs=(
            P(("dp", "expert"), None),
            P(("dp", "expert"), None),
            P(("dp", "expert"), None),
            P(("dp", "expert"), None),
            P(("dp", "expert")),
            P(("dp", "expert")),
            P(("dp", "expert")),
            P(("dp", "expert"), None),
            P("expert", None, "dp"),
            P("expert", None, "dp"),
            P("expert", None, "dp"),
        ),
        check_vma=False,
    )
```

```python
import jax
import jax.numpy as jnp
from jax import lax
from jax.experimental import pallas as pl
from jax.experimental.pallas import tpu as pltpu
from jax.sharding import PartitionSpec as P

TOP = 2
LONG_LEN = 512
SHORT_LEN = 128
TOK_DEV = 640
BOUNDS = (12, 16, 23, 32, 46, 64, 91)
EPSILON = 1e-06
HIGHEST = lax.Precision.HIGHEST
TILE = 128
FT = 256
NEG = -1e30
NN = (((1,), (0,)), ((), ()))
NT = (((1,), (1,)), ((), ()))
TN = (((0,), (0,)), ((), ()))
CURVE = 0.7978845608028654
CUBE = 0.044715
EXTRA = 8
SMALL = pl.CostEstimate(flops=1 << 20, bytes_accessed=1 << 16, transcendentals=0)
MEDIUM = pl.CostEstimate(flops=250_700_000_000, bytes_accessed=1 << 16, transcendentals=0)
LARGE = pl.CostEstimate(flops=1 << 38, bytes_accessed=1 << 28, transcendentals=0)


def dot(a, b, dims=NN):
    return lax.dot_general(a, b, dims, preferred_element_type=jnp.float32)


def normalize_forward(value, gain):
    scale = lax.rsqrt(jnp.mean(value * value, axis=-1, keepdims=True) + EPSILON)
    unit = value * scale
    return (unit * gain, unit, scale)


def normalize_backward(grad, unit, scale, gain):
    gain_grad = jnp.sum(grad * unit, axis=0)
    along = grad * gain
    inner = jnp.mean(along * unit, axis=-1, keepdims=True)
    return (scale * (along - unit * inner), gain_grad)


def bias_strip(bias_row):
    wide = jnp.broadcast_to(bias_row, (TILE, bias_row.shape[1]))
    return pltpu.roll(wide, 0, 1, stride=1, stride_axis=0)


def bias_tile(strip, bias_row, step):
    if abs(step) <= 1:
        start = 2 * TILE - step * TILE
        return strip[:, start : start + TILE]
    last = bias_row.shape[1] - 1
    return bias_row[:, 0:1] if step > 0 else bias_row[:, last : last + 1]


def items_of(tokens, lengths_ref):
    return ((0, LONG_LEN, lengths_ref[0, 0], LONG_LEN // 2), (LONG_LEN, tokens, lengths_ref[0, 1], SHORT_LEN // 2))


def attention_forward_kernel(lengths_ref, bias_ref, q_ref, k_ref, v_ref, mixed_ref, stat_ref, score_ref, exp_ref):
    tokens, lanes = q_ref.shape
    size = lanes // 2
    lane = lax.broadcasted_iota(jnp.int32, (1, lanes), 1)
    values_t = v_ref[...].T
    for start, stop, visible, sure in items_of(tokens, lengths_ref):
        length = stop - start
        count = length // TILE
        outs = []
        for head in range(2):
            bias_row = bias_ref[0, head : head + 1, :]
            strip = bias_strip(bias_row)
            own = (lane >= head * size) & (lane < (head + 1) * size)
            query = jnp.where(own, q_ref[start:stop, :] * 0.125, 0.0).astype(jnp.bfloat16)
            score_ref[0:length, 0:length] = dot(k_ref[start:stop, :], query, NT)
            totals = []
            for col in range(count):
                cols = slice(col * TILE, (col + 1) * TILE)
                top = None
                for row in range(count):
                    rows = slice(row * TILE, (row + 1) * TILE)
                    tile = score_ref[rows, cols] + bias_tile(strip, bias_row, row - col)
                    if (row + 1) * TILE > sure:
                        place = lax.broadcasted_iota(jnp.int32, (TILE, 1), 0) + row * TILE
                        tile = jnp.where(place < visible, tile, NEG)
                    score_ref[rows, cols] = tile
                    peak = jnp.max(tile, axis=0, keepdims=True)
                    top = peak if top is None else jnp.maximum(top, peak)
                total = jnp.zeros((1, TILE), jnp.float32)
                for row in range(count):
                    rows = slice(row * TILE, (row + 1) * TILE)
                    tile = jnp.exp(score_ref[rows, cols] - top)
                    total = total + jnp.sum(tile, axis=0, keepdims=True)
                    exp_ref[rows, cols] = tile.astype(jnp.bfloat16)
                totals.append(total)
                stat_ref[0, head : head + 1, start + col * TILE : start + (col + 1) * TILE] = top + jnp.log(total)
            total = jnp.concatenate(totals, axis=1)
            out = dot(values_t[head * size : (head + 1) * size, start:stop], exp_ref[0:length, 0:length])
            outs.append(out / total)
        mixed_ref[start:stop, :] = jnp.concatenate(outs, axis=0).T.astype(jnp.bfloat16)


def attention_forward(lengths, bias, proj):
    tokens, width = proj.shape[0], proj.shape[1] // 3
    lanes = TILE
    pairs = width // lanes
    return pl.pallas_call(
        attention_forward_kernel,
        grid=(pairs,),
        in_specs=[
            pl.BlockSpec(memory_space=pltpu.SMEM),
            pl.BlockSpec((1, 2, bias.shape[2]), lambda p: (p, 0, 0)),
            pl.BlockSpec((tokens, lanes), lambda p: (0, p)),
            pl.BlockSpec((tokens, lanes), lambda p: (0, pairs + p)),
            pl.BlockSpec((tokens, lanes), lambda p: (0, 2 * pairs + p)),
        ],
        out_specs=[
            pl.BlockSpec((tokens, lanes), lambda p: (0, p)),
            pl.BlockSpec((1, 2, tokens), lambda p: (p, 0, 0)),
        ],
        out_shape=[
            jax.ShapeDtypeStruct((tokens, width), jnp.bfloat16),
            jax.ShapeDtypeStruct((pairs, 2, tokens), jnp.float32),
        ],
        scratch_shapes=[pltpu.VMEM((LONG_LEN, LONG_LEN), jnp.float32), pltpu.VMEM((LONG_LEN, LONG_LEN), jnp.bfloat16)],
        cost_estimate=SMALL,
        name="attention_forward",
    )(lengths, bias, proj, proj, proj)


def attention_backward_kernel(
    lengths_ref, bias_ref, stat_ref, q_ref, k_ref, v_ref, mixed_ref, grad_ref, proj_ref, table_ref,
    score_ref, slope_ref, weight_ref, change_ref, stage_ref, done_ref,
):
    pair = pl.program_id(0)
    pairs = pl.num_programs(0)
    slot = pair % 2

    def copy(part, step):
        at = pl.multiple_of((part * pairs + step) * TILE, TILE)
        return pltpu.make_async_copy(
            stage_ref.at[step % 2, part], proj_ref.at[:, pl.ds(at, TILE)], done_ref.at[step % 2, part]
        )

    @pl.when(pair >= 2)
    def _():
        for part in range(3):
            copy(part, pair - 2).wait()

    tokens, lanes = q_ref.shape
    size = lanes // 2
    lane = lax.broadcasted_iota(jnp.int32, (1, lanes), 1)
    keys_t = k_ref[...].T
    product = (grad_ref[...].astype(jnp.float32) * mixed_ref[...].astype(jnp.float32)).T
    table_ref[...] = jnp.zeros_like(table_ref)
    for start, stop, visible, sure in items_of(tokens, lengths_ref):
        length = stop - start
        count = length // TILE
        query_grads, key_grads, value_grads = [], [], []
        for head in range(2):
            bias_row = bias_ref[0, head : head + 1, :]
            strip = bias_strip(bias_row)
            own = (lane >= head * size) & (lane < (head + 1) * size)
            query = jnp.where(own, q_ref[start:stop, :] * 0.125, 0.0).astype(jnp.bfloat16)
            grad = jnp.where(own, grad_ref[start:stop, :], 0.0).astype(jnp.bfloat16)
            score_ref[0:length, 0:length] = dot(k_ref[start:stop, :], query, NT)
            slope_ref[0:length, 0:length] = dot(v_ref[start:stop, :], grad, NT)
            inner = jnp.sum(product[head * size : (head + 1) * size, start:stop], axis=0, keepdims=True)
            sums = {-1: None, 0: None, 1: None}
            far = {-1: None, 1: None}
            for col in range(count):
                cols = slice(col * TILE, (col + 1) * TILE)
                base = stat_ref[0, head : head + 1, start + col * TILE : start + (col + 1) * TILE]
                middle = inner[:, cols]
                for row in range(count):
                    rows = slice(row * TILE, (row + 1) * TILE)
                    step = row - col
                    tile = score_ref[rows, cols] + (bias_tile(strip, bias_row, step) - base)
                    if (row + 1) * TILE > sure:
                        place = lax.broadcasted_iota(jnp.int32, (TILE, 1), 0) + row * TILE
                        tile = jnp.where(place < visible, tile, NEG)
                    tile = jnp.exp(tile)
                    weight_ref[rows, cols] = tile.astype(jnp.bfloat16)
                    tile = tile * (slope_ref[rows, cols] - middle)
                    change_ref[rows, cols] = tile.astype(jnp.bfloat16)
                    if abs(step) <= 1:
                        sums[step] = tile if sums[step] is None else sums[step] + tile
                    else:
                        side = 1 if step > 0 else -1
                        part = jnp.sum(tile, axis=0, keepdims=True)
                        far[side] = part if far[side] is None else far[side] + part
            for step, value in sums.items():
                if value is not None:
                    at = TILE - step * TILE
                    table_ref[0, head, 0:TILE, at : at + TILE] += value
            for side, value in far.items():
                if value is not None:
                    at = TILE - side * TILE
                    table_ref[0, head, TILE : TILE + 1, at : at + TILE] = value
            value_grads.append(dot(weight_ref[0:length, 0:length], grad))
            key_grads.append(dot(change_ref[0:length, 0:length], query))
            query_grads.append(dot(keys_t[head * size : (head + 1) * size, start:stop], change_ref[0:length, 0:length]))
        stage_ref[slot, 0, start:stop, :] = (jnp.concatenate(query_grads, axis=0).T * 0.125).astype(jnp.bfloat16)
        stage_ref[slot, 1, start:stop, :] = (key_grads[0] + key_grads[1]).astype(jnp.bfloat16)
        stage_ref[slot, 2, start:stop, :] = (value_grads[0] + value_grads[1]).astype(jnp.bfloat16)
    for part in range(3):
        copy(part, pair).start()

    @pl.when(pair == pairs - 1)
    def _():
        for part in range(3):
            copy(part, pair - 1).wait()
            copy(part, pair).wait()


def attention_backward(lengths, bias, stat, proj, mixed, grad):
    tokens, width = mixed.shape
    lanes = TILE
    pairs = width // lanes
    return pl.pallas_call(
        attention_backward_kernel,
        grid=(pairs,),
        in_specs=[
            pl.BlockSpec(memory_space=pltpu.SMEM),
            pl.BlockSpec((1, 2, bias.shape[2]), lambda p: (p, 0, 0)),
            pl.BlockSpec((1, 2, tokens), lambda p: (p, 0, 0)),
            pl.BlockSpec((tokens, lanes), lambda p: (0, p)),
            pl.BlockSpec((tokens, lanes), lambda p: (0, pairs + p)),
            pl.BlockSpec((tokens, lanes), lambda p: (0, 2 * pairs + p)),
            pl.BlockSpec((tokens, lanes), lambda p: (0, p)),
            pl.BlockSpec((tokens, lanes), lambda p: (0, p)),
        ],
        out_specs=[
            pl.BlockSpec(memory_space=pl.ANY),
            pl.BlockSpec((1, 2, TILE + 8, 3 * TILE), lambda p: (p, 0, 0, 0)),
        ],
        out_shape=[
            jax.ShapeDtypeStruct((tokens, 3 * width), jnp.bfloat16),
            jax.ShapeDtypeStruct((pairs, 2, TILE + 8, 3 * TILE), jnp.float32),
        ],
        scratch_shapes=[
            pltpu.VMEM((LONG_LEN, LONG_LEN), jnp.float32),
            pltpu.VMEM((LONG_LEN, LONG_LEN), jnp.float32),
            pltpu.VMEM((LONG_LEN, LONG_LEN), jnp.bfloat16),
            pltpu.VMEM((LONG_LEN, LONG_LEN), jnp.bfloat16),
            pltpu.VMEM((2, 3, tokens, lanes), jnp.bfloat16),
            pltpu.SemaphoreType.DMA((2, 3)),
        ],
        cost_estimate=SMALL,
        name="attention_backward",
    )(lengths, bias, stat, proj, proj, proj, mixed, grad)


def bucket_of(offset):
    distance = jnp.abs(offset)
    far = 8 + sum(((distance >= bound).astype(jnp.int32) for bound in BOUNDS))
    return jnp.where(distance < 8, distance, far) + 16 * (offset > 0).astype(jnp.int32)


def bias_rows(rel_table):
    bucket = bucket_of(2 * TILE - jnp.arange(4 * TILE, dtype=jnp.int32))
    onehot = (bucket[:, None] == jnp.arange(rel_table.shape[0], dtype=jnp.int32)[None, :]).astype(jnp.float32)
    return jnp.einsum("xb,bh->hx", onehot, rel_table, precision=HIGHEST).reshape(-1, 2, 4 * TILE)


def table_sums(tiles, buckets):
    row = jnp.arange(TILE + 8, dtype=jnp.int32)[:, None]
    col = jnp.arange(3 * TILE, dtype=jnp.int32)[None, :]
    near = bucket_of(row - col + TILE)
    far = jnp.where(col < TILE, buckets - 1, buckets // 2 - 1)
    bucket = jnp.where(row < TILE, near, far)
    onehot = (bucket[:, :, None] == jnp.arange(buckets, dtype=jnp.int32)).astype(jnp.float32)
    return jnp.einsum("ghrc,rcb->bgh", tiles, onehot, precision=HIGHEST).reshape(buckets, -1)


def pack_first_kernel(place_ref, routes_ref, rows_ref, *out_refs, experts, capacity):
    target_ref = out_refs[-1]
    tokens = routes_ref.shape[1]
    routes = [routes_ref[rank : rank + 1, :] for rank in range(TOP)]
    label = lax.broadcasted_iota(jnp.int32, (experts, 1), 0)
    picks = [label == route for route in routes]
    named = jnp.where(picks[0] | picks[1], 1.0, 0.0).astype(jnp.bfloat16)
    later = lax.broadcasted_iota(jnp.int32, (1, tokens), 1)
    earlier = lax.broadcasted_iota(jnp.int32, (tokens, 1), 0)
    count = dot(named, jnp.where(earlier < later, 1.0, 0.0).astype(jnp.bfloat16))
    for rank in range(TOP):
        position = jnp.sum(jnp.where(picks[rank], count, 0.0), axis=0, keepdims=True).astype(jnp.int32)
        apart = routes[rank] ^ place_ref[0]
        apart = jnp.where(apart < experts // 2, routes[rank] & (experts // 2 - 1), apart)
        target_ref[rank : rank + 1, :] = apart * capacity + position
    other = jnp.concatenate([routes[1], routes[0]], axis=0).astype(jnp.float32) + 1.0
    pack_kernel(target_ref, rows_ref, *out_refs[:-1], other=other, capacity=capacity)


def pack_kernel(target_ref, rows_ref, *out_refs, other=None, capacity):
    rows = rows_ref[...]
    base = 0
    for out_ref in out_refs:
        stride = capacity + (0 if other is None else EXTRA)
        for at in range(0, out_ref.shape[0], stride):
            slot = lax.broadcasted_iota(jnp.int32, (capacity, 1), 0) + base
            hits = [slot == target_ref[rank : rank + 1, :] for rank in range(TOP)]
            hit = jnp.where(hits[0] | hits[1], 1.0, 0.0).astype(jnp.bfloat16)
            out_ref[at : at + capacity, :] = dot(hit, rows).astype(jnp.bfloat16)
            if other is not None:
                named = sum(jnp.where(hits[rank], other[rank : rank + 1, :], 0.0) for rank in range(TOP))
                ones = jnp.ones((EXTRA, named.shape[1]), jnp.bfloat16)
                out_ref[at + capacity : at + stride, :] = jnp.zeros((EXTRA, out_ref.shape[1]), jnp.bfloat16)
                out_ref[at + capacity : at + stride, 0:capacity] = dot(ones, named.astype(jnp.bfloat16), NT).astype(jnp.bfloat16)
            base += capacity


def block_shapes(experts, rows, width):
    half = experts // 2
    return [jax.ShapeDtypeStruct((n * rows, width), jnp.bfloat16) for n in [half] + [1] * half]


def pack_first(place, routes, rows, experts, capacity):
    blocks = block_shapes(experts, capacity + EXTRA, rows.shape[1])
    *blocks, target = pl.pallas_call(
        lambda *refs: pack_first_kernel(*refs, experts=experts, capacity=capacity),
        in_specs=[pl.BlockSpec(memory_space=pltpu.SMEM), pl.BlockSpec(), pl.BlockSpec()],
        out_shape=blocks + [jax.ShapeDtypeStruct(routes.shape, jnp.int32)],
        cost_estimate=SMALL,
        name="pack_first",
    )(place, routes, rows)
    return blocks, target


def pack(target, rows, experts, capacity):
    return pl.pallas_call(
        lambda *refs: pack_kernel(*refs, capacity=capacity),
        out_shape=block_shapes(experts, capacity, rows.shape[1]),
        cost_estimate=SMALL,
        name="pack_rows",
    )(target, rows)


def gather_rows(target_ref, gates_ref, blocks):
    total = None
    base = 0
    for block in blocks:
        slot = lax.broadcasted_iota(jnp.int32, (1, block.shape[0]), 1) + base
        share = sum(
            jnp.where(target_ref[:, rank : rank + 1] == slot, gates_ref[:, rank : rank + 1], 0.0) for rank in range(TOP)
        )
        part = dot(share.astype(jnp.bfloat16), block[...])
        total = part if total is None else total + part
        base += block.shape[0]
    return total


def output_kernel(target_ref, gates_ref, resid_ref, *refs):
    refs[-1][...] = (resid_ref[...] + gather_rows(target_ref, gates_ref, refs[:-1])).astype(jnp.bfloat16)


def combine_output(target, gates, resid, blocks):
    return pl.pallas_call(
        output_kernel,
        out_shape=jax.ShapeDtypeStruct(resid.shape, jnp.bfloat16),
        cost_estimate=MEDIUM,
        name="combine_output",
    )(target, gates, resid, *blocks)


def combine_kernel(target_ref, gates_ref, resid_ref, scale_ref, gain_ref, upstream_ref, *refs):
    blocks, (grad_ref, low_ref, gain_grad_ref) = refs[:-3], refs[-3:]
    total = gather_rows(target_ref, gates_ref, blocks)
    scale = scale_ref[...]
    unit = resid_ref[...] * scale
    gain_grad_ref[...] = jnp.sum(total * unit, axis=0, keepdims=True)
    along = total * gain_ref[...]
    inner = jnp.mean(along * unit, axis=1, keepdims=True)
    grad = upstream_ref[...].astype(jnp.float32) + scale * (along - unit * inner)
    grad_ref[...] = grad
    low_ref[...] = grad.astype(jnp.bfloat16)


def combine(target, gates, resid, scale, gain, upstream, blocks):
    tokens, width = resid.shape
    return pl.pallas_call(
        combine_kernel,
        out_shape=[
            jax.ShapeDtypeStruct((tokens, width), jnp.float32),
            jax.ShapeDtypeStruct((tokens, width), jnp.bfloat16),
            jax.ShapeDtypeStruct((1, width), jnp.float32),
        ],
        cost_estimate=SMALL,
        name="combine_back",
    )(target, gates, resid, scale, gain, upstream, *blocks)


def spans(blocks, capacity, extra=0):
    base = 0
    for block in blocks:
        for at in range(0, block.shape[0], capacity + extra):
            yield block, at, base
            base += capacity


def expert_kernel(own_ref, slope_ref, wg_ref, wu_ref, wr_ref, other_ref, *refs, ways, parts):
    blocks, refs = refs[:ways], refs[-(8 + ways) :]
    hidden_ref, gate_ref, up_ref, share_ref, router_ref = refs[:5]
    pairs, (x_ref, acc_ref, dots_ref) = refs[5 : 5 + ways], refs[5 + ways :]
    step = pl.program_id(0)
    rows = x_ref.shape[0] // parts

    @pl.when(step == 0)
    def _():
        acc_ref[...] = jnp.zeros_like(acc_ref)
        dots_ref[...] = jnp.zeros_like(dots_ref)
        base = 0
        for block in blocks:
            x_ref[base : base + block.shape[0], :] = block[...]
            base += block.shape[0]

    for part in range(parts):
        span = slice(part * rows, (part + 1) * rows)
        x = x_ref[span, :]
        gate = dot(x, wg_ref[...])
        up = dot(x, wu_ref[...])
        slope = slope_ref[span, :].astype(jnp.float32)
        square = gate * gate
        turn = jnp.tanh(gate * (CURVE + (CURVE * CUBE) * square))
        rise = 0.5 + 0.5 * turn
        unit = gate * rise
        bend = rise + (0.5 * gate) * (1.0 - turn * turn) * (CURVE + (3 * CURVE * CUBE) * square)
        hidden = (unit * up).astype(jnp.bfloat16)
        hidden_ref[span, :] = hidden
        both = hidden.astype(jnp.float32) * slope
        dots_ref[span, :] += both[:, 0:TILE] + both[:, TILE : 2 * TILE]
        gate_grad = (slope * up * bend).astype(jnp.bfloat16)
        up_grad = (slope * unit).astype(jnp.bfloat16)
        gate_ref[span, :] = gate_grad
        up_ref[span, :] = up_grad
        acc_ref[span, :] += dot(gate_grad, wg_ref[...], NT) + dot(up_grad, wu_ref[...], NT)

    @pl.when(step == pl.num_programs(0) - 1)
    def _():
        logits = dot(x_ref[...], wr_ref[...], NT)
        label = lax.broadcasted_iota(jnp.int32, (1, TILE), 1)
        mine = label == own_ref[0]
        theirs = label == other_ref[:, 0:1].astype(jnp.int32) - 1
        first = jnp.sum(jnp.where(mine, logits, 0.0), axis=1, keepdims=True)
        second = jnp.sum(jnp.where(theirs, logits, 0.0), axis=1, keepdims=True)
        top = jnp.maximum(first, second)
        first = jnp.exp(first - top)
        second = jnp.exp(second - top)
        total = first + second
        first = first / total
        second = second / total
        inner = jnp.sum(dots_ref[...], axis=1, keepdims=True)
        coef = inner * second * (jnp.where(mine, 1.0, 0.0) - jnp.where(theirs, 1.0, 0.0))
        share_ref[...] = jnp.broadcast_to(first, share_ref.shape)
        router_ref[...] = dot((first * coef).astype(jnp.bfloat16), x_ref[...], TN)
        acc_ref[...] += dot(coef.astype(jnp.bfloat16), wr_ref[...])
        base = 0
        for pair in pairs:
            pair[...] = acc_ref[base : base + pair.shape[0], :].astype(jnp.bfloat16)
            base += pair.shape[0]


def once(shape):
    return pl.BlockSpec(shape, lambda i: (0, 0), pipeline_mode=pl.Buffered(1))


def expert_rows(own, blocks, slope, wg, wu, wr, other, chunk, kept, parts=2):
    n = slope.shape[0] // 2
    d, f = wg.shape
    ways = len(blocks)
    tile = pl.BlockSpec((n, FT), lambda i: (chunk, i))
    weight = pl.BlockSpec((d, FT), lambda i: (0, i))
    fixed = lambda shape: pl.BlockSpec(shape, lambda i: (0, 0))
    hidden, gate, up, share, router, *pairs = pl.pallas_call(
        lambda *refs: expert_kernel(*refs, ways=ways, parts=parts),
        grid=(f // FT,),
        in_specs=[
            pl.BlockSpec(memory_space=pltpu.SMEM),
            tile,
            weight,
            weight,
            once((TILE, d)),
            pl.BlockSpec((n, TILE), lambda i: (chunk, 0), pipeline_mode=pl.Buffered(1)),
        ]
        + [once(block.shape) for block in blocks]
        + [pl.BlockSpec(memory_space=pl.ANY) for _ in kept],
        out_specs=[tile, tile, tile, fixed((n, TILE)), fixed((TILE, d))] + [fixed(block.shape) for block in blocks],
        out_shape=[jax.ShapeDtypeStruct((2 * n, f), jnp.bfloat16)] * 3
        + [jax.ShapeDtypeStruct((n, TILE), jnp.float32), jax.ShapeDtypeStruct((TILE, d), jnp.float32)]
        + [jax.ShapeDtypeStruct(block.shape, jnp.bfloat16) for block in blocks],
        scratch_shapes=[
            pltpu.VMEM((n, d), jnp.bfloat16),
            pltpu.VMEM((n, d), jnp.float32),
            pltpu.VMEM((n, TILE), jnp.float32),
        ],
        input_output_aliases={6 + ways + k: k for k in range(len(kept))},
        cost_estimate=LARGE if chunk else SMALL,
        name="expert_rows",
    )(own, slope, wg, wu, wr, other, *blocks, *kept)
    return (hidden, gate, up), share, router, pairs


def slope_kernel(wd_ref, *refs, capacity):
    blocks, (out_ref, other_ref, u_ref) = refs[:-3], refs[-3:]

    @pl.when(pl.program_id(0) == 0)
    def _():
        reach = -(-capacity // TILE) * TILE
        for block, at, base in spans(blocks, capacity, EXTRA):
            u_ref[base : base + capacity, :] = block[at : at + capacity, :]
            named = block[at + capacity : at + capacity + EXTRA, 0:reach].astype(jnp.float32).T
            other_ref[base : base + capacity, :] = jnp.broadcast_to(named[0:capacity, 0:1], (capacity, TILE))

    out_ref[...] = dot(u_ref[...], wd_ref[...], NT).astype(jnp.bfloat16)


def slope_rows(blocks, wd, experts, capacity):
    f, d = wd.shape
    n = experts * capacity
    return pl.pallas_call(
        lambda *refs: slope_kernel(*refs, capacity=capacity),
        grid=(f // FT,),
        in_specs=[pl.BlockSpec((FT, d), lambda i: (i, 0))] + [once(block.shape) for block in blocks],
        out_specs=[pl.BlockSpec((n, FT), lambda i: (0, i)), pl.BlockSpec((n, TILE), lambda i: (0, 0))],
        out_shape=[jax.ShapeDtypeStruct((n, f), jnp.bfloat16), jax.ShapeDtypeStruct((n, TILE), jnp.float32)],
        scratch_shapes=[pltpu.VMEM((n, d), jnp.bfloat16)],
        cost_estimate=LARGE,
        name="slope_rows",
    )(wd, *blocks)


def gate_slots(target_ref, blocks, near_ref, far_ref, capacity, extra):
    for block, at, base in spans(blocks, capacity, extra):
        share_ref, start = (near_ref, base) if base < near_ref.shape[0] else (far_ref, base - near_ref.shape[0])
        value = block[at : at + capacity, :].astype(jnp.float32) * share_ref[start : start + capacity, 0:1]
        target_ref[base : base + capacity, :] = value.astype(jnp.bfloat16)


def weight_kernel(hidden, gate, up, near_ref, far_ref, *refs, ways, copies, capacity):
    rows, raw, refs = refs[:ways], refs[ways : 2 * ways], refs[2 * ways :]
    out_ref, rows_ref, raw_ref, stage_ref, down_ref, done_ref, sent_ref = refs
    step = pl.program_id(0)
    steps = pl.num_programs(0)
    d = stage_ref.shape[2] // 2
    piece = d // copies
    part_of = out_ref.shape[0] // copies

    def whole(at):
        return pltpu.make_async_copy(
            stage_ref.at[at % 2], out_ref.at[pl.ds(pl.multiple_of(at * FT, FT), FT), 0 : 2 * d], done_ref.at[at % 2]
        )

    def small(at, part, copy):
        row = at * FT + part * 64
        column = pl.multiple_of(2 * d + row // part_of * piece, piece)
        return pltpu.make_async_copy(
            down_ref.at[at % 2, part * 64 : (part + 1) * 64, copy * piece : (copy + 1) * piece],
            out_ref.at[pl.ds(pl.multiple_of(copy * part_of + row % part_of, 64), 64), pl.ds(column, piece)],
            sent_ref.at[at % 2, part, copy],
        )

    def finish(at):
        whole(at).wait()
        for part in range(FT // 64):
            for copy in range(copies):
                small(at, part, copy).wait()

    @pl.when(step == 0)
    def _():
        gate_slots(rows_ref, rows, near_ref, far_ref, capacity, 0)
        gate_slots(raw_ref, raw, near_ref, far_ref, capacity, EXTRA)

    @pl.when(step >= 2)
    def _():
        finish(step - 2)

    slot = step % 2
    stage_ref[slot, :, 0:d] = dot(gate[...], rows_ref[...], TN).astype(jnp.bfloat16)
    stage_ref[slot, :, d : 2 * d] = dot(up[...], rows_ref[...], TN).astype(jnp.bfloat16)
    down_ref[slot] = dot(hidden[...], raw_ref[...], TN).astype(jnp.bfloat16)
    whole(step).start()
    for part in range(FT // 64):
        for copy in range(copies):
            small(step, part, copy).start()

    @pl.when(step == steps - 1)
    def _():
        finish(step - 1)
        finish(step)


def weight_grads(hidden, gate, up, shares, rows, raw, copies, capacity):
    n, f = hidden.shape
    d = rows[0].shape[1]
    ways = len(rows)
    narrow = pl.BlockSpec((n, FT), lambda i: (0, i))
    return pl.pallas_call(
        lambda *refs: weight_kernel(*refs, ways=ways, copies=copies, capacity=capacity),
        grid=(f // FT,),
        in_specs=[narrow] * 3 + [once(part.shape) for part in (*shares, *rows, *raw)],
        out_specs=pl.BlockSpec(memory_space=pl.ANY),
        out_shape=jax.ShapeDtypeStruct((f, 3 * d), jnp.bfloat16),
        scratch_shapes=[
            pltpu.VMEM((n, d), jnp.bfloat16),
            pltpu.VMEM((n, d), jnp.bfloat16),
            pltpu.VMEM((2, FT, 2 * d), jnp.bfloat16),
            pltpu.VMEM((2, FT, d), jnp.bfloat16),
            pltpu.SemaphoreType.DMA((2,)),
            pltpu.SemaphoreType.DMA((2, FT // 64, copies)),
        ],
        cost_estimate=SMALL,
        name="weight_grads",
    )(hidden, gate, up, *shares, *rows, *raw)


def result_kernel(hidden_ref, wd_ref, *refs):
    results, acc_ref = refs[:-1], refs[-1]
    step = pl.program_id(0)
    part = dot(hidden_ref[...], wd_ref[...])

    @pl.when(step == 0)
    def _():
        acc_ref[...] = part

    @pl.when(step > 0)
    def _():
        acc_ref[...] += part

    @pl.when(step == pl.num_programs(0) - 1)
    def _():
        base = 0
        for result in results:
            result[...] = acc_ref[base : base + result.shape[0], :].astype(jnp.bfloat16)
            base += result.shape[0]


def result_rows(hidden, wd, shapes):
    n, f = hidden.shape
    d = wd.shape[1]
    tile = FT * 2 if f % (FT * 2) == 0 else FT
    return pl.pallas_call(
        result_kernel,
        grid=(f // tile,),
        in_specs=[pl.BlockSpec((n, tile), lambda i: (0, i)), pl.BlockSpec((tile, d), lambda i: (i, 0))],
        out_specs=[pl.BlockSpec(shape, lambda i: (0, 0)) for shape in shapes],
        out_shape=[jax.ShapeDtypeStruct(shape, jnp.bfloat16) for shape in shapes],
        scratch_shapes=[pltpu.VMEM((n, d), jnp.float32)],
        cost_estimate=SMALL,
        name="result_rows",
    )(hidden, wd)


def shared_kernel(
    core_ref, first_ref, wide_ref, second_ref, narrow_ref, mine_ref, away_ref, left_ref, *, steps, unit
):
    step = pl.program_id(0)

    def store(value):
        own = core_ref[0] == 0
        for group in range(mine_ref.shape[0] // unit):
            low = value[2 * group * unit : (2 * group + 1) * unit, :]
            high = value[(2 * group + 1) * unit : (2 * group + 2) * unit, :]
            span = slice(group * unit, (group + 1) * unit)
            mine_ref[span, :] = jnp.where(own, low, high).astype(jnp.bfloat16)
            away_ref[span, :] = jnp.where(own, high, low).astype(jnp.bfloat16)

    @pl.when(step == 0)
    def _():
        left_ref[...] = first_ref[...].T

    @pl.when(step == steps)
    def _():
        left_ref[...] = second_ref[...].T

    @pl.when(step < steps)
    def _():
        store(dot(left_ref[...], wide_ref[...]))

    @pl.when(step >= steps)
    def _():
        store(dot(left_ref[...], narrow_ref[...]))


def shared_grads(core, first, wide, second, narrow, unit):
    tokens, rows = first.shape
    tile = 512
    steps, more = wide.shape[1] // tile, narrow.shape[1] // tile
    whole = once((tokens, rows))
    out = pl.BlockSpec((rows // 2, tile), lambda i: (0, i))
    shape = jax.ShapeDtypeStruct((rows // 2, wide.shape[1] + narrow.shape[1]), jnp.bfloat16)
    return pl.pallas_call(
        lambda *refs: shared_kernel(*refs, steps=steps, unit=unit),
        grid=(steps + more,),
        in_specs=[
            pl.BlockSpec(memory_space=pltpu.SMEM),
            whole,
            pl.BlockSpec((tokens, tile), lambda i: (0, jnp.minimum(i, steps - 1))),
            whole,
            pl.BlockSpec((tokens, tile), lambda i: (0, jnp.maximum(i - steps, 0))),
        ],
        out_specs=[out, out],
        out_shape=[shape, shape],
        scratch_shapes=[pltpu.VMEM((rows, tokens), jnp.bfloat16)],
        cost_estimate=SMALL,
        name="shared_grads",
    )(core, first, wide, second, narrow)


def after(value, *before):
    return lax.optimization_barrier((value,) + before)[0]


def swap(value, axis, step):
    size = lax.axis_size(axis)
    return lax.ppermute(value, axis, [(k, k ^ step) for k in range(size)])


def chip_sums(mine, away, unit):
    copies, chips = lax.axis_size("dp"), lax.axis_size("expert") // 2
    parts = [array.reshape(copies, chips * unit, -1) for array in (mine, swap(away, "expert", 1))]
    place = lax.axis_index("dp")
    pieces = []
    for step in range(copies):
        both = [lax.dynamic_index_in_dim(part, place ^ step, 0, keepdims=False) for part in parts]
        pieces.append((both[0].astype(jnp.float32) + both[1].astype(jnp.float32)).astype(jnp.bfloat16))
    return pieces


def device_sums(pieces, unit, *work):
    arrived = [swap(piece, "dp", step) if step else piece for step, piece in enumerate(pieces)]
    *arrived, _ = lax.optimization_barrier((*arrived, work))
    chips = lax.axis_size("expert") // 2
    total = sum(piece.astype(jnp.float32) for piece in arrived).astype(jnp.bfloat16).reshape(chips, unit, -1)
    place = lax.axis_index("expert") // 2
    return [lax.dynamic_index_in_dim(total, place ^ step, 0, keepdims=False) for step in range(chips)]


def on_device(
    block_input,
    routes,
    item_lengths,
    w_qkv,
    w_attn_out,
    rel_table,
    gain_attn,
    gain_moe,
    w_router,
    w_gate,
    w_up,
    w_down,
    cotangent,
):
    tokens, width = block_input.shape
    experts = w_router.shape[1]
    capacity = TOK_DEV * TOP * 5 // (4 * experts)
    slots = experts * capacity
    buckets = rel_table.shape[0]
    copies, ways = lax.axis_size("dp"), lax.axis_size("expert")
    place = lax.axis_index("expert").astype(jnp.int32)
    own = place.reshape(1)
    labels = jnp.arange(experts, dtype=jnp.int32)
    picks = [routes[:, rank : rank + 1] == labels[None, :] for rank in range(TOP)]
    places = jnp.arange(slots, dtype=jnp.int32)

    half = ways // 2
    groups = [list(range(k * half, (k + 1) * half)) for k in range(2)]

    def near(block):
        parts = block.reshape(half, -1, block.shape[1])
        parts = lax.all_to_all(parts, "expert", split_axis=0, concat_axis=0, axis_index_groups=groups, tiled=True)
        return parts.reshape(block.shape)

    def exchange(blocks):
        far = [swap(block, "expert", half + step) for step, block in enumerate(blocks[1:])]
        return [near(blocks[0])] + far

    packed, target_rows = pack_first(own, routes.T, cotangent, experts, capacity)
    target = target_rows.T
    raw = exchange(packed)
    block_input = after(block_input, *packed)
    inputs = block_input.astype(jnp.float32)
    normed, unit_one, scale_one = normalize_forward(inputs, gain_attn)
    attn_in = normed.astype(jnp.bfloat16)
    bias = bias_rows(rel_table)
    proj = dot(attn_in, w_qkv).astype(jnp.bfloat16)
    mixed, stat = attention_forward(item_lengths, bias, proj)
    attn = dot(mixed, w_attn_out)
    resid = inputs + attn
    second, unit_two, scale_two = normalize_forward(resid, gain_moe)
    moe_in = second.astype(jnp.bfloat16)
    *packed, _ = lax.optimization_barrier((*pack(target_rows, moe_in, experts, capacity), raw))
    rows = exchange(packed)
    logits = dot(moe_in, w_router)
    chosen = jnp.stack([jnp.sum(jnp.where(pick, logits, 0.0), axis=1) for pick in picks], axis=1)
    highest = jnp.max(chosen, axis=1, keepdims=True)
    exps = jnp.exp(chosen - highest)
    gates = exps / jnp.sum(exps, axis=1, keepdims=True)
    gate_weight, up_weight, down_weight = w_gate[0], w_up[0], w_down[0]
    router_rows = jnp.pad(w_router.T, ((0, TILE - experts), (0, 0)))
    slope, other = slope_rows(raw, down_weight, experts, capacity)
    weights = (gate_weight, up_weight, router_rows, other)
    kept, near_share, near_router, near_pairs = expert_rows(own, rows[:1], slope, *weights, 0, ())
    back = [near(near_pairs[0])]
    rows[1:] = [after(block, near_pairs[0]) for block in rows[1:]]
    kept, far_share, far_router, far_pairs = expert_rows(own, rows[1:], slope, *weights, 1, kept)
    back += [swap(block, "expert", half + step) for step, block in enumerate(far_pairs)]
    hidden, gate_pre_grad, up_pre_grad = kept
    shares = (near_share, far_share)
    hidden = after(hidden, back[0])
    weight_grad = weight_grads(hidden, gate_pre_grad, up_pre_grad, shares, rows, raw, copies, capacity)
    weight_sum = lax.psum_scatter(weight_grad, "dp", scatter_dimension=0, tiled=True)
    result = result_rows(after(hidden, weight_grad), down_weight, [block.shape for block in rows])
    *back, held = lax.optimization_barrier((*back, result[0]))
    result = [after(block, *back) for block in (held, *result[1:])]
    returned = exchange(result)
    resid_grad, attn_grad, gain_moe_grad = combine(
        target, gates, resid, scale_two, gain_moe.reshape(1, width), cotangent, back
    )
    mixed_grad = dot(attn_grad, w_attn_out, NT).astype(jnp.bfloat16)
    proj_grad, tiles = attention_backward(item_lengths, bias, stat, proj, mixed, mixed_grad)
    unit = width // (copies * ways)
    mine, away = shared_grads(own % 2, attn_in, proj_grad, mixed, attn_grad, unit)
    pieces = chip_sums(mine, after(away, *returned), unit)
    proj_grad = after(proj_grad, *pieces)
    table_grad = table_sums(tiles, buckets)
    router_grad = (near_router + far_router)[:experts].T
    attn_in_grad = dot(proj_grad, w_qkv, NT)
    input_norm_grad, gain_attn_grad = normalize_backward(attn_in_grad, unit_one, scale_one, gain_attn)
    input_grad = resid_grad + input_norm_grad
    output = combine_output(target, gates, after(resid, *pieces), returned)
    small = (table_grad.reshape(-1), gain_attn_grad, gain_moe_grad, router_grad)
    sizes = [part.size // (copies * ways) for part in small]
    together = jnp.concatenate([part.reshape(copies * ways, -1) for part in small], axis=1)
    halves = device_sums(pieces, unit, input_grad, output, together)
    together = lax.all_to_all(together, ("dp", "expert"), split_axis=0, concat_axis=0, tiled=True)
    together = jnp.sum(together, axis=0)
    at = [sum(sizes[:k]) for k in range(5)]
    table_sum, attn_sum, moe_sum, router_sum = [together[at[k] : at[k + 1]] for k in range(4)]
    piece = width // copies
    down_sum = jnp.concatenate(
        [weight_sum[:, 2 * width + k * piece : 2 * width + (k + 1) * piece] for k in range(copies)], axis=0
    )
    experts_out = (
        weight_sum[:, :width].astype(jnp.float32).T[None],
        weight_sum[:, width : 2 * width].astype(jnp.float32).T[None],
        down_sum.astype(jnp.float32)[None],
    )
    arrived = [swap(part, "expert", 2 * step) if step else part for step, part in enumerate(halves)]
    *arrived, _ = lax.optimization_barrier((*arrived, experts_out))
    sums = sum(part.astype(jnp.float32) for part in arrived)
    return (
        output,
        input_grad,
        sums[:, : 3 * width],
        sums[:, 3 * width :],
        table_sum,
        attn_sum,
        moe_sum,
        router_sum.reshape(-1, experts),
        *experts_out,
    )


def solution(mesh):
    return jax.shard_map(
        on_device,
        mesh=mesh,
        in_specs=(
            P(("dp", "expert"), None),
            P(("dp", "expert"), None),
            P(("dp", "expert"), None),
            P(),
            P(),
            P(),
            P(),
            P(),
            P(),
            P("expert", None, None),
            P("expert", None, None),
            P("expert", None, None),
            P(("dp", "expert"), None),
        ),
        out_specs=(
            P(("dp", "expert"), None),
            P(("dp", "expert"), None),
            P(("dp", "expert"), None),
            P(("dp", "expert"), None),
            P(("dp", "expert")),
            P(("dp", "expert")),
            P(("dp", "expert")),
            P(("dp", "expert"), None),
            P("expert", None, "dp"),
            P("expert", None, "dp"),
            P("expert", None, "dp"),
        ),
        check_vma=False,
    )
```

```python
import jax
import jax.numpy as jnp
from jax import lax
from jax.experimental import pallas as pl
from jax.experimental.pallas import tpu as pltpu
from jax.sharding import PartitionSpec as P

TOP = 2
LONG_LEN = 512
SHORT_LEN = 128
TOK_DEV = 640
BOUNDS = (12, 16, 23, 32, 46, 64, 91)
EPSILON = 1e-06
HIGHEST = lax.Precision.HIGHEST
TILE = 128
FT = 256
NEG = -1e30
NN = (((1,), (0,)), ((), ()))
NT = (((1,), (1,)), ((), ()))
TN = (((0,), (0,)), ((), ()))
CURVE = 0.7978845608028654
CUBE = 0.044715
EXTRA = 8
SMALL = pl.CostEstimate(flops=1 << 20, bytes_accessed=1 << 16, transcendentals=0)
MEDIUM = pl.CostEstimate(flops=238_050_000_000, bytes_accessed=1 << 16, transcendentals=0)
LARGE = pl.CostEstimate(flops=1 << 38, bytes_accessed=1 << 28, transcendentals=0)


def dot(a, b, dims=NN):
    return lax.dot_general(a, b, dims, preferred_element_type=jnp.float32)


def normalize_forward(value, gain):
    scale = lax.rsqrt(jnp.mean(value * value, axis=-1, keepdims=True) + EPSILON)
    unit = value * scale
    return (unit * gain, unit, scale)


def normalize_backward(grad, unit, scale, gain):
    gain_grad = jnp.sum(grad * unit, axis=0)
    along = grad * gain
    inner = jnp.mean(along * unit, axis=-1, keepdims=True)
    return (scale * (along - unit * inner), gain_grad)


def bias_strip(bias_row):
    wide = jnp.broadcast_to(bias_row, (TILE, bias_row.shape[1]))
    return pltpu.roll(wide, 0, 1, stride=1, stride_axis=0)


def bias_tile(strip, bias_row, step):
    if abs(step) <= 1:
        start = 2 * TILE - step * TILE
        return strip[:, start : start + TILE]
    last = bias_row.shape[1] - 1
    return bias_row[:, 0:1] if step > 0 else bias_row[:, last : last + 1]


def items_of(tokens, lengths_ref):
    return ((0, LONG_LEN, lengths_ref[0, 0], LONG_LEN // 2), (LONG_LEN, tokens, lengths_ref[0, 1], SHORT_LEN // 2))


def attention_forward_kernel(lengths_ref, bias_ref, q_ref, k_ref, v_ref, mixed_ref, stat_ref, score_ref, exp_ref):
    tokens, lanes = q_ref.shape
    size = lanes // 2
    lane = lax.broadcasted_iota(jnp.int32, (1, lanes), 1)
    values_t = v_ref[...].T
    for start, stop, visible, sure in items_of(tokens, lengths_ref):
        length = stop - start
        count = length // TILE
        outs = []
        for head in range(2):
            bias_row = bias_ref[0, head : head + 1, :]
            strip = bias_strip(bias_row)
            own = (lane >= head * size) & (lane < (head + 1) * size)
            query = jnp.where(own, q_ref[start:stop, :] * 0.125, 0.0).astype(jnp.bfloat16)
            score_ref[0:length, 0:length] = dot(k_ref[start:stop, :], query, NT)
            totals = []
            for col in range(count):
                cols = slice(col * TILE, (col + 1) * TILE)
                top = None
                for row in range(count):
                    rows = slice(row * TILE, (row + 1) * TILE)
                    tile = score_ref[rows, cols] + bias_tile(strip, bias_row, row - col)
                    if (row + 1) * TILE > sure:
                        place = lax.broadcasted_iota(jnp.int32, (TILE, 1), 0) + row * TILE
                        tile = jnp.where(place < visible, tile, NEG)
                    score_ref[rows, cols] = tile
                    peak = jnp.max(tile, axis=0, keepdims=True)
                    top = peak if top is None else jnp.maximum(top, peak)
                total = jnp.zeros((1, TILE), jnp.float32)
                for row in range(count):
                    rows = slice(row * TILE, (row + 1) * TILE)
                    tile = jnp.exp(score_ref[rows, cols] - top)
                    total = total + jnp.sum(tile, axis=0, keepdims=True)
                    exp_ref[rows, cols] = tile.astype(jnp.bfloat16)
                totals.append(total)
                stat_ref[0, head : head + 1, start + col * TILE : start + (col + 1) * TILE] = top + jnp.log(total)
            total = jnp.concatenate(totals, axis=1)
            out = dot(values_t[head * size : (head + 1) * size, start:stop], exp_ref[0:length, 0:length])
            outs.append(out / total)
        mixed_ref[start:stop, :] = jnp.concatenate(outs, axis=0).T.astype(jnp.bfloat16)


def attention_forward(lengths, bias, proj):
    tokens, width = proj.shape[0], proj.shape[1] // 3
    lanes = TILE
    pairs = width // lanes
    return pl.pallas_call(
        attention_forward_kernel,
        grid=(pairs,),
        in_specs=[
            pl.BlockSpec(memory_space=pltpu.SMEM),
            pl.BlockSpec((1, 2, bias.shape[2]), lambda p: (p, 0, 0)),
            pl.BlockSpec((tokens, lanes), lambda p: (0, p)),
            pl.BlockSpec((tokens, lanes), lambda p: (0, pairs + p)),
            pl.BlockSpec((tokens, lanes), lambda p: (0, 2 * pairs + p)),
        ],
        out_specs=[
            pl.BlockSpec((tokens, lanes), lambda p: (0, p)),
            pl.BlockSpec((1, 2, tokens), lambda p: (p, 0, 0)),
        ],
        out_shape=[
            jax.ShapeDtypeStruct((tokens, width), jnp.bfloat16),
            jax.ShapeDtypeStruct((pairs, 2, tokens), jnp.float32),
        ],
        scratch_shapes=[pltpu.VMEM((LONG_LEN, LONG_LEN), jnp.float32), pltpu.VMEM((LONG_LEN, LONG_LEN), jnp.bfloat16)],
        cost_estimate=SMALL,
        name="attention_forward",
    )(lengths, bias, proj, proj, proj)


def attention_backward_kernel(
    lengths_ref, bias_ref, stat_ref, q_ref, k_ref, v_ref, mixed_ref, grad_ref, proj_ref, table_ref,
    score_ref, slope_ref, weight_ref, change_ref, stage_ref, done_ref,
):
    pair = pl.program_id(0)
    pairs = pl.num_programs(0)
    slot = pair % 2

    def copy(part, step):
        at = pl.multiple_of((part * pairs + step) * TILE, TILE)
        return pltpu.make_async_copy(
            stage_ref.at[step % 2, part], proj_ref.at[:, pl.ds(at, TILE)], done_ref.at[step % 2, part]
        )

    @pl.when(pair >= 2)
    def _():
        for part in range(3):
            copy(part, pair - 2).wait()

    tokens, lanes = q_ref.shape
    size = lanes // 2
    lane = lax.broadcasted_iota(jnp.int32, (1, lanes), 1)
    keys_t = k_ref[...].T
    product = (grad_ref[...].astype(jnp.float32) * mixed_ref[...].astype(jnp.float32)).T
    table_ref[...] = jnp.zeros_like(table_ref)
    for start, stop, visible, sure in items_of(tokens, lengths_ref):
        length = stop - start
        count = length // TILE
        query_grads, key_grads, value_grads = [], [], []
        for head in range(2):
            bias_row = bias_ref[0, head : head + 1, :]
            strip = bias_strip(bias_row)
            own = (lane >= head * size) & (lane < (head + 1) * size)
            query = jnp.where(own, q_ref[start:stop, :] * 0.125, 0.0).astype(jnp.bfloat16)
            grad = jnp.where(own, grad_ref[start:stop, :], 0.0).astype(jnp.bfloat16)
            score_ref[0:length, 0:length] = dot(k_ref[start:stop, :], query, NT)
            slope_ref[0:length, 0:length] = dot(v_ref[start:stop, :], grad, NT)
            inner = jnp.sum(product[head * size : (head + 1) * size, start:stop], axis=0, keepdims=True)
            sums = {-1: None, 0: None, 1: None}
            far = {-1: None, 1: None}
            for col in range(count):
                cols = slice(col * TILE, (col + 1) * TILE)
                base = stat_ref[0, head : head + 1, start + col * TILE : start + (col + 1) * TILE]
                middle = inner[:, cols]
                for row in range(count):
                    rows = slice(row * TILE, (row + 1) * TILE)
                    step = row - col
                    tile = score_ref[rows, cols] + (bias_tile(strip, bias_row, step) - base)
                    if (row + 1) * TILE > sure:
                        place = lax.broadcasted_iota(jnp.int32, (TILE, 1), 0) + row * TILE
                        tile = jnp.where(place < visible, tile, NEG)
                    tile = jnp.exp(tile)
                    weight_ref[rows, cols] = tile.astype(jnp.bfloat16)
                    tile = tile * (slope_ref[rows, cols] - middle)
                    change_ref[rows, cols] = tile.astype(jnp.bfloat16)
                    if abs(step) <= 1:
                        sums[step] = tile if sums[step] is None else sums[step] + tile
                    else:
                        side = 1 if step > 0 else -1
                        part = jnp.sum(tile, axis=0, keepdims=True)
                        far[side] = part if far[side] is None else far[side] + part
            for step, value in sums.items():
                if value is not None:
                    at = TILE - step * TILE
                    table_ref[0, head, 0:TILE, at : at + TILE] += value
            for side, value in far.items():
                if value is not None:
                    at = TILE - side * TILE
                    table_ref[0, head, TILE : TILE + 1, at : at + TILE] = value
            value_grads.append(dot(weight_ref[0:length, 0:length], grad))
            key_grads.append(dot(change_ref[0:length, 0:length], query))
            query_grads.append(dot(keys_t[head * size : (head + 1) * size, start:stop], change_ref[0:length, 0:length]))
        stage_ref[slot, 0, start:stop, :] = (jnp.concatenate(query_grads, axis=0).T * 0.125).astype(jnp.bfloat16)
        stage_ref[slot, 1, start:stop, :] = (key_grads[0] + key_grads[1]).astype(jnp.bfloat16)
        stage_ref[slot, 2, start:stop, :] = (value_grads[0] + value_grads[1]).astype(jnp.bfloat16)
    for part in range(3):
        copy(part, pair).start()

    @pl.when(pair == pairs - 1)
    def _():
        for part in range(3):
            copy(part, pair - 1).wait()
            copy(part, pair).wait()


def attention_backward(lengths, bias, stat, proj, mixed, grad):
    tokens, width = mixed.shape
    lanes = TILE
    pairs = width // lanes
    return pl.pallas_call(
        attention_backward_kernel,
        grid=(pairs,),
        in_specs=[
            pl.BlockSpec(memory_space=pltpu.SMEM),
            pl.BlockSpec((1, 2, bias.shape[2]), lambda p: (p, 0, 0)),
            pl.BlockSpec((1, 2, tokens), lambda p: (p, 0, 0)),
            pl.BlockSpec((tokens, lanes), lambda p: (0, p)),
            pl.BlockSpec((tokens, lanes), lambda p: (0, pairs + p)),
            pl.BlockSpec((tokens, lanes), lambda p: (0, 2 * pairs + p)),
            pl.BlockSpec((tokens, lanes), lambda p: (0, p)),
            pl.BlockSpec((tokens, lanes), lambda p: (0, p)),
        ],
        out_specs=[
            pl.BlockSpec(memory_space=pl.ANY),
            pl.BlockSpec((1, 2, TILE + 8, 3 * TILE), lambda p: (p, 0, 0, 0)),
        ],
        out_shape=[
            jax.ShapeDtypeStruct((tokens, 3 * width), jnp.bfloat16),
            jax.ShapeDtypeStruct((pairs, 2, TILE + 8, 3 * TILE), jnp.float32),
        ],
        scratch_shapes=[
            pltpu.VMEM((LONG_LEN, LONG_LEN), jnp.float32),
            pltpu.VMEM((LONG_LEN, LONG_LEN), jnp.float32),
            pltpu.VMEM((LONG_LEN, LONG_LEN), jnp.bfloat16),
            pltpu.VMEM((LONG_LEN, LONG_LEN), jnp.bfloat16),
            pltpu.VMEM((2, 3, tokens, lanes), jnp.bfloat16),
            pltpu.SemaphoreType.DMA((2, 3)),
        ],
        cost_estimate=SMALL,
        name="attention_backward",
    )(lengths, bias, stat, proj, proj, proj, mixed, grad)


def bucket_of(offset):
    distance = jnp.abs(offset)
    far = 8 + sum(((distance >= bound).astype(jnp.int32) for bound in BOUNDS))
    return jnp.where(distance < 8, distance, far) + 16 * (offset > 0).astype(jnp.int32)


def bias_rows(rel_table):
    bucket = bucket_of(2 * TILE - jnp.arange(4 * TILE, dtype=jnp.int32))
    onehot = (bucket[:, None] == jnp.arange(rel_table.shape[0], dtype=jnp.int32)[None, :]).astype(jnp.float32)
    return jnp.einsum("xb,bh->hx", onehot, rel_table, precision=HIGHEST).reshape(-1, 2, 4 * TILE)


def table_sums(tiles, buckets):
    row = jnp.arange(TILE + 8, dtype=jnp.int32)[:, None]
    col = jnp.arange(3 * TILE, dtype=jnp.int32)[None, :]
    near = bucket_of(row - col + TILE)
    far = jnp.where(col < TILE, buckets - 1, buckets // 2 - 1)
    bucket = jnp.where(row < TILE, near, far)
    onehot = (bucket[:, :, None] == jnp.arange(buckets, dtype=jnp.int32)).astype(jnp.float32)
    return jnp.einsum("ghrc,rcb->bgh", tiles, onehot, precision=HIGHEST).reshape(buckets, -1)


def pack_first_kernel(place_ref, routes_ref, rows_ref, *out_refs, experts, capacity):
    target_ref = out_refs[-1]
    tokens = routes_ref.shape[1]
    routes = [routes_ref[rank : rank + 1, :] for rank in range(TOP)]
    label = lax.broadcasted_iota(jnp.int32, (experts, 1), 0)
    picks = [label == route for route in routes]
    named = jnp.where(picks[0] | picks[1], 1.0, 0.0).astype(jnp.bfloat16)
    later = lax.broadcasted_iota(jnp.int32, (1, tokens), 1)
    earlier = lax.broadcasted_iota(jnp.int32, (tokens, 1), 0)
    count = dot(named, jnp.where(earlier < later, 1.0, 0.0).astype(jnp.bfloat16))
    for rank in range(TOP):
        position = jnp.sum(jnp.where(picks[rank], count, 0.0), axis=0, keepdims=True).astype(jnp.int32)
        apart = routes[rank] ^ place_ref[0]
        apart = jnp.where(apart < experts // 2, routes[rank] & (experts // 2 - 1), apart)
        target_ref[rank : rank + 1, :] = apart * capacity + position
    other = jnp.concatenate([routes[1], routes[0]], axis=0).astype(jnp.float32) + 1.0
    pack_kernel(target_ref, rows_ref, *out_refs[:-1], other=other, capacity=capacity)


def pack_kernel(target_ref, rows_ref, *out_refs, other=None, capacity):
    rows = rows_ref[...]
    base = 0
    for out_ref in out_refs:
        stride = capacity + (0 if other is None else EXTRA)
        for at in range(0, out_ref.shape[0], stride):
            slot = lax.broadcasted_iota(jnp.int32, (capacity, 1), 0) + base
            hits = [slot == target_ref[rank : rank + 1, :] for rank in range(TOP)]
            hit = jnp.where(hits[0] | hits[1], 1.0, 0.0).astype(jnp.bfloat16)
            out_ref[at : at + capacity, :] = dot(hit, rows).astype(jnp.bfloat16)
            if other is not None:
                named = sum(jnp.where(hits[rank], other[rank : rank + 1, :], 0.0) for rank in range(TOP))
                ones = jnp.ones((EXTRA, named.shape[1]), jnp.bfloat16)
                out_ref[at + capacity : at + stride, :] = jnp.zeros((EXTRA, out_ref.shape[1]), jnp.bfloat16)
                out_ref[at + capacity : at + stride, 0:capacity] = dot(ones, named.astype(jnp.bfloat16), NT).astype(jnp.bfloat16)
            base += capacity


def block_shapes(experts, rows, width):
    half = experts // 2
    return [jax.ShapeDtypeStruct((n * rows, width), jnp.bfloat16) for n in [half] + [1] * half]


def pack_first(place, routes, rows, experts, capacity):
    blocks = block_shapes(experts, capacity + EXTRA, rows.shape[1])
    *blocks, target = pl.pallas_call(
        lambda *refs: pack_first_kernel(*refs, experts=experts, capacity=capacity),
        in_specs=[pl.BlockSpec(memory_space=pltpu.SMEM), pl.BlockSpec(), pl.BlockSpec()],
        out_shape=blocks + [jax.ShapeDtypeStruct(routes.shape, jnp.int32)],
        cost_estimate=SMALL,
        name="pack_first",
    )(place, routes, rows)
    return blocks, target


def pack(target, rows, experts, capacity):
    return pl.pallas_call(
        lambda *refs: pack_kernel(*refs, capacity=capacity),
        out_shape=block_shapes(experts, capacity, rows.shape[1]),
        cost_estimate=SMALL,
        name="pack_rows",
    )(target, rows)


def gather_rows(target_ref, gates_ref, blocks):
    total = None
    base = 0
    for block in blocks:
        slot = lax.broadcasted_iota(jnp.int32, (1, block.shape[0]), 1) + base
        share = sum(
            jnp.where(target_ref[:, rank : rank + 1] == slot, gates_ref[:, rank : rank + 1], 0.0) for rank in range(TOP)
        )
        part = dot(share.astype(jnp.bfloat16), block[...])
        total = part if total is None else total + part
        base += block.shape[0]
    return total


def output_kernel(target_ref, gates_ref, resid_ref, *refs):
    refs[-1][...] = (resid_ref[...] + gather_rows(target_ref, gates_ref, refs[:-1])).astype(jnp.bfloat16)


def combine_output(target, gates, resid, blocks):
    return pl.pallas_call(
        output_kernel,
        out_shape=jax.ShapeDtypeStruct(resid.shape, jnp.bfloat16),
        cost_estimate=MEDIUM,
        name="combine_output",
    )(target, gates, resid, *blocks)


def combine_kernel(target_ref, gates_ref, resid_ref, scale_ref, gain_ref, upstream_ref, *refs):
    blocks, (grad_ref, low_ref, gain_grad_ref) = refs[:-3], refs[-3:]
    total = gather_rows(target_ref, gates_ref, blocks)
    scale = scale_ref[...]
    unit = resid_ref[...] * scale
    gain_grad_ref[...] = jnp.sum(total * unit, axis=0, keepdims=True)
    along = total * gain_ref[...]
    inner = jnp.mean(along * unit, axis=1, keepdims=True)
    grad = upstream_ref[...].astype(jnp.float32) + scale * (along - unit * inner)
    grad_ref[...] = grad
    low_ref[...] = grad.astype(jnp.bfloat16)


def combine(target, gates, resid, scale, gain, upstream, blocks):
    tokens, width = resid.shape
    return pl.pallas_call(
        combine_kernel,
        out_shape=[
            jax.ShapeDtypeStruct((tokens, width), jnp.float32),
            jax.ShapeDtypeStruct((tokens, width), jnp.bfloat16),
            jax.ShapeDtypeStruct((1, width), jnp.float32),
        ],
        cost_estimate=SMALL,
        name="combine_back",
    )(target, gates, resid, scale, gain, upstream, *blocks)


def spans(blocks, capacity, extra=0):
    base = 0
    for block in blocks:
        for at in range(0, block.shape[0], capacity + extra):
            yield block, at, base
            base += capacity


def expert_kernel(own_ref, slope_ref, wg_ref, wu_ref, wr_ref, other_ref, *refs, ways, parts):
    blocks, refs = refs[:ways], refs[-(8 + ways) :]
    hidden_ref, gate_ref, up_ref, share_ref, router_ref = refs[:5]
    pairs, (x_ref, acc_ref, dots_ref) = refs[5 : 5 + ways], refs[5 + ways :]
    step = pl.program_id(0)
    rows = x_ref.shape[0] // parts

    @pl.when(step == 0)
    def _():
        acc_ref[...] = jnp.zeros_like(acc_ref)
        dots_ref[...] = jnp.zeros_like(dots_ref)
        base = 0
        for block in blocks:
            x_ref[base : base + block.shape[0], :] = block[...]
            base += block.shape[0]

    for part in range(parts):
        span = slice(part * rows, (part + 1) * rows)
        x = x_ref[span, :]
        gate = dot(x, wg_ref[...])
        up = dot(x, wu_ref[...])
        slope = slope_ref[span, :].astype(jnp.float32)
        square = gate * gate
        rise = 0.5 + 0.5 * jnp.tanh(gate * (CURVE + (CURVE * CUBE) * square))
        unit = gate * rise
        bend = rise + (unit - unit * rise) * (2 * CURVE + (6 * CURVE * CUBE) * square)
        hidden = (unit * up).astype(jnp.bfloat16)
        hidden_ref[span, :] = hidden
        both = hidden.astype(jnp.float32) * slope
        dots_ref[span, :] += both[:, 0:TILE] + both[:, TILE : 2 * TILE]
        gate_grad = (slope * up * bend).astype(jnp.bfloat16)
        up_grad = (slope * unit).astype(jnp.bfloat16)
        gate_ref[span, :] = gate_grad
        up_ref[span, :] = up_grad
        acc_ref[span, :] += dot(gate_grad, wg_ref[...], NT) + dot(up_grad, wu_ref[...], NT)

    @pl.when(step == pl.num_programs(0) - 1)
    def _():
        logits = dot(x_ref[...], wr_ref[...], NT)
        label = lax.broadcasted_iota(jnp.int32, (1, TILE), 1)
        mine = label == own_ref[0]
        theirs = label == other_ref[:, 0:1].astype(jnp.int32) - 1
        first = jnp.sum(jnp.where(mine, logits, 0.0), axis=1, keepdims=True)
        second = jnp.sum(jnp.where(theirs, logits, 0.0), axis=1, keepdims=True)
        top = jnp.maximum(first, second)
        first = jnp.exp(first - top)
        second = jnp.exp(second - top)
        total = first + second
        first = first / total
        second = second / total
        inner = jnp.sum(dots_ref[...], axis=1, keepdims=True)
        coef = inner * second * (jnp.where(mine, 1.0, 0.0) - jnp.where(theirs, 1.0, 0.0))
        share_ref[...] = jnp.broadcast_to(first, share_ref.shape)
        router_ref[...] = dot((first * coef).astype(jnp.bfloat16), x_ref[...], TN)
        acc_ref[...] += dot(coef.astype(jnp.bfloat16), wr_ref[...])
        base = 0
        for pair in pairs:
            pair[...] = acc_ref[base : base + pair.shape[0], :].astype(jnp.bfloat16)
            base += pair.shape[0]


def once(shape):
    return pl.BlockSpec(shape, lambda i: (0, 0), pipeline_mode=pl.Buffered(1))


def expert_rows(own, blocks, slope, wg, wu, wr, other, chunk, kept, parts=2):
    n = slope.shape[0] // 2
    d, f = wg.shape
    ways = len(blocks)
    tile = pl.BlockSpec((n, FT), lambda i: (chunk, i))
    weight = pl.BlockSpec((d, FT), lambda i: (0, i))
    fixed = lambda shape: pl.BlockSpec(shape, lambda i: (0, 0))
    hidden, gate, up, share, router, *pairs = pl.pallas_call(
        lambda *refs: expert_kernel(*refs, ways=ways, parts=parts),
        grid=(f // FT,),
        in_specs=[
            pl.BlockSpec(memory_space=pltpu.SMEM),
            tile,
            weight,
            weight,
            once((TILE, d)),
            pl.BlockSpec((n, TILE), lambda i: (chunk, 0), pipeline_mode=pl.Buffered(1)),
        ]
        + [once(block.shape) for block in blocks]
        + [pl.BlockSpec(memory_space=pl.ANY) for _ in kept],
        out_specs=[tile, tile, tile, fixed((n, TILE)), fixed((TILE, d))] + [fixed(block.shape) for block in blocks],
        out_shape=[jax.ShapeDtypeStruct((2 * n, f), jnp.bfloat16)] * 3
        + [jax.ShapeDtypeStruct((n, TILE), jnp.float32), jax.ShapeDtypeStruct((TILE, d), jnp.float32)]
        + [jax.ShapeDtypeStruct(block.shape, jnp.bfloat16) for block in blocks],
        scratch_shapes=[
            pltpu.VMEM((n, d), jnp.bfloat16),
            pltpu.VMEM((n, d), jnp.float32),
            pltpu.VMEM((n, TILE), jnp.float32),
        ],
        input_output_aliases={6 + ways + k: k for k in range(len(kept))},
        cost_estimate=LARGE if chunk else SMALL,
        name="expert_rows",
    )(own, slope, wg, wu, wr, other, *blocks, *kept)
    return (hidden, gate, up), share, router, pairs


def slope_kernel(wd_ref, *refs, capacity):
    blocks, (out_ref, other_ref, u_ref) = refs[:-3], refs[-3:]

    @pl.when(pl.program_id(0) == 0)
    def _():
        reach = -(-capacity // TILE) * TILE
        for block, at, base in spans(blocks, capacity, EXTRA):
            u_ref[base : base + capacity, :] = block[at : at + capacity, :]
            named = block[at + capacity : at + capacity + EXTRA, 0:reach].astype(jnp.float32).T
            other_ref[base : base + capacity, :] = jnp.broadcast_to(named[0:capacity, 0:1], (capacity, TILE))

    out_ref[...] = dot(u_ref[...], wd_ref[...], NT).astype(jnp.bfloat16)


def slope_rows(blocks, wd, experts, capacity):
    f, d = wd.shape
    n = experts * capacity
    return pl.pallas_call(
        lambda *refs: slope_kernel(*refs, capacity=capacity),
        grid=(f // FT,),
        in_specs=[pl.BlockSpec((FT, d), lambda i: (i, 0))] + [once(block.shape) for block in blocks],
        out_specs=[pl.BlockSpec((n, FT), lambda i: (0, i)), pl.BlockSpec((n, TILE), lambda i: (0, 0))],
        out_shape=[jax.ShapeDtypeStruct((n, f), jnp.bfloat16), jax.ShapeDtypeStruct((n, TILE), jnp.float32)],
        scratch_shapes=[pltpu.VMEM((n, d), jnp.bfloat16)],
        cost_estimate=LARGE,
        name="slope_rows",
    )(wd, *blocks)


def gate_slots(target_ref, blocks, near_ref, far_ref, capacity, extra):
    for block, at, base in spans(blocks, capacity, extra):
        share_ref, start = (near_ref, base) if base < near_ref.shape[0] else (far_ref, base - near_ref.shape[0])
        value = block[at : at + capacity, :].astype(jnp.float32) * share_ref[start : start + capacity, 0:1]
        target_ref[base : base + capacity, :] = value.astype(jnp.bfloat16)


def weight_kernel(hidden, gate, up, near_ref, far_ref, *refs, ways, copies, capacity):
    rows, raw, refs = refs[:ways], refs[ways : 2 * ways], refs[2 * ways :]
    out_ref, rows_ref, raw_ref, stage_ref, down_ref, done_ref, sent_ref = refs
    step = pl.program_id(0)
    steps = pl.num_programs(0)
    d = stage_ref.shape[2] // 2
    piece = d // copies
    part_of = out_ref.shape[0] // copies

    def whole(at):
        return pltpu.make_async_copy(
            stage_ref.at[at % 2], out_ref.at[pl.ds(pl.multiple_of(at * FT, FT), FT), 0 : 2 * d], done_ref.at[at % 2]
        )

    def small(at, part, copy):
        row = at * FT + part * 64
        column = pl.multiple_of(2 * d + row // part_of * piece, piece)
        return pltpu.make_async_copy(
            down_ref.at[at % 2, part * 64 : (part + 1) * 64, copy * piece : (copy + 1) * piece],
            out_ref.at[pl.ds(pl.multiple_of(copy * part_of + row % part_of, 64), 64), pl.ds(column, piece)],
            sent_ref.at[at % 2, part, copy],
        )

    def finish(at):
        whole(at).wait()
        for part in range(FT // 64):
            for copy in range(copies):
                small(at, part, copy).wait()

    @pl.when(step == 0)
    def _():
        gate_slots(rows_ref, rows, near_ref, far_ref, capacity, 0)
        gate_slots(raw_ref, raw, near_ref, far_ref, capacity, EXTRA)

    @pl.when(step >= 2)
    def _():
        finish(step - 2)

    slot = step % 2
    stage_ref[slot, :, 0:d] = dot(gate[...], rows_ref[...], TN).astype(jnp.bfloat16)
    stage_ref[slot, :, d : 2 * d] = dot(up[...], rows_ref[...], TN).astype(jnp.bfloat16)
    down_ref[slot] = dot(hidden[...], raw_ref[...], TN).astype(jnp.bfloat16)
    whole(step).start()
    for part in range(FT // 64):
        for copy in range(copies):
            small(step, part, copy).start()

    @pl.when(step == steps - 1)
    def _():
        finish(step - 1)
        finish(step)


def weight_grads(hidden, gate, up, shares, rows, raw, copies, capacity):
    n, f = hidden.shape
    d = rows[0].shape[1]
    ways = len(rows)
    narrow = pl.BlockSpec((n, FT), lambda i: (0, i))
    return pl.pallas_call(
        lambda *refs: weight_kernel(*refs, ways=ways, copies=copies, capacity=capacity),
        grid=(f // FT,),
        in_specs=[narrow] * 3 + [once(part.shape) for part in (*shares, *rows, *raw)],
        out_specs=pl.BlockSpec(memory_space=pl.ANY),
        out_shape=jax.ShapeDtypeStruct((f, 3 * d), jnp.bfloat16),
        scratch_shapes=[
            pltpu.VMEM((n, d), jnp.bfloat16),
            pltpu.VMEM((n, d), jnp.bfloat16),
            pltpu.VMEM((2, FT, 2 * d), jnp.bfloat16),
            pltpu.VMEM((2, FT, d), jnp.bfloat16),
            pltpu.SemaphoreType.DMA((2,)),
            pltpu.SemaphoreType.DMA((2, FT // 64, copies)),
        ],
        cost_estimate=SMALL,
        name="weight_grads",
    )(hidden, gate, up, *shares, *rows, *raw)


def result_kernel(hidden_ref, wd_ref, *refs):
    results, acc_ref = refs[:-1], refs[-1]
    step = pl.program_id(0)
    part = dot(hidden_ref[...], wd_ref[...])

    @pl.when(step == 0)
    def _():
        acc_ref[...] = part

    @pl.when(step > 0)
    def _():
        acc_ref[...] += part

    @pl.when(step == pl.num_programs(0) - 1)
    def _():
        base = 0
        for result in results:
            result[...] = acc_ref[base : base + result.shape[0], :].astype(jnp.bfloat16)
            base += result.shape[0]


def result_rows(hidden, wd, shapes):
    n, f = hidden.shape
    d = wd.shape[1]
    tile = FT * 2 if f % (FT * 2) == 0 else FT
    return pl.pallas_call(
        result_kernel,
        grid=(f // tile,),
        in_specs=[pl.BlockSpec((n, tile), lambda i: (0, i)), pl.BlockSpec((tile, d), lambda i: (i, 0))],
        out_specs=[pl.BlockSpec(shape, lambda i: (0, 0)) for shape in shapes],
        out_shape=[jax.ShapeDtypeStruct(shape, jnp.bfloat16) for shape in shapes],
        scratch_shapes=[pltpu.VMEM((n, d), jnp.float32)],
        cost_estimate=SMALL,
        name="result_rows",
    )(hidden, wd)


def shared_kernel(
    core_ref, first_ref, wide_ref, second_ref, narrow_ref, mine_ref, away_ref, left_ref, *, steps, unit
):
    step = pl.program_id(0)

    def store(value):
        own = core_ref[0] == 0
        for group in range(mine_ref.shape[0] // unit):
            low = value[2 * group * unit : (2 * group + 1) * unit, :]
            high = value[(2 * group + 1) * unit : (2 * group + 2) * unit, :]
            span = slice(group * unit, (group + 1) * unit)
            mine_ref[span, :] = jnp.where(own, low, high).astype(jnp.bfloat16)
            away_ref[span, :] = jnp.where(own, high, low).astype(jnp.bfloat16)

    @pl.when(step == 0)
    def _():
        left_ref[...] = first_ref[...].T

    @pl.when(step == steps)
    def _():
        left_ref[...] = second_ref[...].T

    @pl.when(step < steps)
    def _():
        store(dot(left_ref[...], wide_ref[...]))

    @pl.when(step >= steps)
    def _():
        store(dot(left_ref[...], narrow_ref[...]))


def shared_grads(core, first, wide, second, narrow, unit):
    tokens, rows = first.shape
    tile = 512
    steps, more = wide.shape[1] // tile, narrow.shape[1] // tile
    whole = once((tokens, rows))
    out = pl.BlockSpec((rows // 2, tile), lambda i: (0, i))
    shape = jax.ShapeDtypeStruct((rows // 2, wide.shape[1] + narrow.shape[1]), jnp.bfloat16)
    return pl.pallas_call(
        lambda *refs: shared_kernel(*refs, steps=steps, unit=unit),
        grid=(steps + more,),
        in_specs=[
            pl.BlockSpec(memory_space=pltpu.SMEM),
            whole,
            pl.BlockSpec((tokens, tile), lambda i: (0, jnp.minimum(i, steps - 1))),
            whole,
            pl.BlockSpec((tokens, tile), lambda i: (0, jnp.maximum(i - steps, 0))),
        ],
        out_specs=[out, out],
        out_shape=[shape, shape],
        scratch_shapes=[pltpu.VMEM((rows, tokens), jnp.bfloat16)],
        cost_estimate=SMALL,
        name="shared_grads",
    )(core, first, wide, second, narrow)


def after(value, *before):
    return lax.optimization_barrier((value,) + before)[0]


def swap(value, axis, step):
    size = lax.axis_size(axis)
    return lax.ppermute(value, axis, [(k, k ^ step) for k in range(size)])


def parted(value, bit):
    return [lax.dynamic_index_in_dim(value, place, 0, keepdims=False) for place in (bit, 1 - bit)]


def added(first, second):
    return (first.astype(jnp.float32) + second.astype(jnp.float32)).astype(jnp.bfloat16)


def dp_halves(mine, away, unit):
    copies, chips = lax.axis_size("dp"), lax.axis_size("expert") // 2
    parts = [array.reshape(copies // 2, 2, chips * unit, -1) for array in (mine, swap(away, "expert", 1))]
    place = lax.axis_index("dp")
    cut = mine.shape[1] // 2
    low = [jnp.swapaxes(part[..., :cut], 0, 1) for part in parts]
    high = [part[..., cut:] for part in parts]
    halves = []
    for pair, bit in ((low, place % 2), (high, place // 2)):
        stay, leave = zip(*(parted(part, bit) for part in pair))
        halves.append((added(*stay), added(*leave)))
    return halves


def dp_sums(halves, unit, *work):
    place = lax.axis_index("dp")
    came = [swap(leave, "dp", step) for (_, leave), step in zip(halves, (1, 2))]
    *came, _ = lax.optimization_barrier((*came, work))
    total = []
    for (stay, _), other, bit, step in zip(halves, came, (place // 2, place % 2), (2, 1)):
        mine, mine_too = (parted(part, bit) for part in (stay, other))
        leave = swap(added(mine[1], mine_too[1]), "dp", step)
        total.append(mine[0].astype(jnp.float32) + mine_too[0].astype(jnp.float32) + leave.astype(jnp.float32))
    chips = lax.axis_size("expert") // 2
    total = jnp.concatenate(total, axis=1).astype(jnp.bfloat16).reshape(chips, unit, -1)
    place = lax.axis_index("expert") // 2
    return [lax.dynamic_index_in_dim(total, place ^ step, 0, keepdims=False) for step in range(chips)]


def on_device(
    block_input,
    routes,
    item_lengths,
    w_qkv,
    w_attn_out,
    rel_table,
    gain_attn,
    gain_moe,
    w_router,
    w_gate,
    w_up,
    w_down,
    cotangent,
):
    tokens, width = block_input.shape
    experts = w_router.shape[1]
    capacity = TOK_DEV * TOP * 5 // (4 * experts)
    slots = experts * capacity
    buckets = rel_table.shape[0]
    copies, ways = lax.axis_size("dp"), lax.axis_size("expert")
    place = lax.axis_index("expert").astype(jnp.int32)
    own = place.reshape(1)
    labels = jnp.arange(experts, dtype=jnp.int32)
    picks = [routes[:, rank : rank + 1] == labels[None, :] for rank in range(TOP)]
    places = jnp.arange(slots, dtype=jnp.int32)

    half = ways // 2
    groups = [list(range(k * half, (k + 1) * half)) for k in range(2)]

    def near(block):
        parts = block.reshape(half, -1, block.shape[1])
        parts = lax.all_to_all(parts, "expert", split_axis=0, concat_axis=0, axis_index_groups=groups, tiled=True)
        return parts.reshape(block.shape)

    def exchange(blocks, *before):
        far = [swap(block, "expert", half + step) for step, block in enumerate(blocks[1:])]
        return [near(after(blocks[0], *before))] + far

    packed, target_rows = pack_first(own, routes.T, cotangent, experts, capacity)
    target = target_rows.T
    block_input = after(block_input, *packed)
    inputs = block_input.astype(jnp.float32)
    normed, unit_one, scale_one = normalize_forward(inputs, gain_attn)
    raw = exchange(packed, scale_one)
    attn_in = normed.astype(jnp.bfloat16)
    bias = bias_rows(rel_table)
    proj = dot(attn_in, w_qkv).astype(jnp.bfloat16)
    mixed, stat = attention_forward(item_lengths, bias, proj)
    attn = dot(mixed, w_attn_out)
    resid = inputs + attn
    second, unit_two, scale_two = normalize_forward(resid, gain_moe)
    moe_in = second.astype(jnp.bfloat16)
    *packed, _ = lax.optimization_barrier((*pack(target_rows, moe_in, experts, capacity), raw))
    logits = dot(moe_in, w_router)
    chosen = jnp.stack([jnp.sum(jnp.where(pick, logits, 0.0), axis=1) for pick in picks], axis=1)
    highest = jnp.max(chosen, axis=1, keepdims=True)
    exps = jnp.exp(chosen - highest)
    gates = exps / jnp.sum(exps, axis=1, keepdims=True)
    rows = exchange(packed, gates)
    gate_weight, up_weight, down_weight = w_gate[0], w_up[0], w_down[0]
    router_rows = jnp.pad(w_router.T, ((0, TILE - experts), (0, 0)))
    slope, other = slope_rows(raw, down_weight, experts, capacity)
    weights = (gate_weight, up_weight, router_rows, other)
    kept, near_share, near_router, near_pairs = expert_rows(own, rows[:1], slope, *weights, 0, ())
    back = [near(near_pairs[0])]
    rows[1:] = [after(block, near_pairs[0]) for block in rows[1:]]
    kept, far_share, far_router, far_pairs = expert_rows(own, rows[1:], slope, *weights, 1, kept)
    back += [swap(block, "expert", half + step) for step, block in enumerate(far_pairs)]
    hidden, gate_pre_grad, up_pre_grad = kept
    shares = (near_share, far_share)
    hidden = after(hidden, back[0])
    weight_grad = weight_grads(hidden, gate_pre_grad, up_pre_grad, shares, rows, raw, copies, capacity)
    weight_sum = lax.psum_scatter(weight_grad, "dp", scatter_dimension=0, tiled=True)
    result = result_rows(after(hidden, weight_grad), down_weight, [block.shape for block in rows])
    *back, held = lax.optimization_barrier((*back, result[0]))
    result = [after(block, *back) for block in (held, *result[1:])]
    returned = exchange(result)
    resid_grad, attn_grad, gain_moe_grad = combine(
        target, gates, resid, scale_two, gain_moe.reshape(1, width), cotangent, back
    )
    mixed_grad = dot(attn_grad, w_attn_out, NT).astype(jnp.bfloat16)
    proj_grad, tiles = attention_backward(item_lengths, bias, stat, proj, mixed, mixed_grad)
    unit = width // (copies * ways)
    mine, away = shared_grads(own % 2, attn_in, proj_grad, mixed, attn_grad, unit)
    dp_parts = dp_halves(mine, after(away, *returned), unit)
    proj_grad, _ = lax.optimization_barrier((proj_grad, dp_parts))
    table_grad = table_sums(tiles, buckets)
    router_grad = (near_router + far_router)[:experts].T
    attn_in_grad = dot(proj_grad, w_qkv, NT)
    input_norm_grad, gain_attn_grad = normalize_backward(attn_in_grad, unit_one, scale_one, gain_attn)
    input_grad = resid_grad + input_norm_grad
    output = combine_output(target, gates, after(resid, dp_parts[0][1]), returned)
    small = (table_grad.reshape(-1), gain_attn_grad, gain_moe_grad, router_grad)
    sizes = [part.size // (copies * ways) for part in small]
    together = jnp.concatenate([part.reshape(copies * ways, -1) for part in small], axis=1)
    halves = dp_sums(dp_parts, unit, input_grad, output, together)
    together = lax.all_to_all(together, ("dp", "expert"), split_axis=0, concat_axis=0, tiled=True)
    together = jnp.sum(together, axis=0)
    at = [sum(sizes[:k]) for k in range(5)]
    table_sum, attn_sum, moe_sum, router_sum = [together[at[k] : at[k + 1]] for k in range(4)]
    piece = width // copies
    down_sum = jnp.concatenate(
        [weight_sum[:, 2 * width + k * piece : 2 * width + (k + 1) * piece] for k in range(copies)], axis=0
    )
    experts_out = (
        weight_sum[:, :width].astype(jnp.float32).T[None],
        weight_sum[:, width : 2 * width].astype(jnp.float32).T[None],
        down_sum.astype(jnp.float32)[None],
    )
    arrived = [swap(part, "expert", 2 * step) if step else part for step, part in enumerate(halves)]
    *arrived, _ = lax.optimization_barrier((*arrived, experts_out))
    sums = sum(part.astype(jnp.float32) for part in arrived)
    return (
        output,
        input_grad,
        sums[:, : 3 * width],
        sums[:, 3 * width :],
        table_sum,
        attn_sum,
        moe_sum,
        router_sum.reshape(-1, experts),
        *experts_out,
    )


def solution(mesh):
    return jax.shard_map(
        on_device,
        mesh=mesh,
        in_specs=(
            P(("dp", "expert"), None),
            P(("dp", "expert"), None),
            P(("dp", "expert"), None),
            P(),
            P(),
            P(),
            P(),
            P(),
            P(),
            P("expert", None, None),
            P("expert", None, None),
            P("expert", None, None),
            P(("dp", "expert"), None),
        ),
        out_specs=(
            P(("dp", "expert"), None),
            P(("dp", "expert"), None),
            P(("dp", "expert"), None),
            P(("dp", "expert"), None),
            P(("dp", "expert")),
            P(("dp", "expert")),
            P(("dp", "expert")),
            P(("dp", "expert"), None),
            P("expert", None, "dp"),
            P("expert", None, "dp"),
            P("expert", None, "dp"),
        ),
        check_vma=False,
    )
```

```python
import jax
import jax.numpy as jnp
from jax import lax
from jax.experimental import pallas as pl
from jax.experimental.pallas import tpu as pltpu
from jax.sharding import PartitionSpec as P

TOP = 2
LONG_LEN = 512
SHORT_LEN = 128
TOK_DEV = 640
BOUNDS = (12, 16, 23, 32, 46, 64, 91)
EPSILON = 1e-06
HIGHEST = lax.Precision.HIGHEST
TILE = 128
FT = 256
NEG = -1e30
NN = (((1,), (0,)), ((), ()))
NT = (((1,), (1,)), ((), ()))
TN = (((0,), (0,)), ((), ()))
CURVE = 0.7978845608028654
CUBE = 0.044715
EXTRA = 8
SHORT = pl.CostEstimate(flops=23_000_000_000, bytes_accessed=1 << 16, transcendentals=0)
SMALL = pl.CostEstimate(flops=1 << 20, bytes_accessed=1 << 16, transcendentals=0)
MEDIUM = pl.CostEstimate(flops=233_450_000_000, bytes_accessed=1 << 16, transcendentals=0)
LARGE = pl.CostEstimate(flops=1 << 38, bytes_accessed=1 << 28, transcendentals=0)


def dot(a, b, dims=NN):
    return lax.dot_general(a, b, dims, preferred_element_type=jnp.float32)


def normalize_forward(value, gain):
    scale = lax.rsqrt(jnp.mean(value * value, axis=-1, keepdims=True) + EPSILON)
    unit = value * scale
    return (unit * gain, unit, scale)


def normalize_backward(grad, unit, scale, gain):
    gain_grad = jnp.sum(grad * unit, axis=0)
    along = grad * gain
    inner = jnp.mean(along * unit, axis=-1, keepdims=True)
    return (scale * (along - unit * inner), gain_grad)


def bias_strip(bias_row):
    wide = jnp.broadcast_to(bias_row, (TILE, bias_row.shape[1]))
    return pltpu.roll(wide, 0, 1, stride=1, stride_axis=0)


def bias_tile(strip, bias_row, step):
    if abs(step) <= 1:
        start = 2 * TILE - step * TILE
        return strip[:, start : start + TILE]
    last = bias_row.shape[1] - 1
    return bias_row[:, 0:1] if step > 0 else bias_row[:, last : last + 1]


def items_of(tokens, lengths_ref):
    return ((0, LONG_LEN, lengths_ref[0, 0], LONG_LEN // 2), (LONG_LEN, tokens, lengths_ref[0, 1], SHORT_LEN // 2))


def attention_forward_kernel(lengths_ref, bias_ref, q_ref, k_ref, v_ref, mixed_ref, stat_ref, score_ref, exp_ref):
    tokens, lanes = q_ref.shape
    size = lanes // 2
    lane = lax.broadcasted_iota(jnp.int32, (1, lanes), 1)
    values_t = v_ref[...].T
    for start, stop, visible, sure in items_of(tokens, lengths_ref):
        length = stop - start
        count = length // TILE
        outs = []
        for head in range(2):
            bias_row = bias_ref[0, head : head + 1, :]
            strip = bias_strip(bias_row)
            own = (lane >= head * size) & (lane < (head + 1) * size)
            query = jnp.where(own, q_ref[start:stop, :] * 0.125, 0.0).astype(jnp.bfloat16)
            score_ref[0:length, 0:length] = dot(k_ref[start:stop, :], query, NT)
            totals = []
            for col in range(count):
                cols = slice(col * TILE, (col + 1) * TILE)
                top = None
                for row in range(count):
                    rows = slice(row * TILE, (row + 1) * TILE)
                    tile = score_ref[rows, cols] + bias_tile(strip, bias_row, row - col)
                    if (row + 1) * TILE > sure:
                        place = lax.broadcasted_iota(jnp.int32, (TILE, 1), 0) + row * TILE
                        tile = jnp.where(place < visible, tile, NEG)
                    score_ref[rows, cols] = tile
                    peak = jnp.max(tile, axis=0, keepdims=True)
                    top = peak if top is None else jnp.maximum(top, peak)
                total = jnp.zeros((1, TILE), jnp.float32)
                for row in range(count):
                    rows = slice(row * TILE, (row + 1) * TILE)
                    tile = jnp.exp(score_ref[rows, cols] - top)
                    total = total + jnp.sum(tile, axis=0, keepdims=True)
                    exp_ref[rows, cols] = tile.astype(jnp.bfloat16)
                totals.append(total)
                stat_ref[0, head : head + 1, start + col * TILE : start + (col + 1) * TILE] = top + jnp.log(total)
            total = jnp.concatenate(totals, axis=1)
            out = dot(values_t[head * size : (head + 1) * size, start:stop], exp_ref[0:length, 0:length])
            outs.append(out / total)
        mixed_ref[start:stop, :] = jnp.concatenate(outs, axis=0).T.astype(jnp.bfloat16)


def attention_forward(lengths, bias, proj):
    tokens, width = proj.shape[0], proj.shape[1] // 3
    lanes = TILE
    pairs = width // lanes
    return pl.pallas_call(
        attention_forward_kernel,
        grid=(pairs,),
        in_specs=[
            pl.BlockSpec(memory_space=pltpu.SMEM),
            pl.BlockSpec((1, 2, bias.shape[2]), lambda p: (p, 0, 0)),
            pl.BlockSpec((tokens, lanes), lambda p: (0, p)),
            pl.BlockSpec((tokens, lanes), lambda p: (0, pairs + p)),
            pl.BlockSpec((tokens, lanes), lambda p: (0, 2 * pairs + p)),
        ],
        out_specs=[
            pl.BlockSpec((tokens, lanes), lambda p: (0, p)),
            pl.BlockSpec((1, 2, tokens), lambda p: (p, 0, 0)),
        ],
        out_shape=[
            jax.ShapeDtypeStruct((tokens, width), jnp.bfloat16),
            jax.ShapeDtypeStruct((pairs, 2, tokens), jnp.float32),
        ],
        scratch_shapes=[pltpu.VMEM((LONG_LEN, LONG_LEN), jnp.float32), pltpu.VMEM((LONG_LEN, LONG_LEN), jnp.bfloat16)],
        cost_estimate=SMALL,
        name="attention_forward",
    )(lengths, bias, proj, proj, proj)


def attention_backward_kernel(
    lengths_ref, bias_ref, stat_ref, q_ref, k_ref, v_ref, mixed_ref, grad_ref, proj_ref, table_ref,
    score_ref, slope_ref, weight_ref, change_ref, stage_ref, done_ref,
):
    pair = pl.program_id(0)
    pairs = pl.num_programs(0)
    slot = pair % 2

    def copy(part, step):
        at = pl.multiple_of((part * pairs + step) * TILE, TILE)
        return pltpu.make_async_copy(
            stage_ref.at[step % 2, part], proj_ref.at[:, pl.ds(at, TILE)], done_ref.at[step % 2, part]
        )

    @pl.when(pair >= 2)
    def _():
        for part in range(3):
            copy(part, pair - 2).wait()

    tokens, lanes = q_ref.shape
    size = lanes // 2
    lane = lax.broadcasted_iota(jnp.int32, (1, lanes), 1)
    keys_t = k_ref[...].T
    product = (grad_ref[...].astype(jnp.float32) * mixed_ref[...].astype(jnp.float32)).T
    table_ref[...] = jnp.zeros_like(table_ref)
    for start, stop, visible, sure in items_of(tokens, lengths_ref):
        length = stop - start
        count = length // TILE
        query_grads, key_grads, value_grads = [], [], []
        for head in range(2):
            bias_row = bias_ref[0, head : head + 1, :]
            strip = bias_strip(bias_row)
            own = (lane >= head * size) & (lane < (head + 1) * size)
            query = jnp.where(own, q_ref[start:stop, :] * 0.125, 0.0).astype(jnp.bfloat16)
            grad = jnp.where(own, grad_ref[start:stop, :], 0.0).astype(jnp.bfloat16)
            score_ref[0:length, 0:length] = dot(k_ref[start:stop, :], query, NT)
            slope_ref[0:length, 0:length] = dot(v_ref[start:stop, :], grad, NT)
            inner = jnp.sum(product[head * size : (head + 1) * size, start:stop], axis=0, keepdims=True)
            sums = {-1: None, 0: None, 1: None}
            far = {-1: None, 1: None}
            for col in range(count):
                cols = slice(col * TILE, (col + 1) * TILE)
                base = stat_ref[0, head : head + 1, start + col * TILE : start + (col + 1) * TILE]
                middle = inner[:, cols]
                for row in range(count):
                    rows = slice(row * TILE, (row + 1) * TILE)
                    step = row - col
                    tile = score_ref[rows, cols] + (bias_tile(strip, bias_row, step) - base)
                    if (row + 1) * TILE > sure:
                        place = lax.broadcasted_iota(jnp.int32, (TILE, 1), 0) + row * TILE
                        tile = jnp.where(place < visible, tile, NEG)
                    tile = jnp.exp(tile)
                    weight_ref[rows, cols] = tile.astype(jnp.bfloat16)
                    tile = tile * (slope_ref[rows, cols] - middle)
                    change_ref[rows, cols] = tile.astype(jnp.bfloat16)
                    if abs(step) <= 1:
                        sums[step] = tile if sums[step] is None else sums[step] + tile
                    else:
                        side = 1 if step > 0 else -1
                        part = jnp.sum(tile, axis=0, keepdims=True)
                        far[side] = part if far[side] is None else far[side] + part
            for step, value in sums.items():
                if value is not None:
                    at = TILE - step * TILE
                    table_ref[0, head, 0:TILE, at : at + TILE] += value
            for side, value in far.items():
                if value is not None:
                    at = TILE - side * TILE
                    table_ref[0, head, TILE : TILE + 1, at : at + TILE] = value
            value_grads.append(dot(weight_ref[0:length, 0:length], grad))
            key_grads.append(dot(change_ref[0:length, 0:length], query))
            query_grads.append(dot(keys_t[head * size : (head + 1) * size, start:stop], change_ref[0:length, 0:length]))
        stage_ref[slot, 0, start:stop, :] = (jnp.concatenate(query_grads, axis=0).T * 0.125).astype(jnp.bfloat16)
        stage_ref[slot, 1, start:stop, :] = (key_grads[0] + key_grads[1]).astype(jnp.bfloat16)
        stage_ref[slot, 2, start:stop, :] = (value_grads[0] + value_grads[1]).astype(jnp.bfloat16)
    for part in range(3):
        copy(part, pair).start()

    @pl.when(pair == pairs - 1)
    def _():
        for part in range(3):
            copy(part, pair - 1).wait()
            copy(part, pair).wait()


def attention_backward(lengths, bias, stat, proj, mixed, grad):
    tokens, width = mixed.shape
    lanes = TILE
    pairs = width // lanes
    return pl.pallas_call(
        attention_backward_kernel,
        grid=(pairs,),
        in_specs=[
            pl.BlockSpec(memory_space=pltpu.SMEM),
            pl.BlockSpec((1, 2, bias.shape[2]), lambda p: (p, 0, 0)),
            pl.BlockSpec((1, 2, tokens), lambda p: (p, 0, 0)),
            pl.BlockSpec((tokens, lanes), lambda p: (0, p)),
            pl.BlockSpec((tokens, lanes), lambda p: (0, pairs + p)),
            pl.BlockSpec((tokens, lanes), lambda p: (0, 2 * pairs + p)),
            pl.BlockSpec((tokens, lanes), lambda p: (0, p)),
            pl.BlockSpec((tokens, lanes), lambda p: (0, p)),
        ],
        out_specs=[
            pl.BlockSpec(memory_space=pl.ANY),
            pl.BlockSpec((1, 2, TILE + 8, 3 * TILE), lambda p: (p, 0, 0, 0)),
        ],
        out_shape=[
            jax.ShapeDtypeStruct((tokens, 3 * width), jnp.bfloat16),
            jax.ShapeDtypeStruct((pairs, 2, TILE + 8, 3 * TILE), jnp.float32),
        ],
        scratch_shapes=[
            pltpu.VMEM((LONG_LEN, LONG_LEN), jnp.float32),
            pltpu.VMEM((LONG_LEN, LONG_LEN), jnp.float32),
            pltpu.VMEM((LONG_LEN, LONG_LEN), jnp.bfloat16),
            pltpu.VMEM((LONG_LEN, LONG_LEN), jnp.bfloat16),
            pltpu.VMEM((2, 3, tokens, lanes), jnp.bfloat16),
            pltpu.SemaphoreType.DMA((2, 3)),
        ],
        cost_estimate=SMALL,
        name="attention_backward",
    )(lengths, bias, stat, proj, proj, proj, mixed, grad)


def bucket_of(offset):
    distance = jnp.abs(offset)
    far = 8 + sum(((distance >= bound).astype(jnp.int32) for bound in BOUNDS))
    return jnp.where(distance < 8, distance, far) + 16 * (offset > 0).astype(jnp.int32)


def bias_rows(rel_table):
    bucket = bucket_of(2 * TILE - jnp.arange(4 * TILE, dtype=jnp.int32))
    onehot = (bucket[:, None] == jnp.arange(rel_table.shape[0], dtype=jnp.int32)[None, :]).astype(jnp.float32)
    return jnp.einsum("xb,bh->hx", onehot, rel_table, precision=HIGHEST).reshape(-1, 2, 4 * TILE)


def table_sums(tiles, buckets):
    row = jnp.arange(TILE + 8, dtype=jnp.int32)[:, None]
    col = jnp.arange(3 * TILE, dtype=jnp.int32)[None, :]
    near = bucket_of(row - col + TILE)
    far = jnp.where(col < TILE, buckets - 1, buckets // 2 - 1)
    bucket = jnp.where(row < TILE, near, far)
    onehot = (bucket[:, :, None] == jnp.arange(buckets, dtype=jnp.int32)).astype(jnp.float32)
    return jnp.einsum("ghrc,rcb->bgh", tiles, onehot, precision=HIGHEST).reshape(buckets, -1)


def pack_first_kernel(place_ref, routes_ref, rows_ref, *out_refs, experts, capacity):
    target_ref = out_refs[-1]
    tokens = routes_ref.shape[1]
    routes = [routes_ref[rank : rank + 1, :] for rank in range(TOP)]
    label = lax.broadcasted_iota(jnp.int32, (experts, 1), 0)
    picks = [label == route for route in routes]
    named = jnp.where(picks[0] | picks[1], 1.0, 0.0).astype(jnp.bfloat16)
    later = lax.broadcasted_iota(jnp.int32, (1, tokens), 1)
    earlier = lax.broadcasted_iota(jnp.int32, (tokens, 1), 0)
    count = dot(named, jnp.where(earlier < later, 1.0, 0.0).astype(jnp.bfloat16))
    for rank in range(TOP):
        position = jnp.sum(jnp.where(picks[rank], count, 0.0), axis=0, keepdims=True).astype(jnp.int32)
        apart = routes[rank] ^ place_ref[0]
        apart = jnp.where(apart < experts // 2, routes[rank] & (experts // 2 - 1), apart)
        target_ref[rank : rank + 1, :] = apart * capacity + position
    other = jnp.concatenate([routes[1], routes[0]], axis=0).astype(jnp.float32) + 1.0
    pack_kernel(target_ref, rows_ref, *out_refs[:-1], other=other, capacity=capacity)


def pack_kernel(target_ref, rows_ref, *out_refs, other=None, capacity):
    rows = rows_ref[...]
    base = 0
    for out_ref in out_refs:
        stride = capacity + (0 if other is None else EXTRA)
        for at in range(0, out_ref.shape[0], stride):
            slot = lax.broadcasted_iota(jnp.int32, (capacity, 1), 0) + base
            hits = [slot == target_ref[rank : rank + 1, :] for rank in range(TOP)]
            hit = jnp.where(hits[0] | hits[1], 1.0, 0.0).astype(jnp.bfloat16)
            out_ref[at : at + capacity, :] = dot(hit, rows).astype(jnp.bfloat16)
            if other is not None:
                named = sum(jnp.where(hits[rank], other[rank : rank + 1, :], 0.0) for rank in range(TOP))
                ones = jnp.ones((EXTRA, named.shape[1]), jnp.bfloat16)
                out_ref[at + capacity : at + stride, :] = jnp.zeros((EXTRA, out_ref.shape[1]), jnp.bfloat16)
                out_ref[at + capacity : at + stride, 0:capacity] = dot(ones, named.astype(jnp.bfloat16), NT).astype(jnp.bfloat16)
            base += capacity


def block_shapes(experts, rows, width):
    half = experts // 2
    return [jax.ShapeDtypeStruct((n * rows, width), jnp.bfloat16) for n in [half] + [1] * half]


def pack_first(place, routes, rows, experts, capacity):
    blocks = block_shapes(experts, capacity + EXTRA, rows.shape[1])
    *blocks, target = pl.pallas_call(
        lambda *refs: pack_first_kernel(*refs, experts=experts, capacity=capacity),
        in_specs=[pl.BlockSpec(memory_space=pltpu.SMEM), pl.BlockSpec(), pl.BlockSpec()],
        out_shape=blocks + [jax.ShapeDtypeStruct(routes.shape, jnp.int32)],
        cost_estimate=SMALL,
        name="pack_first",
    )(place, routes, rows)
    return blocks, target


def pack(target, rows, experts, capacity):
    return pl.pallas_call(
        lambda *refs: pack_kernel(*refs, capacity=capacity),
        out_shape=block_shapes(experts, capacity, rows.shape[1]),
        cost_estimate=SMALL,
        name="pack_rows",
    )(target, rows)


def gather_rows(target_ref, gates_ref, blocks):
    total = None
    base = 0
    for block in blocks:
        slot = lax.broadcasted_iota(jnp.int32, (1, block.shape[0]), 1) + base
        share = sum(
            jnp.where(target_ref[:, rank : rank + 1] == slot, gates_ref[:, rank : rank + 1], 0.0) for rank in range(TOP)
        )
        part = dot(share.astype(jnp.bfloat16), block[...])
        total = part if total is None else total + part
        base += block.shape[0]
    return total


def output_kernel(target_ref, gates_ref, resid_ref, *refs):
    refs[-1][...] = (resid_ref[...] + gather_rows(target_ref, gates_ref, refs[:-1])).astype(jnp.bfloat16)


def combine_output(target, gates, resid, blocks):
    return pl.pallas_call(
        output_kernel,
        out_shape=jax.ShapeDtypeStruct(resid.shape, jnp.bfloat16),
        cost_estimate=MEDIUM,
        name="combine_output",
    )(target, gates, resid, *blocks)


def combine_kernel(target_ref, gates_ref, resid_ref, scale_ref, gain_ref, upstream_ref, *refs):
    blocks, (grad_ref, low_ref, gain_grad_ref) = refs[:-3], refs[-3:]
    total = gather_rows(target_ref, gates_ref, blocks)
    scale = scale_ref[...]
    unit = resid_ref[...] * scale
    gain_grad_ref[...] = jnp.sum(total * unit, axis=0, keepdims=True)
    along = total * gain_ref[...]
    inner = jnp.mean(along * unit, axis=1, keepdims=True)
    grad = upstream_ref[...].astype(jnp.float32) + scale * (along - unit * inner)
    grad_ref[...] = grad
    low_ref[...] = grad.astype(jnp.bfloat16)


def combine(target, gates, resid, scale, gain, upstream, blocks):
    tokens, width = resid.shape
    return pl.pallas_call(
        combine_kernel,
        out_shape=[
            jax.ShapeDtypeStruct((tokens, width), jnp.float32),
            jax.ShapeDtypeStruct((tokens, width), jnp.bfloat16),
            jax.ShapeDtypeStruct((1, width), jnp.float32),
        ],
        cost_estimate=SMALL,
        name="combine_back",
    )(target, gates, resid, scale, gain, upstream, *blocks)


def spans(blocks, capacity, extra=0):
    base = 0
    for block in blocks:
        for at in range(0, block.shape[0], capacity + extra):
            yield block, at, base
            base += capacity


def expert_kernel(own_ref, slope_ref, wg_ref, wu_ref, wr_ref, other_ref, *refs, ways, parts):
    blocks, refs = refs[:ways], refs[-(8 + ways) :]
    hidden_ref, gate_ref, up_ref, share_ref, router_ref = refs[:5]
    pairs, (x_ref, acc_ref, dots_ref) = refs[5 : 5 + ways], refs[5 + ways :]
    step = pl.program_id(0)
    rows = x_ref.shape[0] // parts

    @pl.when(step == 0)
    def _():
        acc_ref[...] = jnp.zeros_like(acc_ref)
        dots_ref[...] = jnp.zeros_like(dots_ref)
        base = 0
        for block in blocks:
            x_ref[base : base + block.shape[0], :] = block[...]
            base += block.shape[0]

    for part in range(parts):
        span = slice(part * rows, (part + 1) * rows)
        x = x_ref[span, :]
        gate = dot(x, wg_ref[...])
        up = dot(x, wu_ref[...])
        slope = slope_ref[span, :].astype(jnp.float32)
        square = gate * gate
        rise = 0.5 + 0.5 * jnp.tanh(gate * (CURVE + (CURVE * CUBE) * square))
        unit = gate * rise
        bend = rise + (unit - unit * rise) * (2 * CURVE + (6 * CURVE * CUBE) * square)
        hidden = (unit * up).astype(jnp.bfloat16)
        hidden_ref[span, :] = hidden
        both = hidden.astype(jnp.float32) * slope
        dots_ref[span, :] += both[:, 0:TILE] + both[:, TILE : 2 * TILE]
        gate_grad = (slope * up * bend).astype(jnp.bfloat16)
        up_grad = (slope * unit).astype(jnp.bfloat16)
        gate_ref[span, :] = gate_grad
        up_ref[span, :] = up_grad
        acc_ref[span, :] += dot(gate_grad, wg_ref[...], NT) + dot(up_grad, wu_ref[...], NT)

    @pl.when(step == pl.num_programs(0) - 1)
    def _():
        logits = dot(x_ref[...], wr_ref[...], NT)
        label = lax.broadcasted_iota(jnp.int32, (1, TILE), 1)
        mine = label == own_ref[0]
        theirs = label == other_ref[:, 0:1].astype(jnp.int32) - 1
        first = jnp.sum(jnp.where(mine, logits, 0.0), axis=1, keepdims=True)
        second = jnp.sum(jnp.where(theirs, logits, 0.0), axis=1, keepdims=True)
        top = jnp.maximum(first, second)
        first = jnp.exp(first - top)
        second = jnp.exp(second - top)
        total = first + second
        first = first / total
        second = second / total
        inner = jnp.sum(dots_ref[...], axis=1, keepdims=True)
        coef = inner * second * (jnp.where(mine, 1.0, 0.0) - jnp.where(theirs, 1.0, 0.0))
        share_ref[...] = jnp.broadcast_to(first, share_ref.shape)
        router_ref[...] = dot((first * coef).astype(jnp.bfloat16), x_ref[...], TN)
        acc_ref[...] += dot(coef.astype(jnp.bfloat16), wr_ref[...])
        base = 0
        for pair in pairs:
            pair[...] = acc_ref[base : base + pair.shape[0], :].astype(jnp.bfloat16)
            base += pair.shape[0]


def once(shape):
    return pl.BlockSpec(shape, lambda i: (0, 0), pipeline_mode=pl.Buffered(1))


def expert_rows(own, blocks, slope, wg, wu, wr, other, chunk, kept, parts=2):
    n = slope.shape[0] // 2
    d, f = wg.shape
    ways = len(blocks)
    tile = pl.BlockSpec((n, FT), lambda i: (chunk, i))
    weight = pl.BlockSpec((d, FT), lambda i: (0, i))
    fixed = lambda shape: pl.BlockSpec(shape, lambda i: (0, 0))
    hidden, gate, up, share, router, *pairs = pl.pallas_call(
        lambda *refs: expert_kernel(*refs, ways=ways, parts=parts),
        grid=(f // FT,),
        in_specs=[
            pl.BlockSpec(memory_space=pltpu.SMEM),
            tile,
            weight,
            weight,
            once((TILE, d)),
            pl.BlockSpec((n, TILE), lambda i: (chunk, 0), pipeline_mode=pl.Buffered(1)),
        ]
        + [once(block.shape) for block in blocks]
        + [pl.BlockSpec(memory_space=pl.ANY) for _ in kept],
        out_specs=[tile, tile, tile, fixed((n, TILE)), fixed((TILE, d))] + [fixed(block.shape) for block in blocks],
        out_shape=[jax.ShapeDtypeStruct((2 * n, f), jnp.bfloat16)] * 3
        + [jax.ShapeDtypeStruct((n, TILE), jnp.float32), jax.ShapeDtypeStruct((TILE, d), jnp.float32)]
        + [jax.ShapeDtypeStruct(block.shape, jnp.bfloat16) for block in blocks],
        scratch_shapes=[
            pltpu.VMEM((n, d), jnp.bfloat16),
            pltpu.VMEM((n, d), jnp.float32),
            pltpu.VMEM((n, TILE), jnp.float32),
        ],
        input_output_aliases={6 + ways + k: k for k in range(len(kept))},
        cost_estimate=SHORT if chunk else SMALL,
        name="expert_rows",
    )(own, slope, wg, wu, wr, other, *blocks, *kept)
    return (hidden, gate, up), share, router, pairs


def slope_kernel(wd_ref, *refs, capacity):
    blocks, (out_ref, other_ref, u_ref) = refs[:-3], refs[-3:]

    @pl.when(pl.program_id(0) == 0)
    def _():
        reach = -(-capacity // TILE) * TILE
        for block, at, base in spans(blocks, capacity, EXTRA):
            u_ref[base : base + capacity, :] = block[at : at + capacity, :]
            named = block[at + capacity : at + capacity + EXTRA, 0:reach].astype(jnp.float32).T
            other_ref[base : base + capacity, :] = jnp.broadcast_to(named[0:capacity, 0:1], (capacity, TILE))

    out_ref[...] = dot(u_ref[...], wd_ref[...], NT).astype(jnp.bfloat16)


def slope_rows(blocks, wd, experts, capacity):
    f, d = wd.shape
    n = experts * capacity
    return pl.pallas_call(
        lambda *refs: slope_kernel(*refs, capacity=capacity),
        grid=(f // FT,),
        in_specs=[pl.BlockSpec((FT, d), lambda i: (i, 0))] + [once(block.shape) for block in blocks],
        out_specs=[pl.BlockSpec((n, FT), lambda i: (0, i)), pl.BlockSpec((n, TILE), lambda i: (0, 0))],
        out_shape=[jax.ShapeDtypeStruct((n, f), jnp.bfloat16), jax.ShapeDtypeStruct((n, TILE), jnp.float32)],
        scratch_shapes=[pltpu.VMEM((n, d), jnp.bfloat16)],
        cost_estimate=LARGE,
        name="slope_rows",
    )(wd, *blocks)


def gate_slots(target_ref, blocks, near_ref, far_ref, capacity, extra):
    for block, at, base in spans(blocks, capacity, extra):
        share_ref, start = (near_ref, base) if base < near_ref.shape[0] else (far_ref, base - near_ref.shape[0])
        value = block[at : at + capacity, :].astype(jnp.float32) * share_ref[start : start + capacity, 0:1]
        target_ref[base : base + capacity, :] = value.astype(jnp.bfloat16)


def weight_kernel(hidden, gate, up, near_ref, far_ref, *refs, ways, copies, capacity):
    rows, raw, refs = refs[:ways], refs[ways : 2 * ways], refs[2 * ways :]
    out_ref, rows_ref, raw_ref, stage_ref, down_ref, done_ref, sent_ref = refs
    step = pl.program_id(0)
    steps = pl.num_programs(0)
    d = stage_ref.shape[2] // 2
    piece = d // copies
    part_of = out_ref.shape[0] // copies

    def whole(at):
        return pltpu.make_async_copy(
            stage_ref.at[at % 2], out_ref.at[pl.ds(pl.multiple_of(at * FT, FT), FT), 0 : 2 * d], done_ref.at[at % 2]
        )

    def small(at, part, copy):
        row = at * FT + part * 64
        column = pl.multiple_of(2 * d + row // part_of * piece, piece)
        return pltpu.make_async_copy(
            down_ref.at[at % 2, part * 64 : (part + 1) * 64, copy * piece : (copy + 1) * piece],
            out_ref.at[pl.ds(pl.multiple_of(copy * part_of + row % part_of, 64), 64), pl.ds(column, piece)],
            sent_ref.at[at % 2, part, copy],
        )

    def finish(at):
        whole(at).wait()
        for part in range(FT // 64):
            for copy in range(copies):
                small(at, part, copy).wait()

    @pl.when(step == 0)
    def _():
        gate_slots(rows_ref, rows, near_ref, far_ref, capacity, 0)
        gate_slots(raw_ref, raw, near_ref, far_ref, capacity, EXTRA)

    @pl.when(step >= 2)
    def _():
        finish(step - 2)

    slot = step % 2
    stage_ref[slot, :, 0:d] = dot(gate[...], rows_ref[...], TN).astype(jnp.bfloat16)
    stage_ref[slot, :, d : 2 * d] = dot(up[...], rows_ref[...], TN).astype(jnp.bfloat16)
    down_ref[slot] = dot(hidden[...], raw_ref[...], TN).astype(jnp.bfloat16)
    whole(step).start()
    for part in range(FT // 64):
        for copy in range(copies):
            small(step, part, copy).start()

    @pl.when(step == steps - 1)
    def _():
        finish(step - 1)
        finish(step)


def weight_grads(hidden, gate, up, shares, rows, raw, copies, capacity):
    n, f = hidden.shape
    d = rows[0].shape[1]
    ways = len(rows)
    narrow = pl.BlockSpec((n, FT), lambda i: (0, i))
    return pl.pallas_call(
        lambda *refs: weight_kernel(*refs, ways=ways, copies=copies, capacity=capacity),
        grid=(f // FT,),
        in_specs=[narrow] * 3 + [once(part.shape) for part in (*shares, *rows, *raw)],
        out_specs=pl.BlockSpec(memory_space=pl.ANY),
        out_shape=jax.ShapeDtypeStruct((f, 3 * d), jnp.bfloat16),
        scratch_shapes=[
            pltpu.VMEM((n, d), jnp.bfloat16),
            pltpu.VMEM((n, d), jnp.bfloat16),
            pltpu.VMEM((2, FT, 2 * d), jnp.bfloat16),
            pltpu.VMEM((2, FT, d), jnp.bfloat16),
            pltpu.SemaphoreType.DMA((2,)),
            pltpu.SemaphoreType.DMA((2, FT // 64, copies)),
        ],
        cost_estimate=SMALL,
        name="weight_grads",
    )(hidden, gate, up, *shares, *rows, *raw)


def result_kernel(hidden_ref, wd_ref, *refs):
    results, acc_ref = refs[:-1], refs[-1]
    step = pl.program_id(0)
    part = dot(hidden_ref[...], wd_ref[...])

    @pl.when(step == 0)
    def _():
        acc_ref[...] = part

    @pl.when(step > 0)
    def _():
        acc_ref[...] += part

    @pl.when(step == pl.num_programs(0) - 1)
    def _():
        base = 0
        for result in results:
            result[...] = acc_ref[base : base + result.shape[0], :].astype(jnp.bfloat16)
            base += result.shape[0]


def result_rows(hidden, wd, shapes):
    n, f = hidden.shape
    d = wd.shape[1]
    tile = FT * 2 if f % (FT * 2) == 0 else FT
    return pl.pallas_call(
        result_kernel,
        grid=(f // tile,),
        in_specs=[pl.BlockSpec((n, tile), lambda i: (0, i)), pl.BlockSpec((tile, d), lambda i: (i, 0))],
        out_specs=[pl.BlockSpec(shape, lambda i: (0, 0)) for shape in shapes],
        out_shape=[jax.ShapeDtypeStruct(shape, jnp.bfloat16) for shape in shapes],
        scratch_shapes=[pltpu.VMEM((n, d), jnp.float32)],
        cost_estimate=SMALL,
        name="result_rows",
    )(hidden, wd)


def shared_kernel(
    core_ref, first_ref, wide_ref, second_ref, narrow_ref, mine_ref, away_ref, left_ref, *, steps, unit
):
    step = pl.program_id(0)

    def store(value):
        own = core_ref[0] == 0
        for group in range(mine_ref.shape[0] // unit):
            low = value[2 * group * unit : (2 * group + 1) * unit, :]
            high = value[(2 * group + 1) * unit : (2 * group + 2) * unit, :]
            span = slice(group * unit, (group + 1) * unit)
            mine_ref[span, :] = jnp.where(own, low, high).astype(jnp.bfloat16)
            away_ref[span, :] = jnp.where(own, high, low).astype(jnp.bfloat16)

    @pl.when(step == 0)
    def _():
        left_ref[...] = first_ref[...].T

    @pl.when(step == steps)
    def _():
        left_ref[...] = second_ref[...].T

    @pl.when(step < steps)
    def _():
        store(dot(left_ref[...], wide_ref[...]))

    @pl.when(step >= steps)
    def _():
        store(dot(left_ref[...], narrow_ref[...]))


def shared_grads(core, first, wide, second, narrow, unit):
    tokens, rows = first.shape
    tile = 512
    steps, more = wide.shape[1] // tile, narrow.shape[1] // tile
    whole = once((tokens, rows))
    out = pl.BlockSpec((rows // 2, tile), lambda i: (0, i))
    shape = jax.ShapeDtypeStruct((rows // 2, wide.shape[1] + narrow.shape[1]), jnp.bfloat16)
    return pl.pallas_call(
        lambda *refs: shared_kernel(*refs, steps=steps, unit=unit),
        grid=(steps + more,),
        in_specs=[
            pl.BlockSpec(memory_space=pltpu.SMEM),
            whole,
            pl.BlockSpec((tokens, tile), lambda i: (0, jnp.minimum(i, steps - 1))),
            whole,
            pl.BlockSpec((tokens, tile), lambda i: (0, jnp.maximum(i - steps, 0))),
        ],
        out_specs=[out, out],
        out_shape=[shape, shape],
        scratch_shapes=[pltpu.VMEM((rows, tokens), jnp.bfloat16)],
        cost_estimate=SMALL,
        name="shared_grads",
    )(core, first, wide, second, narrow)


def after(value, *before):
    return lax.optimization_barrier((value,) + before)[0]


def swap(value, axis, step):
    size = lax.axis_size(axis)
    return lax.ppermute(value, axis, [(k, k ^ step) for k in range(size)])


def parted(value, bit):
    return [lax.dynamic_index_in_dim(value, place, 0, keepdims=False) for place in (bit, 1 - bit)]


def added(first, second):
    return (first.astype(jnp.float32) + second.astype(jnp.float32)).astype(jnp.bfloat16)


def dp_halves(parts, unit):
    copies, chips = lax.axis_size("dp"), lax.axis_size("expert") // 2
    parts = [part.reshape(copies // 2, 2, chips * unit, -1) for part in parts]
    place = lax.axis_index("dp")
    cut = parts[0].shape[-1] // 2
    low = [jnp.swapaxes(part[..., :cut], 0, 1) for part in parts]
    high = [part[..., cut:] for part in parts]
    halves = []
    for pair, bit in ((low, place % 2), (high, place // 2)):
        stay, leave = zip(*(parted(part, bit) for part in pair))
        halves.append((added(*stay), added(*leave)))
    return halves


def dp_sums(halves, unit, *work):
    place = lax.axis_index("dp")
    came = [swap(leave, "dp", step) for (_, leave), step in zip(halves, (1, 2))]
    *came, _ = lax.optimization_barrier((*came, work))
    total = []
    for (stay, _), other, bit, step in zip(halves, came, (place // 2, place % 2), (2, 1)):
        mine, mine_too = (parted(part, bit) for part in (stay, other))
        leave = swap(added(mine[1], mine_too[1]), "dp", step)
        total.append(mine[0].astype(jnp.float32) + mine_too[0].astype(jnp.float32) + leave.astype(jnp.float32))
    chips = lax.axis_size("expert") // 2
    total = jnp.concatenate(total, axis=1).astype(jnp.bfloat16).reshape(chips, unit, -1)
    place = lax.axis_index("expert") // 2
    return [lax.dynamic_index_in_dim(total, place ^ step, 0, keepdims=False) for step in range(chips)]


def total_of(parts):
    return sum(part.astype(jnp.float32) for part in parts)


def chip_parts(parts, unit):
    copies, chips = lax.axis_size("dp"), lax.axis_size("expert") // 2
    place = lax.axis_index("expert") // 2
    parts = [part.reshape(copies, chips, unit, -1) for part in parts]
    return [
        added(*(lax.dynamic_index_in_dim(part, place ^ step, 1, keepdims=False) for part in parts))
        for step in range(chips)
    ]


def sent(parts, axis, stride):
    return [swap(part, axis, stride * step) if step else part for step, part in enumerate(parts)]


def on_device(
    block_input,
    routes,
    item_lengths,
    w_qkv,
    w_attn_out,
    rel_table,
    gain_attn,
    gain_moe,
    w_router,
    w_gate,
    w_up,
    w_down,
    cotangent,
):
    tokens, width = block_input.shape
    experts = w_router.shape[1]
    capacity = TOK_DEV * TOP * 5 // (4 * experts)
    slots = experts * capacity
    buckets = rel_table.shape[0]
    copies, ways = lax.axis_size("dp"), lax.axis_size("expert")
    place = lax.axis_index("expert").astype(jnp.int32)
    own = place.reshape(1)
    labels = jnp.arange(experts, dtype=jnp.int32)
    picks = [routes[:, rank : rank + 1] == labels[None, :] for rank in range(TOP)]
    places = jnp.arange(slots, dtype=jnp.int32)

    half = ways // 2
    groups = [list(range(k * half, (k + 1) * half)) for k in range(2)]

    def near(block):
        parts = block.reshape(half, -1, block.shape[1])
        parts = lax.all_to_all(parts, "expert", split_axis=0, concat_axis=0, axis_index_groups=groups, tiled=True)
        return parts.reshape(block.shape)

    def exchange(blocks, *before):
        far = [swap(block, "expert", half + step) for step, block in enumerate(blocks[1:])]
        return [near(after(blocks[0], *before))] + far

    packed, target_rows = pack_first(own, routes.T, cotangent, experts, capacity)
    target = target_rows.T
    block_input = after(block_input, *packed)
    inputs = block_input.astype(jnp.float32)
    normed, unit_one, scale_one = normalize_forward(inputs, gain_attn)
    raw = exchange(packed, scale_one)
    attn_in = normed.astype(jnp.bfloat16)
    bias = bias_rows(rel_table)
    proj = dot(attn_in, w_qkv).astype(jnp.bfloat16)
    mixed, stat = attention_forward(item_lengths, bias, proj)
    attn = dot(mixed, w_attn_out)
    resid = inputs + attn
    second, unit_two, scale_two = normalize_forward(resid, gain_moe)
    moe_in = second.astype(jnp.bfloat16)
    *packed, _ = lax.optimization_barrier((*pack(target_rows, moe_in, experts, capacity), raw))
    logits = dot(moe_in, w_router)
    chosen = jnp.stack([jnp.sum(jnp.where(pick, logits, 0.0), axis=1) for pick in picks], axis=1)
    highest = jnp.max(chosen, axis=1, keepdims=True)
    exps = jnp.exp(chosen - highest)
    gates = exps / jnp.sum(exps, axis=1, keepdims=True)
    rows = exchange(packed, gates)
    gate_weight, up_weight, down_weight = w_gate[0], w_up[0], w_down[0]
    router_rows = jnp.pad(w_router.T, ((0, TILE - experts), (0, 0)))
    slope, other = slope_rows(raw, down_weight, experts, capacity)
    weights = (gate_weight, up_weight, router_rows, other)
    kept, near_share, near_router, near_pairs = expert_rows(own, rows[:1], slope, *weights, 0, ())
    back = [near(near_pairs[0])]
    rows[1:] = [after(block, near_pairs[0]) for block in rows[1:]]
    kept, far_share, far_router, far_pairs = expert_rows(own, rows[1:], slope, *weights, 1, kept)
    back += [swap(block, "expert", half + step) for step, block in enumerate(far_pairs)]
    hidden, gate_pre_grad, up_pre_grad = kept
    shares = (near_share, far_share)
    hidden = after(hidden, back[0])
    weight_grad = weight_grads(hidden, gate_pre_grad, up_pre_grad, shares, rows, raw, copies, capacity)
    weight_sum = lax.psum_scatter(weight_grad, "dp", scatter_dimension=0, tiled=True)
    result = result_rows(after(hidden, weight_grad), down_weight, [block.shape for block in rows])
    *back, held = lax.optimization_barrier((*back, result[0]))
    result = [after(block, *back) for block in (held, *result[1:])]
    returned = exchange(result)
    resid_grad, attn_grad, gain_moe_grad = combine(
        target, gates, resid, scale_two, gain_moe.reshape(1, width), cotangent, back
    )
    mixed_grad = dot(attn_grad, w_attn_out, NT).astype(jnp.bfloat16)
    proj_grad, tiles = attention_backward(item_lengths, bias, stat, proj, mixed, mixed_grad)
    unit = width // (copies * ways)
    mine, away = shared_grads(own % 2, attn_in, proj_grad, mixed, attn_grad, unit)
    both = (mine, swap(after(away, *returned), "expert", 1))
    cut = mine.shape[1] // 2
    dp_parts = dp_halves([part[:, :cut] for part in both], unit)
    z_parts = chip_parts([part[:, cut:] for part in both], unit)
    proj_grad, _ = lax.optimization_barrier((proj_grad, (dp_parts, z_parts)))
    table_grad = table_sums(tiles, buckets)
    router_grad = (near_router + far_router)[:experts].T
    attn_in_grad = dot(proj_grad, w_qkv, NT)
    input_norm_grad, gain_attn_grad = normalize_backward(attn_in_grad, unit_one, scale_one, gain_attn)
    input_grad = resid_grad + input_norm_grad
    output = combine_output(target, gates, after(resid, dp_parts[0][1]), returned)
    small = (table_grad.reshape(-1), gain_attn_grad, gain_moe_grad, router_grad)
    sizes = [part.size // (copies * ways) for part in small]
    together = jnp.concatenate([part.reshape(copies * ways, -1) for part in small], axis=1)
    halves = dp_sums(dp_parts, unit, input_grad, output, together)
    *z_came, _ = lax.optimization_barrier((*sent(z_parts, "expert", 2), halves))
    z_sum = total_of(z_came).astype(jnp.bfloat16)
    dp_place = lax.axis_index("dp")
    z_sum = [lax.dynamic_index_in_dim(z_sum, dp_place ^ step, 0, keepdims=False) for step in range(copies)]
    together = lax.all_to_all(together, ("dp", "expert"), split_axis=0, concat_axis=0, tiled=True)
    together = jnp.sum(together, axis=0)
    at = [sum(sizes[:k]) for k in range(5)]
    table_sum, attn_sum, moe_sum, router_sum = [together[at[k] : at[k + 1]] for k in range(4)]
    piece = width // copies
    down_sum = jnp.concatenate(
        [weight_sum[:, 2 * width + k * piece : 2 * width + (k + 1) * piece] for k in range(copies)], axis=0
    )
    experts_out = (
        weight_sum[:, :width].astype(jnp.float32).T[None],
        weight_sum[:, width : 2 * width].astype(jnp.float32).T[None],
        down_sum.astype(jnp.float32)[None],
    )
    low, high = sent(halves, "expert", 2), sent(z_sum, "dp", 1)
    (low, high), _ = lax.optimization_barrier(((low, high), experts_out))
    sums = jnp.concatenate([total_of(low), total_of(high)], axis=1)
    return (
        output,
        input_grad,
        sums[:, : 3 * width],
        sums[:, 3 * width :],
        table_sum,
        attn_sum,
        moe_sum,
        router_sum.reshape(-1, experts),
        *experts_out,
    )


def solution(mesh):
    return jax.shard_map(
        on_device,
        mesh=mesh,
        in_specs=(
            P(("dp", "expert"), None),
            P(("dp", "expert"), None),
            P(("dp", "expert"), None),
            P(),
            P(),
            P(),
            P(),
            P(),
            P(),
            P("expert", None, None),
            P("expert", None, None),
            P("expert", None, None),
            P(("dp", "expert"), None),
        ),
        out_specs=(
            P(("dp", "expert"), None),
            P(("dp", "expert"), None),
            P(("dp", "expert"), None),
            P(("dp", "expert"), None),
            P(("dp", "expert")),
            P(("dp", "expert")),
            P(("dp", "expert")),
            P(("dp", "expert"), None),
            P("expert", None, "dp"),
            P("expert", None, "dp"),
            P("expert", None, "dp"),
        ),
        check_vma=False,
    )
```

```python
import jax
import jax.numpy as jnp
from jax import lax
from jax.experimental import pallas as pl
from jax.experimental.pallas import tpu as pltpu
from jax.sharding import PartitionSpec as P

TOP = 2
LONG_LEN = 512
SHORT_LEN = 128
TOK_DEV = 640
BOUNDS = (12, 16, 23, 32, 46, 64, 91)
EPSILON = 1e-06
HIGHEST = lax.Precision.HIGHEST
TILE = 128
FT = 256
NEG = -1e30
NN = (((1,), (0,)), ((), ()))
NT = (((1,), (1,)), ((), ()))
TN = (((0,), (0,)), ((), ()))
CURVE = 0.7978845608028654
CUBE = 0.044715
EXTRA = 8
SHORT = pl.CostEstimate(flops=23_000_000_000, bytes_accessed=1 << 16, transcendentals=0)
SMALL = pl.CostEstimate(flops=1 << 20, bytes_accessed=1 << 16, transcendentals=0)
MEDIUM = pl.CostEstimate(flops=235_750_000_000, bytes_accessed=1 << 16, transcendentals=0)
LARGE = pl.CostEstimate(flops=1 << 38, bytes_accessed=1 << 28, transcendentals=0)


def dot(a, b, dims=NN):
    return lax.dot_general(a, b, dims, preferred_element_type=jnp.float32)


def normalize_forward(value, gain):
    scale = lax.rsqrt(jnp.mean(value * value, axis=-1, keepdims=True) + EPSILON)
    unit = value * scale
    return (unit * gain, unit, scale)


def normalize_backward(grad, unit, scale, gain):
    gain_grad = jnp.sum(grad * unit, axis=0)
    along = grad * gain
    inner = jnp.mean(along * unit, axis=-1, keepdims=True)
    return (scale * (along - unit * inner), gain_grad)


def bias_strip(bias_row):
    wide = jnp.broadcast_to(bias_row, (TILE, bias_row.shape[1]))
    return pltpu.roll(wide, 0, 1, stride=1, stride_axis=0)


def bias_tile(strip, bias_row, step):
    if abs(step) <= 1:
        start = 2 * TILE - step * TILE
        return strip[:, start : start + TILE]
    last = bias_row.shape[1] - 1
    return bias_row[:, 0:1] if step > 0 else bias_row[:, last : last + 1]


def items_of(tokens, lengths_ref):
    return ((0, LONG_LEN, lengths_ref[0, 0], LONG_LEN // 2), (LONG_LEN, tokens, lengths_ref[0, 1], SHORT_LEN // 2))


def attention_forward_kernel(lengths_ref, bias_ref, q_ref, k_ref, v_ref, mixed_ref, stat_ref, score_ref, exp_ref):
    tokens, lanes = q_ref.shape
    size = lanes // 2
    lane = lax.broadcasted_iota(jnp.int32, (1, lanes), 1)
    values_t = v_ref[...].T
    for start, stop, visible, sure in items_of(tokens, lengths_ref):
        length = stop - start
        count = length // TILE
        outs = []
        for head in range(2):
            bias_row = bias_ref[0, head : head + 1, :]
            strip = bias_strip(bias_row)
            own = (lane >= head * size) & (lane < (head + 1) * size)
            query = jnp.where(own, q_ref[start:stop, :] * 0.125, 0.0).astype(jnp.bfloat16)
            score_ref[0:length, 0:length] = dot(k_ref[start:stop, :], query, NT)
            totals = []
            for col in range(count):
                cols = slice(col * TILE, (col + 1) * TILE)
                top = None
                for row in range(count):
                    rows = slice(row * TILE, (row + 1) * TILE)
                    tile = score_ref[rows, cols] + bias_tile(strip, bias_row, row - col)
                    if (row + 1) * TILE > sure:
                        place = lax.broadcasted_iota(jnp.int32, (TILE, 1), 0) + row * TILE
                        tile = jnp.where(place < visible, tile, NEG)
                    score_ref[rows, cols] = tile
                    peak = jnp.max(tile, axis=0, keepdims=True)
                    top = peak if top is None else jnp.maximum(top, peak)
                total = jnp.zeros((1, TILE), jnp.float32)
                for row in range(count):
                    rows = slice(row * TILE, (row + 1) * TILE)
                    tile = jnp.exp(score_ref[rows, cols] - top)
                    total = total + jnp.sum(tile, axis=0, keepdims=True)
                    exp_ref[rows, cols] = tile.astype(jnp.bfloat16)
                totals.append(total)
                stat_ref[0, head : head + 1, start + col * TILE : start + (col + 1) * TILE] = top + jnp.log(total)
            total = jnp.concatenate(totals, axis=1)
            out = dot(values_t[head * size : (head + 1) * size, start:stop], exp_ref[0:length, 0:length])
            outs.append(out / total)
        mixed_ref[start:stop, :] = jnp.concatenate(outs, axis=0).T.astype(jnp.bfloat16)


def attention_forward(lengths, bias, proj):
    tokens, width = proj.shape[0], proj.shape[1] // 3
    lanes = TILE
    pairs = width // lanes
    return pl.pallas_call(
        attention_forward_kernel,
        grid=(pairs,),
        in_specs=[
            pl.BlockSpec(memory_space=pltpu.SMEM),
            pl.BlockSpec((1, 2, bias.shape[2]), lambda p: (p, 0, 0)),
            pl.BlockSpec((tokens, lanes), lambda p: (0, p)),
            pl.BlockSpec((tokens, lanes), lambda p: (0, pairs + p)),
            pl.BlockSpec((tokens, lanes), lambda p: (0, 2 * pairs + p)),
        ],
        out_specs=[
            pl.BlockSpec((tokens, lanes), lambda p: (0, p)),
            pl.BlockSpec((1, 2, tokens), lambda p: (p, 0, 0)),
        ],
        out_shape=[
            jax.ShapeDtypeStruct((tokens, width), jnp.bfloat16),
            jax.ShapeDtypeStruct((pairs, 2, tokens), jnp.float32),
        ],
        scratch_shapes=[pltpu.VMEM((LONG_LEN, LONG_LEN), jnp.float32), pltpu.VMEM((LONG_LEN, LONG_LEN), jnp.bfloat16)],
        cost_estimate=SMALL,
        name="attention_forward",
    )(lengths, bias, proj, proj, proj)


def attention_backward_kernel(
    lengths_ref, bias_ref, stat_ref, q_ref, k_ref, v_ref, mixed_ref, grad_ref, proj_ref, table_ref,
    score_ref, slope_ref, weight_ref, change_ref, stage_ref, done_ref,
):
    pair = pl.program_id(0)
    pairs = pl.num_programs(0)
    slot = pair % 2

    def copy(part, step):
        at = pl.multiple_of((part * pairs + step) * TILE, TILE)
        return pltpu.make_async_copy(
            stage_ref.at[step % 2, part], proj_ref.at[:, pl.ds(at, TILE)], done_ref.at[step % 2, part]
        )

    @pl.when(pair >= 2)
    def _():
        for part in range(3):
            copy(part, pair - 2).wait()

    tokens, lanes = q_ref.shape
    size = lanes // 2
    lane = lax.broadcasted_iota(jnp.int32, (1, lanes), 1)
    keys_t = k_ref[...].T
    product = (grad_ref[...].astype(jnp.float32) * mixed_ref[...].astype(jnp.float32)).T
    table_ref[...] = jnp.zeros_like(table_ref)
    for start, stop, visible, sure in items_of(tokens, lengths_ref):
        length = stop - start
        count = length // TILE
        query_grads, key_grads, value_grads = [], [], []
        for head in range(2):
            bias_row = bias_ref[0, head : head + 1, :]
            strip = bias_strip(bias_row)
            own = (lane >= head * size) & (lane < (head + 1) * size)
            query = jnp.where(own, q_ref[start:stop, :] * 0.125, 0.0).astype(jnp.bfloat16)
            grad = jnp.where(own, grad_ref[start:stop, :], 0.0).astype(jnp.bfloat16)
            score_ref[0:length, 0:length] = dot(k_ref[start:stop, :], query, NT)
            slope_ref[0:length, 0:length] = dot(v_ref[start:stop, :], grad, NT)
            inner = jnp.sum(product[head * size : (head + 1) * size, start:stop], axis=0, keepdims=True)
            sums = {-1: None, 0: None, 1: None}
            far = {-1: None, 1: None}
            for col in range(count):
                cols = slice(col * TILE, (col + 1) * TILE)
                base = stat_ref[0, head : head + 1, start + col * TILE : start + (col + 1) * TILE]
                middle = inner[:, cols]
                for row in range(count):
                    rows = slice(row * TILE, (row + 1) * TILE)
                    step = row - col
                    tile = score_ref[rows, cols] + (bias_tile(strip, bias_row, step) - base)
                    if (row + 1) * TILE > sure:
                        place = lax.broadcasted_iota(jnp.int32, (TILE, 1), 0) + row * TILE
                        tile = jnp.where(place < visible, tile, NEG)
                    tile = jnp.exp(tile)
                    weight_ref[rows, cols] = tile.astype(jnp.bfloat16)
                    tile = tile * (slope_ref[rows, cols] - middle)
                    change_ref[rows, cols] = tile.astype(jnp.bfloat16)
                    if abs(step) <= 1:
                        sums[step] = tile if sums[step] is None else sums[step] + tile
                    else:
                        side = 1 if step > 0 else -1
                        part = jnp.sum(tile, axis=0, keepdims=True)
                        far[side] = part if far[side] is None else far[side] + part
            for step, value in sums.items():
                if value is not None:
                    at = TILE - step * TILE
                    table_ref[0, head, 0:TILE, at : at + TILE] += value
            for side, value in far.items():
                if value is not None:
                    at = TILE - side * TILE
                    table_ref[0, head, TILE : TILE + 1, at : at + TILE] = value
            value_grads.append(dot(weight_ref[0:length, 0:length], grad))
            key_grads.append(dot(change_ref[0:length, 0:length], query))
            query_grads.append(dot(keys_t[head * size : (head + 1) * size, start:stop], change_ref[0:length, 0:length]))
        stage_ref[slot, 0, start:stop, :] = (jnp.concatenate(query_grads, axis=0).T * 0.125).astype(jnp.bfloat16)
        stage_ref[slot, 1, start:stop, :] = (key_grads[0] + key_grads[1]).astype(jnp.bfloat16)
        stage_ref[slot, 2, start:stop, :] = (value_grads[0] + value_grads[1]).astype(jnp.bfloat16)
    for part in range(3):
        copy(part, pair).start()

    @pl.when(pair == pairs - 1)
    def _():
        for part in range(3):
            copy(part, pair - 1).wait()
            copy(part, pair).wait()


def attention_backward(lengths, bias, stat, proj, mixed, grad):
    tokens, width = mixed.shape
    lanes = TILE
    pairs = width // lanes
    return pl.pallas_call(
        attention_backward_kernel,
        grid=(pairs,),
        in_specs=[
            pl.BlockSpec(memory_space=pltpu.SMEM),
            pl.BlockSpec((1, 2, bias.shape[2]), lambda p: (p, 0, 0)),
            pl.BlockSpec((1, 2, tokens), lambda p: (p, 0, 0)),
            pl.BlockSpec((tokens, lanes), lambda p: (0, p)),
            pl.BlockSpec((tokens, lanes), lambda p: (0, pairs + p)),
            pl.BlockSpec((tokens, lanes), lambda p: (0, 2 * pairs + p)),
            pl.BlockSpec((tokens, lanes), lambda p: (0, p)),
            pl.BlockSpec((tokens, lanes), lambda p: (0, p)),
        ],
        out_specs=[
            pl.BlockSpec(memory_space=pl.ANY),
            pl.BlockSpec((1, 2, TILE + 8, 3 * TILE), lambda p: (p, 0, 0, 0)),
        ],
        out_shape=[
            jax.ShapeDtypeStruct((tokens, 3 * width), jnp.bfloat16),
            jax.ShapeDtypeStruct((pairs, 2, TILE + 8, 3 * TILE), jnp.float32),
        ],
        scratch_shapes=[
            pltpu.VMEM((LONG_LEN, LONG_LEN), jnp.float32),
            pltpu.VMEM((LONG_LEN, LONG_LEN), jnp.float32),
            pltpu.VMEM((LONG_LEN, LONG_LEN), jnp.bfloat16),
            pltpu.VMEM((LONG_LEN, LONG_LEN), jnp.bfloat16),
            pltpu.VMEM((2, 3, tokens, lanes), jnp.bfloat16),
            pltpu.SemaphoreType.DMA((2, 3)),
        ],
        cost_estimate=SMALL,
        name="attention_backward",
    )(lengths, bias, stat, proj, proj, proj, mixed, grad)


def bucket_of(offset):
    distance = jnp.abs(offset)
    far = 8 + sum(((distance >= bound).astype(jnp.int32) for bound in BOUNDS))
    return jnp.where(distance < 8, distance, far) + 16 * (offset > 0).astype(jnp.int32)


def bias_rows(rel_table):
    bucket = bucket_of(2 * TILE - jnp.arange(4 * TILE, dtype=jnp.int32))
    onehot = (bucket[:, None] == jnp.arange(rel_table.shape[0], dtype=jnp.int32)[None, :]).astype(jnp.float32)
    return jnp.einsum("xb,bh->hx", onehot, rel_table, precision=HIGHEST).reshape(-1, 2, 4 * TILE)


def table_sums(tiles, buckets):
    row = jnp.arange(TILE + 8, dtype=jnp.int32)[:, None]
    col = jnp.arange(3 * TILE, dtype=jnp.int32)[None, :]
    near = bucket_of(row - col + TILE)
    far = jnp.where(col < TILE, buckets - 1, buckets // 2 - 1)
    bucket = jnp.where(row < TILE, near, far)
    onehot = (bucket[:, :, None] == jnp.arange(buckets, dtype=jnp.int32)).astype(jnp.float32)
    return jnp.einsum("ghrc,rcb->bgh", tiles, onehot, precision=HIGHEST).reshape(buckets, -1)


def pack_first_kernel(place_ref, routes_ref, rows_ref, *out_refs, experts, capacity):
    target_ref = out_refs[-1]
    tokens = routes_ref.shape[1]
    routes = [routes_ref[rank : rank + 1, :] for rank in range(TOP)]
    label = lax.broadcasted_iota(jnp.int32, (experts, 1), 0)
    picks = [label == route for route in routes]
    named = jnp.where(picks[0] | picks[1], 1.0, 0.0).astype(jnp.bfloat16)
    later = lax.broadcasted_iota(jnp.int32, (1, tokens), 1)
    earlier = lax.broadcasted_iota(jnp.int32, (tokens, 1), 0)
    count = dot(named, jnp.where(earlier < later, 1.0, 0.0).astype(jnp.bfloat16))
    for rank in range(TOP):
        position = jnp.sum(jnp.where(picks[rank], count, 0.0), axis=0, keepdims=True).astype(jnp.int32)
        apart = routes[rank] ^ place_ref[0]
        apart = jnp.where(apart < experts // 2, routes[rank] & (experts // 2 - 1), apart)
        target_ref[rank : rank + 1, :] = apart * capacity + position
    other = jnp.concatenate([routes[1], routes[0]], axis=0).astype(jnp.float32) + 1.0
    pack_kernel(target_ref, rows_ref, *out_refs[:-1], other=other, capacity=capacity)


def pack_kernel(target_ref, rows_ref, *out_refs, other=None, capacity):
    rows = rows_ref[...]
    base = 0
    for out_ref in out_refs:
        stride = capacity + (0 if other is None else EXTRA)
        for at in range(0, out_ref.shape[0], stride):
            slot = lax.broadcasted_iota(jnp.int32, (capacity, 1), 0) + base
            hits = [slot == target_ref[rank : rank + 1, :] for rank in range(TOP)]
            hit = jnp.where(hits[0] | hits[1], 1.0, 0.0).astype(jnp.bfloat16)
            out_ref[at : at + capacity, :] = dot(hit, rows).astype(jnp.bfloat16)
            if other is not None:
                named = sum(jnp.where(hits[rank], other[rank : rank + 1, :], 0.0) for rank in range(TOP))
                ones = jnp.ones((EXTRA, named.shape[1]), jnp.bfloat16)
                out_ref[at + capacity : at + stride, :] = jnp.zeros((EXTRA, out_ref.shape[1]), jnp.bfloat16)
                out_ref[at + capacity : at + stride, 0:capacity] = dot(ones, named.astype(jnp.bfloat16), NT).astype(jnp.bfloat16)
            base += capacity


def block_shapes(experts, rows, width):
    half = experts // 2
    return [jax.ShapeDtypeStruct((n * rows, width), jnp.bfloat16) for n in [half] + [1] * half]


def pack_first(place, routes, rows, experts, capacity):
    blocks = block_shapes(experts, capacity + EXTRA, rows.shape[1])
    *blocks, target = pl.pallas_call(
        lambda *refs: pack_first_kernel(*refs, experts=experts, capacity=capacity),
        in_specs=[pl.BlockSpec(memory_space=pltpu.SMEM), pl.BlockSpec(), pl.BlockSpec()],
        out_shape=blocks + [jax.ShapeDtypeStruct(routes.shape, jnp.int32)],
        cost_estimate=SMALL,
        name="pack_first",
    )(place, routes, rows)
    return blocks, target


def pack(target, rows, experts, capacity):
    return pl.pallas_call(
        lambda *refs: pack_kernel(*refs, capacity=capacity),
        out_shape=block_shapes(experts, capacity, rows.shape[1]),
        cost_estimate=SMALL,
        name="pack_rows",
    )(target, rows)


def gather_rows(target_ref, gates_ref, blocks):
    total = None
    base = 0
    for block in blocks:
        slot = lax.broadcasted_iota(jnp.int32, (1, block.shape[0]), 1) + base
        share = sum(
            jnp.where(target_ref[:, rank : rank + 1] == slot, gates_ref[:, rank : rank + 1], 0.0) for rank in range(TOP)
        )
        part = dot(share.astype(jnp.bfloat16), block[...])
        total = part if total is None else total + part
        base += block.shape[0]
    return total


def output_kernel(target_ref, gates_ref, resid_ref, *refs):
    refs[-1][...] = (resid_ref[...] + gather_rows(target_ref, gates_ref, refs[:-1])).astype(jnp.bfloat16)


def combine_output(target, gates, resid, blocks):
    return pl.pallas_call(
        output_kernel,
        out_shape=jax.ShapeDtypeStruct(resid.shape, jnp.bfloat16),
        cost_estimate=MEDIUM,
        name="combine_output",
    )(target, gates, resid, *blocks)


def combine_kernel(target_ref, gates_ref, resid_ref, scale_ref, gain_ref, upstream_ref, *refs):
    blocks, (grad_ref, low_ref, gain_grad_ref) = refs[:-3], refs[-3:]
    total = gather_rows(target_ref, gates_ref, blocks)
    scale = scale_ref[...]
    unit = resid_ref[...] * scale
    gain_grad_ref[...] = jnp.sum(total * unit, axis=0, keepdims=True)
    along = total * gain_ref[...]
    inner = jnp.mean(along * unit, axis=1, keepdims=True)
    grad = upstream_ref[...].astype(jnp.float32) + scale * (along - unit * inner)
    grad_ref[...] = grad
    low_ref[...] = grad.astype(jnp.bfloat16)


def combine(target, gates, resid, scale, gain, upstream, blocks):
    tokens, width = resid.shape
    return pl.pallas_call(
        combine_kernel,
        out_shape=[
            jax.ShapeDtypeStruct((tokens, width), jnp.float32),
            jax.ShapeDtypeStruct((tokens, width), jnp.bfloat16),
            jax.ShapeDtypeStruct((1, width), jnp.float32),
        ],
        cost_estimate=SMALL,
        name="combine_back",
    )(target, gates, resid, scale, gain, upstream, *blocks)


def spans(blocks, capacity, extra=0):
    base = 0
    for block in blocks:
        for at in range(0, block.shape[0], capacity + extra):
            yield block, at, base
            base += capacity


def expert_kernel(own_ref, slope_ref, wg_ref, wu_ref, wr_ref, other_ref, *refs, ways, parts):
    blocks, refs = refs[:ways], refs[-(8 + ways) :]
    hidden_ref, gate_ref, up_ref, share_ref, router_ref = refs[:5]
    pairs, (x_ref, acc_ref, dots_ref) = refs[5 : 5 + ways], refs[5 + ways :]
    step = pl.program_id(0)
    rows = x_ref.shape[0] // parts

    @pl.when(step == 0)
    def _():
        acc_ref[...] = jnp.zeros_like(acc_ref)
        dots_ref[...] = jnp.zeros_like(dots_ref)
        base = 0
        for block in blocks:
            x_ref[base : base + block.shape[0], :] = block[...]
            base += block.shape[0]

    for part in range(parts):
        span = slice(part * rows, (part + 1) * rows)
        x = x_ref[span, :]
        gate = dot(x, wg_ref[...])
        up = dot(x, wu_ref[...])
        slope = slope_ref[span, :].astype(jnp.float32)
        square = gate * gate
        rise = 0.5 + 0.5 * jnp.tanh(gate * (CURVE + (CURVE * CUBE) * square))
        unit = gate * rise
        bend = rise + (unit - unit * rise) * (2 * CURVE + (6 * CURVE * CUBE) * square)
        hidden = (unit * up).astype(jnp.bfloat16)
        hidden_ref[span, :] = hidden
        both = hidden.astype(jnp.float32) * slope
        dots_ref[span, :] += both[:, 0:TILE] + both[:, TILE : 2 * TILE]
        gate_grad = (slope * up * bend).astype(jnp.bfloat16)
        up_grad = (slope * unit).astype(jnp.bfloat16)
        gate_ref[span, :] = gate_grad
        up_ref[span, :] = up_grad
        acc_ref[span, :] += dot(gate_grad, wg_ref[...], NT) + dot(up_grad, wu_ref[...], NT)

    @pl.when(step == pl.num_programs(0) - 1)
    def _():
        logits = dot(x_ref[...], wr_ref[...], NT)
        label = lax.broadcasted_iota(jnp.int32, (1, TILE), 1)
        mine = label == own_ref[0]
        theirs = label == other_ref[:, 0:1].astype(jnp.int32) - 1
        first = jnp.sum(jnp.where(mine, logits, 0.0), axis=1, keepdims=True)
        second = jnp.sum(jnp.where(theirs, logits, 0.0), axis=1, keepdims=True)
        top = jnp.maximum(first, second)
        first = jnp.exp(first - top)
        second = jnp.exp(second - top)
        total = first + second
        first = first / total
        second = second / total
        inner = jnp.sum(dots_ref[...], axis=1, keepdims=True)
        coef = inner * second * (jnp.where(mine, 1.0, 0.0) - jnp.where(theirs, 1.0, 0.0))
        share_ref[...] = jnp.broadcast_to(first, share_ref.shape)
        router_ref[...] = dot((first * coef).astype(jnp.bfloat16), x_ref[...], TN)
        acc_ref[...] += dot(coef.astype(jnp.bfloat16), wr_ref[...])
        base = 0
        for pair in pairs:
            pair[...] = acc_ref[base : base + pair.shape[0], :].astype(jnp.bfloat16)
            base += pair.shape[0]


def once(shape):
    return pl.BlockSpec(shape, lambda i: (0, 0), pipeline_mode=pl.Buffered(1))


def expert_rows(own, blocks, slope, wg, wu, wr, other, chunk, kept, parts=2):
    n = slope.shape[0] // 2
    d, f = wg.shape
    ways = len(blocks)
    tile = pl.BlockSpec((n, FT), lambda i: (chunk, i))
    weight = pl.BlockSpec((d, FT), lambda i: (0, i))
    fixed = lambda shape: pl.BlockSpec(shape, lambda i: (0, 0))
    hidden, gate, up, share, router, *pairs = pl.pallas_call(
        lambda *refs: expert_kernel(*refs, ways=ways, parts=parts),
        grid=(f // FT,),
        in_specs=[
            pl.BlockSpec(memory_space=pltpu.SMEM),
            tile,
            weight,
            weight,
            once((TILE, d)),
            pl.BlockSpec((n, TILE), lambda i: (chunk, 0), pipeline_mode=pl.Buffered(1)),
        ]
        + [once(block.shape) for block in blocks]
        + [pl.BlockSpec(memory_space=pl.ANY) for _ in kept],
        out_specs=[tile, tile, tile, fixed((n, TILE)), fixed((TILE, d))] + [fixed(block.shape) for block in blocks],
        out_shape=[jax.ShapeDtypeStruct((2 * n, f), jnp.bfloat16)] * 3
        + [jax.ShapeDtypeStruct((n, TILE), jnp.float32), jax.ShapeDtypeStruct((TILE, d), jnp.float32)]
        + [jax.ShapeDtypeStruct(block.shape, jnp.bfloat16) for block in blocks],
        scratch_shapes=[
            pltpu.VMEM((n, d), jnp.bfloat16),
            pltpu.VMEM((n, d), jnp.float32),
            pltpu.VMEM((n, TILE), jnp.float32),
        ],
        input_output_aliases={6 + ways + k: k for k in range(len(kept))},
        cost_estimate=SHORT if chunk else SMALL,
        name="expert_rows",
    )(own, slope, wg, wu, wr, other, *blocks, *kept)
    return (hidden, gate, up), share, router, pairs


def slope_kernel(wd_ref, *refs, capacity):
    blocks, (out_ref, other_ref, u_ref) = refs[:-3], refs[-3:]

    @pl.when(pl.program_id(0) == 0)
    def _():
        reach = -(-capacity // TILE) * TILE
        for block, at, base in spans(blocks, capacity, EXTRA):
            u_ref[base : base + capacity, :] = block[at : at + capacity, :]
            named = block[at + capacity : at + capacity + EXTRA, 0:reach].astype(jnp.float32).T
            other_ref[base : base + capacity, :] = jnp.broadcast_to(named[0:capacity, 0:1], (capacity, TILE))

    out_ref[...] = dot(u_ref[...], wd_ref[...], NT).astype(jnp.bfloat16)


def slope_rows(blocks, wd, experts, capacity):
    f, d = wd.shape
    n = experts * capacity
    return pl.pallas_call(
        lambda *refs: slope_kernel(*refs, capacity=capacity),
        grid=(f // FT,),
        in_specs=[pl.BlockSpec((FT, d), lambda i: (i, 0))] + [once(block.shape) for block in blocks],
        out_specs=[pl.BlockSpec((n, FT), lambda i: (0, i)), pl.BlockSpec((n, TILE), lambda i: (0, 0))],
        out_shape=[jax.ShapeDtypeStruct((n, f), jnp.bfloat16), jax.ShapeDtypeStruct((n, TILE), jnp.float32)],
        scratch_shapes=[pltpu.VMEM((n, d), jnp.bfloat16)],
        cost_estimate=LARGE,
        name="slope_rows",
    )(wd, *blocks)


def gate_slots(target_ref, blocks, near_ref, far_ref, capacity, extra):
    for block, at, base in spans(blocks, capacity, extra):
        share_ref, start = (near_ref, base) if base < near_ref.shape[0] else (far_ref, base - near_ref.shape[0])
        value = block[at : at + capacity, :].astype(jnp.float32) * share_ref[start : start + capacity, 0:1]
        target_ref[base : base + capacity, :] = value.astype(jnp.bfloat16)


def weight_kernel(hidden, gate, up, near_ref, far_ref, *refs, ways, copies, capacity):
    rows, raw, refs = refs[:ways], refs[ways : 2 * ways], refs[2 * ways :]
    out_ref, rows_ref, raw_ref, stage_ref, down_ref, done_ref, sent_ref = refs
    step = pl.program_id(0)
    steps = pl.num_programs(0)
    d = stage_ref.shape[2] // 2
    piece = d // copies
    part_of = out_ref.shape[0] // copies

    def whole(at):
        return pltpu.make_async_copy(
            stage_ref.at[at % 2], out_ref.at[pl.ds(pl.multiple_of(at * FT, FT), FT), 0 : 2 * d], done_ref.at[at % 2]
        )

    def small(at, part, copy):
        row = at * FT + part * 64
        column = pl.multiple_of(2 * d + row // part_of * piece, piece)
        return pltpu.make_async_copy(
            down_ref.at[at % 2, part * 64 : (part + 1) * 64, copy * piece : (copy + 1) * piece],
            out_ref.at[pl.ds(pl.multiple_of(copy * part_of + row % part_of, 64), 64), pl.ds(column, piece)],
            sent_ref.at[at % 2, part, copy],
        )

    def finish(at):
        whole(at).wait()
        for part in range(FT // 64):
            for copy in range(copies):
                small(at, part, copy).wait()

    @pl.when(step == 0)
    def _():
        gate_slots(rows_ref, rows, near_ref, far_ref, capacity, 0)
        gate_slots(raw_ref, raw, near_ref, far_ref, capacity, EXTRA)

    @pl.when(step >= 2)
    def _():
        finish(step - 2)

    slot = step % 2
    stage_ref[slot, :, 0:d] = dot(gate[...], rows_ref[...], TN).astype(jnp.bfloat16)
    stage_ref[slot, :, d : 2 * d] = dot(up[...], rows_ref[...], TN).astype(jnp.bfloat16)
    down_ref[slot] = dot(hidden[...], raw_ref[...], TN).astype(jnp.bfloat16)
    whole(step).start()
    for part in range(FT // 64):
        for copy in range(copies):
            small(step, part, copy).start()

    @pl.when(step == steps - 1)
    def _():
        finish(step - 1)
        finish(step)


def weight_grads(hidden, gate, up, shares, rows, raw, copies, capacity):
    n, f = hidden.shape
    d = rows[0].shape[1]
    ways = len(rows)
    narrow = pl.BlockSpec((n, FT), lambda i: (0, i))
    return pl.pallas_call(
        lambda *refs: weight_kernel(*refs, ways=ways, copies=copies, capacity=capacity),
        grid=(f // FT,),
        in_specs=[narrow] * 3 + [once(part.shape) for part in (*shares, *rows, *raw)],
        out_specs=pl.BlockSpec(memory_space=pl.ANY),
        out_shape=jax.ShapeDtypeStruct((f, 3 * d), jnp.bfloat16),
        scratch_shapes=[
            pltpu.VMEM((n, d), jnp.bfloat16),
            pltpu.VMEM((n, d), jnp.bfloat16),
            pltpu.VMEM((2, FT, 2 * d), jnp.bfloat16),
            pltpu.VMEM((2, FT, d), jnp.bfloat16),
            pltpu.SemaphoreType.DMA((2,)),
            pltpu.SemaphoreType.DMA((2, FT // 64, copies)),
        ],
        cost_estimate=SMALL,
        name="weight_grads",
    )(hidden, gate, up, *shares, *rows, *raw)


def result_kernel(hidden_ref, wd_ref, *refs):
    results, acc_ref = refs[:-1], refs[-1]
    step = pl.program_id(0)
    part = dot(hidden_ref[...], wd_ref[...])

    @pl.when(step == 0)
    def _():
        acc_ref[...] = part

    @pl.when(step > 0)
    def _():
        acc_ref[...] += part

    @pl.when(step == pl.num_programs(0) - 1)
    def _():
        base = 0
        for result in results:
            result[...] = acc_ref[base : base + result.shape[0], :].astype(jnp.bfloat16)
            base += result.shape[0]


def result_rows(hidden, wd, shapes):
    n, f = hidden.shape
    d = wd.shape[1]
    tile = FT * 2 if f % (FT * 2) == 0 else FT
    return pl.pallas_call(
        result_kernel,
        grid=(f // tile,),
        in_specs=[pl.BlockSpec((n, tile), lambda i: (0, i)), pl.BlockSpec((tile, d), lambda i: (i, 0))],
        out_specs=[pl.BlockSpec(shape, lambda i: (0, 0)) for shape in shapes],
        out_shape=[jax.ShapeDtypeStruct(shape, jnp.bfloat16) for shape in shapes],
        scratch_shapes=[pltpu.VMEM((n, d), jnp.float32)],
        cost_estimate=SMALL,
        name="result_rows",
    )(hidden, wd)


def shared_kernel(
    core_ref, first_ref, wide_ref, second_ref, narrow_ref, mine_ref, away_ref, left_ref, *, steps, unit
):
    step = pl.program_id(0)

    def store(value):
        own = core_ref[0] == 0
        for group in range(mine_ref.shape[0] // unit):
            low = value[2 * group * unit : (2 * group + 1) * unit, :]
            high = value[(2 * group + 1) * unit : (2 * group + 2) * unit, :]
            span = slice(group * unit, (group + 1) * unit)
            mine_ref[span, :] = jnp.where(own, low, high).astype(jnp.bfloat16)
            away_ref[span, :] = jnp.where(own, high, low).astype(jnp.bfloat16)

    @pl.when(step == 0)
    def _():
        left_ref[...] = first_ref[...].T

    @pl.when(step == steps)
    def _():
        left_ref[...] = second_ref[...].T

    @pl.when(step < steps)
    def _():
        store(dot(left_ref[...], wide_ref[...]))

    @pl.when(step >= steps)
    def _():
        store(dot(left_ref[...], narrow_ref[...]))


def shared_grads(core, first, wide, second, narrow, unit):
    tokens, rows = first.shape
    tile = 512
    steps, more = wide.shape[1] // tile, narrow.shape[1] // tile
    whole = once((tokens, rows))
    out = pl.BlockSpec((rows // 2, tile), lambda i: (0, i))
    shape = jax.ShapeDtypeStruct((rows // 2, wide.shape[1] + narrow.shape[1]), jnp.bfloat16)
    return pl.pallas_call(
        lambda *refs: shared_kernel(*refs, steps=steps, unit=unit),
        grid=(steps + more,),
        in_specs=[
            pl.BlockSpec(memory_space=pltpu.SMEM),
            whole,
            pl.BlockSpec((tokens, tile), lambda i: (0, jnp.minimum(i, steps - 1))),
            whole,
            pl.BlockSpec((tokens, tile), lambda i: (0, jnp.maximum(i - steps, 0))),
        ],
        out_specs=[out, out],
        out_shape=[shape, shape],
        scratch_shapes=[pltpu.VMEM((rows, tokens), jnp.bfloat16)],
        cost_estimate=SMALL,
        name="shared_grads",
    )(core, first, wide, second, narrow)


def after(value, *before):
    return lax.optimization_barrier((value,) + before)[0]


def swap(value, axis, step):
    size = lax.axis_size(axis)
    return lax.ppermute(value, axis, [(k, k ^ step) for k in range(size)])


def parted(value, bit):
    return [lax.dynamic_index_in_dim(value, place, 0, keepdims=False) for place in (bit, 1 - bit)]


def added(first, second):
    return (first.astype(jnp.float32) + second.astype(jnp.float32)).astype(jnp.bfloat16)


def dp_halves(parts, unit):
    copies, chips = lax.axis_size("dp"), lax.axis_size("expert") // 2
    parts = [part.reshape(copies // 2, 2, chips * unit, -1) for part in parts]
    place = lax.axis_index("dp")
    cut = parts[0].shape[-1] // 2
    low = [jnp.swapaxes(part[..., :cut], 0, 1) for part in parts]
    high = [part[..., cut:] for part in parts]
    halves = []
    for pair, bit in ((low, place % 2), (high, place // 2)):
        stay, leave = zip(*(parted(part, bit) for part in pair))
        halves.append((added(*stay), added(*leave)))
    return halves


def dp_sums(halves, unit, *work):
    place = lax.axis_index("dp")
    came = [swap(leave, "dp", step) for (_, leave), step in zip(halves, (1, 2))]
    *came, _ = lax.optimization_barrier((*came, work))
    total = []
    for (stay, _), other, bit, step in zip(halves, came, (place // 2, place % 2), (2, 1)):
        mine, mine_too = (parted(part, bit) for part in (stay, other))
        leave = swap(added(mine[1], mine_too[1]), "dp", step)
        total.append(mine[0].astype(jnp.float32) + mine_too[0].astype(jnp.float32) + leave.astype(jnp.float32))
    chips = lax.axis_size("expert") // 2
    total = jnp.concatenate(total, axis=1).astype(jnp.bfloat16).reshape(chips, unit, -1)
    place = lax.axis_index("expert") // 2
    return [lax.dynamic_index_in_dim(total, place ^ step, 0, keepdims=False) for step in range(chips)]


def total_of(parts):
    return sum(part.astype(jnp.float32) for part in parts)


def chip_parts(parts, unit):
    copies, chips = lax.axis_size("dp"), lax.axis_size("expert") // 2
    place = lax.axis_index("expert") // 2
    parts = [part.reshape(copies, chips, unit, -1) for part in parts]
    return [
        added(*(lax.dynamic_index_in_dim(part, place ^ step, 1, keepdims=False) for part in parts))
        for step in range(chips)
    ]


def sent(parts, axis, stride):
    return [swap(part, axis, stride * step) if step else part for step, part in enumerate(parts)]


def on_device(
    block_input,
    routes,
    item_lengths,
    w_qkv,
    w_attn_out,
    rel_table,
    gain_attn,
    gain_moe,
    w_router,
    w_gate,
    w_up,
    w_down,
    cotangent,
):
    tokens, width = block_input.shape
    experts = w_router.shape[1]
    capacity = TOK_DEV * TOP * 5 // (4 * experts)
    slots = experts * capacity
    buckets = rel_table.shape[0]
    copies, ways = lax.axis_size("dp"), lax.axis_size("expert")
    place = lax.axis_index("expert").astype(jnp.int32)
    own = place.reshape(1)
    labels = jnp.arange(experts, dtype=jnp.int32)
    picks = [routes[:, rank : rank + 1] == labels[None, :] for rank in range(TOP)]
    places = jnp.arange(slots, dtype=jnp.int32)

    half = ways // 2
    groups = [list(range(k * half, (k + 1) * half)) for k in range(2)]

    def near(block):
        parts = block.reshape(half, -1, block.shape[1])
        parts = lax.all_to_all(parts, "expert", split_axis=0, concat_axis=0, axis_index_groups=groups, tiled=True)
        return parts.reshape(block.shape)

    def exchange(blocks, *before):
        far = [swap(block, "expert", half + step) for step, block in enumerate(blocks[1:])]
        return [near(after(blocks[0], *before))] + far

    packed, target_rows = pack_first(own, routes.T, cotangent, experts, capacity)
    target = target_rows.T
    block_input = after(block_input, *packed)
    inputs = block_input.astype(jnp.float32)
    normed, unit_one, scale_one = normalize_forward(inputs, gain_attn)
    raw = exchange(packed, scale_one)
    attn_in = normed.astype(jnp.bfloat16)
    bias = bias_rows(rel_table)
    proj = dot(attn_in, w_qkv).astype(jnp.bfloat16)
    mixed, stat = attention_forward(item_lengths, bias, proj)
    attn = dot(mixed, w_attn_out)
    resid = inputs + attn
    second, unit_two, scale_two = normalize_forward(resid, gain_moe)
    moe_in = second.astype(jnp.bfloat16)
    *packed, _ = lax.optimization_barrier((*pack(target_rows, moe_in, experts, capacity), raw))
    logits = dot(moe_in, w_router)
    chosen = jnp.stack([jnp.sum(jnp.where(pick, logits, 0.0), axis=1) for pick in picks], axis=1)
    highest = jnp.max(chosen, axis=1, keepdims=True)
    exps = jnp.exp(chosen - highest)
    gates = exps / jnp.sum(exps, axis=1, keepdims=True)
    rows = exchange(packed, gates)
    gate_weight, up_weight, down_weight = w_gate[0], w_up[0], w_down[0]
    router_rows = jnp.pad(w_router.T, ((0, TILE - experts), (0, 0)))
    slope, other = slope_rows(raw, down_weight, experts, capacity)
    weights = (gate_weight, up_weight, router_rows, other)
    kept, near_share, near_router, near_pairs = expert_rows(own, rows[:1], slope, *weights, 0, ())
    back = [near(near_pairs[0])]
    rows[1:] = [after(block, near_pairs[0]) for block in rows[1:]]
    kept, far_share, far_router, far_pairs = expert_rows(own, rows[1:], slope, *weights, 1, kept)
    back += [swap(block, "expert", half + step) for step, block in enumerate(far_pairs)]
    hidden, gate_pre_grad, up_pre_grad = kept
    shares = (near_share, far_share)
    hidden = after(hidden, back[0])
    weight_grad = weight_grads(hidden, gate_pre_grad, up_pre_grad, shares, rows, raw, copies, capacity)
    weight_sum = lax.psum_scatter(weight_grad, "dp", scatter_dimension=0, tiled=True)
    result = result_rows(after(hidden, weight_grad), down_weight, [block.shape for block in rows])
    *back, held = lax.optimization_barrier((*back, result[0]))
    result = [after(block, *back) for block in (held, *result[1:])]
    returned = exchange(result)
    resid_grad, attn_grad, gain_moe_grad = combine(
        target, gates, resid, scale_two, gain_moe.reshape(1, width), cotangent, back
    )
    mixed_grad = dot(attn_grad, w_attn_out, NT).astype(jnp.bfloat16)
    proj_grad, tiles = attention_backward(item_lengths, bias, stat, proj, mixed, mixed_grad)
    unit = width // (copies * ways)
    mine, away = shared_grads(own % 2, attn_in, proj_grad, mixed, attn_grad, unit)
    both = (mine, swap(after(away, *returned), "expert", 1))
    cut = mine.shape[1] // 2
    dp_parts = dp_halves([part[:, :cut] for part in both], unit)
    z_parts = chip_parts([part[:, cut:] for part in both], unit)
    proj_grad, _ = lax.optimization_barrier((proj_grad, (dp_parts, z_parts)))
    table_grad = table_sums(tiles, buckets)
    router_grad = (near_router + far_router)[:experts].T
    attn_in_grad = dot(proj_grad, w_qkv, NT)
    input_norm_grad, gain_attn_grad = normalize_backward(attn_in_grad, unit_one, scale_one, gain_attn)
    input_grad = resid_grad + input_norm_grad
    output = combine_output(target, gates, after(resid, dp_parts[0][1]), returned)
    small = (table_grad.reshape(-1), gain_attn_grad, gain_moe_grad, router_grad)
    sizes = [part.size // (copies * ways) for part in small]
    together = jnp.concatenate([part.reshape(copies * ways, -1) for part in small], axis=1)
    *z_came, _ = lax.optimization_barrier((*sent(z_parts, "expert", 2), (input_grad, output, together)))
    halves = dp_sums(dp_parts, unit, input_grad, output, together, z_came)
    z_sum = total_of(z_came).astype(jnp.bfloat16)
    dp_place = lax.axis_index("dp")
    z_sum = [lax.dynamic_index_in_dim(z_sum, dp_place ^ step, 0, keepdims=False) for step in range(copies)]
    together = lax.all_to_all(together, ("dp", "expert"), split_axis=0, concat_axis=0, tiled=True)
    piece = width // copies
    down_sum = jnp.concatenate(
        [weight_sum[:, 2 * width + k * piece : 2 * width + (k + 1) * piece] for k in range(copies)], axis=0
    )
    experts_out = (
        weight_sum[:, :width].astype(jnp.float32).T[None],
        weight_sum[:, width : 2 * width].astype(jnp.float32).T[None],
        down_sum.astype(jnp.float32)[None],
    )
    low, high = sent(halves, "expert", 2), sent(z_sum, "dp", 1)
    (low, high), together, _ = lax.optimization_barrier(((low, high), together, experts_out))
    together = jnp.sum(together, axis=0)
    at = [sum(sizes[:k]) for k in range(5)]
    table_sum, attn_sum, moe_sum, router_sum = [together[at[k] : at[k + 1]] for k in range(4)]
    sums = jnp.concatenate([total_of(low), total_of(high)], axis=1)
    return (
        output,
        input_grad,
        sums[:, : 3 * width],
        sums[:, 3 * width :],
        table_sum,
        attn_sum,
        moe_sum,
        router_sum.reshape(-1, experts),
        *experts_out,
    )


def solution(mesh):
    return jax.shard_map(
        on_device,
        mesh=mesh,
        in_specs=(
            P(("dp", "expert"), None),
            P(("dp", "expert"), None),
            P(("dp", "expert"), None),
            P(),
            P(),
            P(),
            P(),
            P(),
            P(),
            P("expert", None, None),
            P("expert", None, None),
            P("expert", None, None),
            P(("dp", "expert"), None),
        ),
        out_specs=(
            P(("dp", "expert"), None),
            P(("dp", "expert"), None),
            P(("dp", "expert"), None),
            P(("dp", "expert"), None),
            P(("dp", "expert")),
            P(("dp", "expert")),
            P(("dp", "expert")),
            P(("dp", "expert"), None),
            P("expert", None, "dp"),
            P("expert", None, "dp"),
            P("expert", None, "dp"),
        ),
        check_vma=False,
    )
```

```python
import jax
import jax.numpy as jnp
from jax import lax
from jax.experimental import pallas as pl
from jax.experimental.pallas import tpu as pltpu
from jax.sharding import PartitionSpec as P

TOP = 2
LONG_LEN = 512
SHORT_LEN = 128
TOK_DEV = 640
BOUNDS = (12, 16, 23, 32, 46, 64, 91)
EPSILON = 1e-06
HIGHEST = lax.Precision.HIGHEST
TILE = 128
FT = 256
NEG = -1e30
NN = (((1,), (0,)), ((), ()))
NT = (((1,), (1,)), ((), ()))
TN = (((0,), (0,)), ((), ()))
CURVE = 0.7978845608028654
CUBE = 0.044715
EXTRA = 8
SHORT = pl.CostEstimate(flops=23_000_000_000, bytes_accessed=1 << 16, transcendentals=0)
SMALL = pl.CostEstimate(flops=1 << 20, bytes_accessed=1 << 16, transcendentals=0)
MEDIUM = pl.CostEstimate(flops=249_550_000_000, bytes_accessed=1 << 16, transcendentals=0)
LARGE = pl.CostEstimate(flops=1 << 38, bytes_accessed=1 << 28, transcendentals=0)


def dot(a, b, dims=NN):
    return lax.dot_general(a, b, dims, preferred_element_type=jnp.float32)


def normalize_forward(value, gain):
    scale = lax.rsqrt(jnp.mean(value * value, axis=-1, keepdims=True) + EPSILON)
    unit = value * scale
    return (unit * gain, unit, scale)


def normalize_backward(grad, unit, scale, gain):
    gain_grad = jnp.sum(grad * unit, axis=0)
    along = grad * gain
    inner = jnp.mean(along * unit, axis=-1, keepdims=True)
    return (scale * (along - unit * inner), gain_grad)


def bias_strip(bias_row):
    wide = jnp.broadcast_to(bias_row, (TILE, bias_row.shape[1]))
    return pltpu.roll(wide, 0, 1, stride=1, stride_axis=0)


def bias_tile(strip, bias_row, step):
    if abs(step) <= 1:
        start = 2 * TILE - step * TILE
        return strip[:, start : start + TILE]
    last = bias_row.shape[1] - 1
    return bias_row[:, 0:1] if step > 0 else bias_row[:, last : last + 1]


def items_of(tokens, lengths_ref):
    return ((0, LONG_LEN, lengths_ref[0, 0], LONG_LEN // 2), (LONG_LEN, tokens, lengths_ref[0, 1], SHORT_LEN // 2))


def attention_forward_kernel(lengths_ref, bias_ref, q_ref, k_ref, v_ref, mixed_ref, stat_ref, score_ref, exp_ref):
    tokens, lanes = q_ref.shape
    size = lanes // 2
    lane = lax.broadcasted_iota(jnp.int32, (1, lanes), 1)
    values_t = v_ref[...].T
    for start, stop, visible, sure in items_of(tokens, lengths_ref):
        length = stop - start
        count = length // TILE
        outs = []
        for head in range(2):
            bias_row = bias_ref[0, head : head + 1, :]
            strip = bias_strip(bias_row)
            own = (lane >= head * size) & (lane < (head + 1) * size)
            query = jnp.where(own, q_ref[start:stop, :] * 0.125, 0.0).astype(jnp.bfloat16)
            score_ref[0:length, 0:length] = dot(k_ref[start:stop, :], query, NT)
            totals = []
            for col in range(count):
                cols = slice(col * TILE, (col + 1) * TILE)
                top = None
                for row in range(count):
                    rows = slice(row * TILE, (row + 1) * TILE)
                    tile = score_ref[rows, cols] + bias_tile(strip, bias_row, row - col)
                    if (row + 1) * TILE > sure:
                        place = lax.broadcasted_iota(jnp.int32, (TILE, 1), 0) + row * TILE
                        tile = jnp.where(place < visible, tile, NEG)
                    score_ref[rows, cols] = tile
                    peak = jnp.max(tile, axis=0, keepdims=True)
                    top = peak if top is None else jnp.maximum(top, peak)
                total = jnp.zeros((1, TILE), jnp.float32)
                for row in range(count):
                    rows = slice(row * TILE, (row + 1) * TILE)
                    tile = jnp.exp(score_ref[rows, cols] - top)
                    total = total + jnp.sum(tile, axis=0, keepdims=True)
                    exp_ref[rows, cols] = tile.astype(jnp.bfloat16)
                totals.append(total)
                stat_ref[0, head : head + 1, start + col * TILE : start + (col + 1) * TILE] = top + jnp.log(total)
            total = jnp.concatenate(totals, axis=1)
            out = dot(values_t[head * size : (head + 1) * size, start:stop], exp_ref[0:length, 0:length])
            outs.append(out / total)
        mixed_ref[start:stop, :] = jnp.concatenate(outs, axis=0).T.astype(jnp.bfloat16)


def attention_forward(lengths, bias, proj):
    tokens, width = proj.shape[0], proj.shape[1] // 3
    lanes = TILE
    pairs = width // lanes
    return pl.pallas_call(
        attention_forward_kernel,
        grid=(pairs,),
        in_specs=[
            pl.BlockSpec(memory_space=pltpu.SMEM),
            pl.BlockSpec((1, 2, bias.shape[2]), lambda p: (p, 0, 0)),
            pl.BlockSpec((tokens, lanes), lambda p: (0, p)),
            pl.BlockSpec((tokens, lanes), lambda p: (0, pairs + p)),
            pl.BlockSpec((tokens, lanes), lambda p: (0, 2 * pairs + p)),
        ],
        out_specs=[
            pl.BlockSpec((tokens, lanes), lambda p: (0, p)),
            pl.BlockSpec((1, 2, tokens), lambda p: (p, 0, 0)),
        ],
        out_shape=[
            jax.ShapeDtypeStruct((tokens, width), jnp.bfloat16),
            jax.ShapeDtypeStruct((pairs, 2, tokens), jnp.float32),
        ],
        scratch_shapes=[pltpu.VMEM((LONG_LEN, LONG_LEN), jnp.float32), pltpu.VMEM((LONG_LEN, LONG_LEN), jnp.bfloat16)],
        cost_estimate=SMALL,
        name="attention_forward",
    )(lengths, bias, proj, proj, proj)


def attention_backward_kernel(
    lengths_ref, bias_ref, stat_ref, q_ref, k_ref, v_ref, mixed_ref, grad_ref, proj_ref, table_ref,
    score_ref, slope_ref, weight_ref, change_ref, stage_ref, done_ref,
):
    pair = pl.program_id(0)
    pairs = pl.num_programs(0)
    slot = pair % 2

    def copy(part, step):
        at = pl.multiple_of((part * pairs + step) * TILE, TILE)
        return pltpu.make_async_copy(
            stage_ref.at[step % 2, part], proj_ref.at[:, pl.ds(at, TILE)], done_ref.at[step % 2, part]
        )

    @pl.when(pair >= 2)
    def _():
        for part in range(3):
            copy(part, pair - 2).wait()

    tokens, lanes = q_ref.shape
    size = lanes // 2
    lane = lax.broadcasted_iota(jnp.int32, (1, lanes), 1)
    keys_t = k_ref[...].T
    product = (grad_ref[...].astype(jnp.float32) * mixed_ref[...].astype(jnp.float32)).T
    table_ref[...] = jnp.zeros_like(table_ref)
    for start, stop, visible, sure in items_of(tokens, lengths_ref):
        length = stop - start
        count = length // TILE
        query_grads, key_grads, value_grads = [], [], []
        for head in range(2):
            bias_row = bias_ref[0, head : head + 1, :]
            strip = bias_strip(bias_row)
            own = (lane >= head * size) & (lane < (head + 1) * size)
            query = jnp.where(own, q_ref[start:stop, :] * 0.125, 0.0).astype(jnp.bfloat16)
            grad = jnp.where(own, grad_ref[start:stop, :], 0.0).astype(jnp.bfloat16)
            score_ref[0:length, 0:length] = dot(k_ref[start:stop, :], query, NT)
            slope_ref[0:length, 0:length] = dot(v_ref[start:stop, :], grad, NT)
            inner = jnp.sum(product[head * size : (head + 1) * size, start:stop], axis=0, keepdims=True)
            sums = {-1: None, 0: None, 1: None}
            far = {-1: None, 1: None}
            for col in range(count):
                cols = slice(col * TILE, (col + 1) * TILE)
                base = stat_ref[0, head : head + 1, start + col * TILE : start + (col + 1) * TILE]
                middle = inner[:, cols]
                for row in range(count):
                    rows = slice(row * TILE, (row + 1) * TILE)
                    step = row - col
                    tile = score_ref[rows, cols] + (bias_tile(strip, bias_row, step) - base)
                    if (row + 1) * TILE > sure:
                        place = lax.broadcasted_iota(jnp.int32, (TILE, 1), 0) + row * TILE
                        tile = jnp.where(place < visible, tile, NEG)
                    tile = jnp.exp(tile)
                    weight_ref[rows, cols] = tile.astype(jnp.bfloat16)
                    tile = tile * (slope_ref[rows, cols] - middle)
                    change_ref[rows, cols] = tile.astype(jnp.bfloat16)
                    if abs(step) <= 1:
                        sums[step] = tile if sums[step] is None else sums[step] + tile
                    else:
                        side = 1 if step > 0 else -1
                        part = jnp.sum(tile, axis=0, keepdims=True)
                        far[side] = part if far[side] is None else far[side] + part
            for step, value in sums.items():
                if value is not None:
                    at = TILE - step * TILE
                    table_ref[0, head, 0:TILE, at : at + TILE] += value
            for side, value in far.items():
                if value is not None:
                    at = TILE - side * TILE
                    table_ref[0, head, TILE : TILE + 1, at : at + TILE] = value
            value_grads.append(dot(weight_ref[0:length, 0:length], grad))
            key_grads.append(dot(change_ref[0:length, 0:length], query))
            query_grads.append(dot(keys_t[head * size : (head + 1) * size, start:stop], change_ref[0:length, 0:length]))
        stage_ref[slot, 0, start:stop, :] = (jnp.concatenate(query_grads, axis=0).T * 0.125).astype(jnp.bfloat16)
        stage_ref[slot, 1, start:stop, :] = (key_grads[0] + key_grads[1]).astype(jnp.bfloat16)
        stage_ref[slot, 2, start:stop, :] = (value_grads[0] + value_grads[1]).astype(jnp.bfloat16)
    for part in range(3):
        copy(part, pair).start()

    @pl.when(pair == pairs - 1)
    def _():
        for part in range(3):
            copy(part, pair - 1).wait()
            copy(part, pair).wait()


def attention_backward(lengths, bias, stat, proj, mixed, grad):
    tokens, width = mixed.shape
    lanes = TILE
    pairs = width // lanes
    return pl.pallas_call(
        attention_backward_kernel,
        grid=(pairs,),
        in_specs=[
            pl.BlockSpec(memory_space=pltpu.SMEM),
            pl.BlockSpec((1, 2, bias.shape[2]), lambda p: (p, 0, 0)),
            pl.BlockSpec((1, 2, tokens), lambda p: (p, 0, 0)),
            pl.BlockSpec((tokens, lanes), lambda p: (0, p)),
            pl.BlockSpec((tokens, lanes), lambda p: (0, pairs + p)),
            pl.BlockSpec((tokens, lanes), lambda p: (0, 2 * pairs + p)),
            pl.BlockSpec((tokens, lanes), lambda p: (0, p)),
            pl.BlockSpec((tokens, lanes), lambda p: (0, p)),
        ],
        out_specs=[
            pl.BlockSpec(memory_space=pl.ANY),
            pl.BlockSpec((1, 2, TILE + 8, 3 * TILE), lambda p: (p, 0, 0, 0)),
        ],
        out_shape=[
            jax.ShapeDtypeStruct((tokens, 3 * width), jnp.bfloat16),
            jax.ShapeDtypeStruct((pairs, 2, TILE + 8, 3 * TILE), jnp.float32),
        ],
        scratch_shapes=[
            pltpu.VMEM((LONG_LEN, LONG_LEN), jnp.float32),
            pltpu.VMEM((LONG_LEN, LONG_LEN), jnp.float32),
            pltpu.VMEM((LONG_LEN, LONG_LEN), jnp.bfloat16),
            pltpu.VMEM((LONG_LEN, LONG_LEN), jnp.bfloat16),
            pltpu.VMEM((2, 3, tokens, lanes), jnp.bfloat16),
            pltpu.SemaphoreType.DMA((2, 3)),
        ],
        cost_estimate=SMALL,
        name="attention_backward",
    )(lengths, bias, stat, proj, proj, proj, mixed, grad)


def bucket_of(offset):
    distance = jnp.abs(offset)
    far = 8 + sum(((distance >= bound).astype(jnp.int32) for bound in BOUNDS))
    return jnp.where(distance < 8, distance, far) + 16 * (offset > 0).astype(jnp.int32)


def bias_rows(rel_table):
    bucket = bucket_of(2 * TILE - jnp.arange(4 * TILE, dtype=jnp.int32))
    onehot = (bucket[:, None] == jnp.arange(rel_table.shape[0], dtype=jnp.int32)[None, :]).astype(jnp.float32)
    return jnp.einsum("xb,bh->hx", onehot, rel_table, precision=HIGHEST).reshape(-1, 2, 4 * TILE)


def table_sums(tiles, buckets):
    row = jnp.arange(TILE + 8, dtype=jnp.int32)[:, None]
    col = jnp.arange(3 * TILE, dtype=jnp.int32)[None, :]
    near = bucket_of(row - col + TILE)
    far = jnp.where(col < TILE, buckets - 1, buckets // 2 - 1)
    bucket = jnp.where(row < TILE, near, far)
    onehot = (bucket[:, :, None] == jnp.arange(buckets, dtype=jnp.int32)).astype(jnp.float32)
    return jnp.einsum("ghrc,rcb->bgh", tiles, onehot, precision=HIGHEST).reshape(buckets, -1)


def pack_first_kernel(place_ref, routes_ref, rows_ref, *out_refs, experts, capacity):
    target_ref = out_refs[-1]
    tokens = routes_ref.shape[1]
    routes = [routes_ref[rank : rank + 1, :] for rank in range(TOP)]
    label = lax.broadcasted_iota(jnp.int32, (experts, 1), 0)
    picks = [label == route for route in routes]
    named = jnp.where(picks[0] | picks[1], 1.0, 0.0).astype(jnp.bfloat16)
    later = lax.broadcasted_iota(jnp.int32, (1, tokens), 1)
    earlier = lax.broadcasted_iota(jnp.int32, (tokens, 1), 0)
    count = dot(named, jnp.where(earlier < later, 1.0, 0.0).astype(jnp.bfloat16))
    for rank in range(TOP):
        position = jnp.sum(jnp.where(picks[rank], count, 0.0), axis=0, keepdims=True).astype(jnp.int32)
        apart = routes[rank] ^ place_ref[0]
        apart = jnp.where(apart < experts // 2, routes[rank] & (experts // 2 - 1), apart)
        target_ref[rank : rank + 1, :] = apart * capacity + position
    other = jnp.concatenate([routes[1], routes[0]], axis=0).astype(jnp.float32) + 1.0
    pack_kernel(target_ref, rows_ref, *out_refs[:-1], other=other, capacity=capacity)


def pack_kernel(target_ref, rows_ref, *out_refs, other=None, capacity):
    rows = rows_ref[...]
    base = 0
    for out_ref in out_refs:
        stride = capacity + (0 if other is None else EXTRA)
        for at in range(0, out_ref.shape[0], stride):
            slot = lax.broadcasted_iota(jnp.int32, (capacity, 1), 0) + base
            hits = [slot == target_ref[rank : rank + 1, :] for rank in range(TOP)]
            hit = jnp.where(hits[0] | hits[1], 1.0, 0.0).astype(jnp.bfloat16)
            out_ref[at : at + capacity, :] = dot(hit, rows).astype(jnp.bfloat16)
            if other is not None:
                named = sum(jnp.where(hits[rank], other[rank : rank + 1, :], 0.0) for rank in range(TOP))
                ones = jnp.ones((EXTRA, named.shape[1]), jnp.bfloat16)
                out_ref[at + capacity : at + stride, :] = jnp.zeros((EXTRA, out_ref.shape[1]), jnp.bfloat16)
                out_ref[at + capacity : at + stride, 0:capacity] = dot(ones, named.astype(jnp.bfloat16), NT).astype(jnp.bfloat16)
            base += capacity


def block_shapes(experts, rows, width):
    half = experts // 2
    return [jax.ShapeDtypeStruct((n * rows, width), jnp.bfloat16) for n in [half] + [1] * half]


def pack_first(place, routes, rows, experts, capacity):
    blocks = block_shapes(experts, capacity + EXTRA, rows.shape[1])
    *blocks, target = pl.pallas_call(
        lambda *refs: pack_first_kernel(*refs, experts=experts, capacity=capacity),
        in_specs=[pl.BlockSpec(memory_space=pltpu.SMEM), pl.BlockSpec(), pl.BlockSpec()],
        out_shape=blocks + [jax.ShapeDtypeStruct(routes.shape, jnp.int32)],
        cost_estimate=SMALL,
        name="pack_first",
    )(place, routes, rows)
    return blocks, target


def pack(target, rows, experts, capacity):
    return pl.pallas_call(
        lambda *refs: pack_kernel(*refs, capacity=capacity),
        out_shape=block_shapes(experts, capacity, rows.shape[1]),
        cost_estimate=SMALL,
        name="pack_rows",
    )(target, rows)


def gather_rows(target_ref, gates_ref, blocks):
    total = None
    base = 0
    for block in blocks:
        slot = lax.broadcasted_iota(jnp.int32, (1, block.shape[0]), 1) + base
        share = sum(
            jnp.where(target_ref[:, rank : rank + 1] == slot, gates_ref[:, rank : rank + 1], 0.0) for rank in range(TOP)
        )
        part = dot(share.astype(jnp.bfloat16), block[...])
        total = part if total is None else total + part
        base += block.shape[0]
    return total


def output_kernel(target_ref, gates_ref, resid_ref, *refs):
    refs[-1][...] = (resid_ref[...] + gather_rows(target_ref, gates_ref, refs[:-1])).astype(jnp.bfloat16)


def combine_output(target, gates, resid, blocks):
    return pl.pallas_call(
        output_kernel,
        out_shape=jax.ShapeDtypeStruct(resid.shape, jnp.bfloat16),
        cost_estimate=MEDIUM,
        name="combine_output",
    )(target, gates, resid, *blocks)


def combine_kernel(target_ref, gates_ref, resid_ref, scale_ref, gain_ref, upstream_ref, *refs):
    blocks, (grad_ref, low_ref, gain_grad_ref) = refs[:-3], refs[-3:]
    total = gather_rows(target_ref, gates_ref, blocks)
    scale = scale_ref[...]
    unit = resid_ref[...] * scale
    gain_grad_ref[...] = jnp.sum(total * unit, axis=0, keepdims=True)
    along = total * gain_ref[...]
    inner = jnp.mean(along * unit, axis=1, keepdims=True)
    grad = upstream_ref[...].astype(jnp.float32) + scale * (along - unit * inner)
    grad_ref[...] = grad
    low_ref[...] = grad.astype(jnp.bfloat16)


def combine(target, gates, resid, scale, gain, upstream, blocks):
    tokens, width = resid.shape
    return pl.pallas_call(
        combine_kernel,
        out_shape=[
            jax.ShapeDtypeStruct((tokens, width), jnp.float32),
            jax.ShapeDtypeStruct((tokens, width), jnp.bfloat16),
            jax.ShapeDtypeStruct((1, width), jnp.float32),
        ],
        cost_estimate=SMALL,
        name="combine_back",
    )(target, gates, resid, scale, gain, upstream, *blocks)


def spans(blocks, capacity, extra=0):
    base = 0
    for block in blocks:
        for at in range(0, block.shape[0], capacity + extra):
            yield block, at, base
            base += capacity


def expert_kernel(own_ref, slope_ref, wg_ref, wu_ref, wr_ref, other_ref, *refs, ways, parts):
    blocks, refs = refs[:ways], refs[-(8 + ways) :]
    hidden_ref, gate_ref, up_ref, share_ref, router_ref = refs[:5]
    pairs, (x_ref, acc_ref, dots_ref) = refs[5 : 5 + ways], refs[5 + ways :]
    step = pl.program_id(0)
    rows = x_ref.shape[0] // parts

    @pl.when(step == 0)
    def _():
        acc_ref[...] = jnp.zeros_like(acc_ref)
        dots_ref[...] = jnp.zeros_like(dots_ref)
        base = 0
        for block in blocks:
            x_ref[base : base + block.shape[0], :] = block[...]
            base += block.shape[0]

    for part in range(parts):
        span = slice(part * rows, (part + 1) * rows)
        x = x_ref[span, :]
        gate = dot(x, wg_ref[...])
        up = dot(x, wu_ref[...])
        slope = slope_ref[span, :].astype(jnp.float32)
        square = gate * gate
        rise = 0.5 + 0.5 * jnp.tanh(gate * (CURVE + (CURVE * CUBE) * square))
        unit = gate * rise
        bend = rise + (unit - unit * rise) * (2 * CURVE + (6 * CURVE * CUBE) * square)
        hidden = (unit * up).astype(jnp.bfloat16)
        hidden_ref[span, :] = hidden
        both = hidden.astype(jnp.float32) * slope
        dots_ref[span, :] += both[:, 0:TILE] + both[:, TILE : 2 * TILE]
        gate_grad = (slope * up * bend).astype(jnp.bfloat16)
        up_grad = (slope * unit).astype(jnp.bfloat16)
        gate_ref[span, :] = gate_grad
        up_ref[span, :] = up_grad
        acc_ref[span, :] += dot(gate_grad, wg_ref[...], NT) + dot(up_grad, wu_ref[...], NT)

    @pl.when(step == pl.num_programs(0) - 1)
    def _():
        logits = dot(x_ref[...], wr_ref[...], NT)
        label = lax.broadcasted_iota(jnp.int32, (1, TILE), 1)
        mine = label == own_ref[0]
        theirs = label == other_ref[:, 0:1].astype(jnp.int32) - 1
        first = jnp.sum(jnp.where(mine, logits, 0.0), axis=1, keepdims=True)
        second = jnp.sum(jnp.where(theirs, logits, 0.0), axis=1, keepdims=True)
        top = jnp.maximum(first, second)
        first = jnp.exp(first - top)
        second = jnp.exp(second - top)
        total = first + second
        first = first / total
        second = second / total
        inner = jnp.sum(dots_ref[...], axis=1, keepdims=True)
        coef = inner * second * (jnp.where(mine, 1.0, 0.0) - jnp.where(theirs, 1.0, 0.0))
        share_ref[...] = jnp.broadcast_to(first, share_ref.shape)
        router_ref[...] = dot((first * coef).astype(jnp.bfloat16), x_ref[...], TN)
        acc_ref[...] += dot(coef.astype(jnp.bfloat16), wr_ref[...])
        base = 0
        for pair in pairs:
            pair[...] = acc_ref[base : base + pair.shape[0], :].astype(jnp.bfloat16)
            base += pair.shape[0]


def once(shape):
    return pl.BlockSpec(shape, lambda i: (0, 0), pipeline_mode=pl.Buffered(1))


def expert_rows(own, blocks, slope, wg, wu, wr, other, chunk, kept, parts=2):
    n = slope.shape[0] // 2
    d, f = wg.shape
    ways = len(blocks)
    tile = pl.BlockSpec((n, FT), lambda i: (chunk, i))
    weight = pl.BlockSpec((d, FT), lambda i: (0, i))
    fixed = lambda shape: pl.BlockSpec(shape, lambda i: (0, 0))
    hidden, gate, up, share, router, *pairs = pl.pallas_call(
        lambda *refs: expert_kernel(*refs, ways=ways, parts=parts),
        grid=(f // FT,),
        in_specs=[
            pl.BlockSpec(memory_space=pltpu.SMEM),
            tile,
            weight,
            weight,
            once((TILE, d)),
            pl.BlockSpec((n, TILE), lambda i: (chunk, 0), pipeline_mode=pl.Buffered(1)),
        ]
        + [once(block.shape) for block in blocks]
        + [pl.BlockSpec(memory_space=pl.ANY) for _ in kept],
        out_specs=[tile, tile, tile, fixed((n, TILE)), fixed((TILE, d))] + [fixed(block.shape) for block in blocks],
        out_shape=[jax.ShapeDtypeStruct((2 * n, f), jnp.bfloat16)] * 3
        + [jax.ShapeDtypeStruct((n, TILE), jnp.float32), jax.ShapeDtypeStruct((TILE, d), jnp.float32)]
        + [jax.ShapeDtypeStruct(block.shape, jnp.bfloat16) for block in blocks],
        scratch_shapes=[
            pltpu.VMEM((n, d), jnp.bfloat16),
            pltpu.VMEM((n, d), jnp.float32),
            pltpu.VMEM((n, TILE), jnp.float32),
        ],
        input_output_aliases={6 + ways + k: k for k in range(len(kept))},
        cost_estimate=SHORT if chunk else SMALL,
        name="expert_rows",
    )(own, slope, wg, wu, wr, other, *blocks, *kept)
    return (hidden, gate, up), share, router, pairs


def slope_kernel(wd_ref, *refs, capacity):
    blocks, (out_ref, other_ref, u_ref) = refs[:-3], refs[-3:]

    @pl.when(pl.program_id(0) == 0)
    def _():
        reach = -(-capacity // TILE) * TILE
        for block, at, base in spans(blocks, capacity, EXTRA):
            u_ref[base : base + capacity, :] = block[at : at + capacity, :]
            named = block[at + capacity : at + capacity + EXTRA, 0:reach].astype(jnp.float32).T
            other_ref[base : base + capacity, :] = jnp.broadcast_to(named[0:capacity, 0:1], (capacity, TILE))

    out_ref[...] = dot(u_ref[...], wd_ref[...], NT).astype(jnp.bfloat16)


def slope_rows(blocks, wd, experts, capacity):
    f, d = wd.shape
    n = experts * capacity
    return pl.pallas_call(
        lambda *refs: slope_kernel(*refs, capacity=capacity),
        grid=(f // FT,),
        in_specs=[pl.BlockSpec((FT, d), lambda i: (i, 0))] + [once(block.shape) for block in blocks],
        out_specs=[pl.BlockSpec((n, FT), lambda i: (0, i)), pl.BlockSpec((n, TILE), lambda i: (0, 0))],
        out_shape=[jax.ShapeDtypeStruct((n, f), jnp.bfloat16), jax.ShapeDtypeStruct((n, TILE), jnp.float32)],
        scratch_shapes=[pltpu.VMEM((n, d), jnp.bfloat16)],
        cost_estimate=LARGE,
        name="slope_rows",
    )(wd, *blocks)


def gate_slots(target_ref, blocks, near_ref, far_ref, capacity, extra):
    for block, at, base in spans(blocks, capacity, extra):
        share_ref, start = (near_ref, base) if base < near_ref.shape[0] else (far_ref, base - near_ref.shape[0])
        value = block[at : at + capacity, :].astype(jnp.float32) * share_ref[start : start + capacity, 0:1]
        target_ref[base : base + capacity, :] = value.astype(jnp.bfloat16)


def weight_kernel(hidden, gate, up, near_ref, far_ref, *refs, ways, copies, capacity):
    rows, raw, refs = refs[:ways], refs[ways : 2 * ways], refs[2 * ways :]
    out_ref, rows_ref, raw_ref, stage_ref, down_ref, done_ref, sent_ref = refs
    step = pl.program_id(0)
    steps = pl.num_programs(0)
    d = stage_ref.shape[2] // 2
    piece = d // copies
    part_of = out_ref.shape[0] // copies

    def whole(at):
        return pltpu.make_async_copy(
            stage_ref.at[at % 2], out_ref.at[pl.ds(pl.multiple_of(at * FT, FT), FT), 0 : 2 * d], done_ref.at[at % 2]
        )

    def small(at, part, copy):
        row = at * FT + part * 64
        column = pl.multiple_of(2 * d + row // part_of * piece, piece)
        return pltpu.make_async_copy(
            down_ref.at[at % 2, part * 64 : (part + 1) * 64, copy * piece : (copy + 1) * piece],
            out_ref.at[pl.ds(pl.multiple_of(copy * part_of + row % part_of, 64), 64), pl.ds(column, piece)],
            sent_ref.at[at % 2, part, copy],
        )

    def finish(at):
        whole(at).wait()
        for part in range(FT // 64):
            for copy in range(copies):
                small(at, part, copy).wait()

    @pl.when(step == 0)
    def _():
        gate_slots(rows_ref, rows, near_ref, far_ref, capacity, 0)
        gate_slots(raw_ref, raw, near_ref, far_ref, capacity, EXTRA)

    @pl.when(step >= 2)
    def _():
        finish(step - 2)

    slot = step % 2
    stage_ref[slot, :, 0:d] = dot(gate[...], rows_ref[...], TN).astype(jnp.bfloat16)
    stage_ref[slot, :, d : 2 * d] = dot(up[...], rows_ref[...], TN).astype(jnp.bfloat16)
    down_ref[slot] = dot(hidden[...], raw_ref[...], TN).astype(jnp.bfloat16)
    whole(step).start()
    for part in range(FT // 64):
        for copy in range(copies):
            small(step, part, copy).start()

    @pl.when(step == steps - 1)
    def _():
        finish(step - 1)
        finish(step)


def weight_grads(hidden, gate, up, shares, rows, raw, copies, capacity):
    n, f = hidden.shape
    d = rows[0].shape[1]
    ways = len(rows)
    narrow = pl.BlockSpec((n, FT), lambda i: (0, i))
    return pl.pallas_call(
        lambda *refs: weight_kernel(*refs, ways=ways, copies=copies, capacity=capacity),
        grid=(f // FT,),
        in_specs=[narrow] * 3 + [once(part.shape) for part in (*shares, *rows, *raw)],
        out_specs=pl.BlockSpec(memory_space=pl.ANY),
        out_shape=jax.ShapeDtypeStruct((f, 3 * d), jnp.bfloat16),
        scratch_shapes=[
            pltpu.VMEM((n, d), jnp.bfloat16),
            pltpu.VMEM((n, d), jnp.bfloat16),
            pltpu.VMEM((2, FT, 2 * d), jnp.bfloat16),
            pltpu.VMEM((2, FT, d), jnp.bfloat16),
            pltpu.SemaphoreType.DMA((2,)),
            pltpu.SemaphoreType.DMA((2, FT // 64, copies)),
        ],
        cost_estimate=SMALL,
        name="weight_grads",
    )(hidden, gate, up, *shares, *rows, *raw)


def result_kernel(hidden_ref, wd_ref, *refs):
    results, acc_ref = refs[:-1], refs[-1]
    step = pl.program_id(0)
    part = dot(hidden_ref[...], wd_ref[...])

    @pl.when(step == 0)
    def _():
        acc_ref[...] = part

    @pl.when(step > 0)
    def _():
        acc_ref[...] += part

    @pl.when(step == pl.num_programs(0) - 1)
    def _():
        base = 0
        for result in results:
            result[...] = acc_ref[base : base + result.shape[0], :].astype(jnp.bfloat16)
            base += result.shape[0]


def result_rows(hidden, wd, shapes):
    n, f = hidden.shape
    d = wd.shape[1]
    tile = FT * 2 if f % (FT * 2) == 0 else FT
    return pl.pallas_call(
        result_kernel,
        grid=(f // tile,),
        in_specs=[pl.BlockSpec((n, tile), lambda i: (0, i)), pl.BlockSpec((tile, d), lambda i: (i, 0))],
        out_specs=[pl.BlockSpec(shape, lambda i: (0, 0)) for shape in shapes],
        out_shape=[jax.ShapeDtypeStruct(shape, jnp.bfloat16) for shape in shapes],
        scratch_shapes=[pltpu.VMEM((n, d), jnp.float32)],
        cost_estimate=SMALL,
        name="result_rows",
    )(hidden, wd)


def shared_kernel(core_ref, first_ref, wide_ref, second_ref, narrow_ref, *refs, steps, early, unit):
    low_refs, high_refs, left_ref = refs[:2], refs[2:4], refs[4]
    step = pl.program_id(0)

    def store(value):
        own = core_ref[0] == 0

        def fill(mine_ref, away_ref):
            for group in range(mine_ref.shape[0] // unit):
                low = value[2 * group * unit : (2 * group + 1) * unit, :]
                high = value[(2 * group + 1) * unit : (2 * group + 2) * unit, :]
                span = slice(group * unit, (group + 1) * unit)
                mine_ref[span, :] = jnp.where(own, low, high).astype(jnp.bfloat16)
                away_ref[span, :] = jnp.where(own, high, low).astype(jnp.bfloat16)

        pl.when(step < early)(lambda: fill(*low_refs))
        pl.when(step >= early)(lambda: fill(*high_refs))

    @pl.when(step == 0)
    def _():
        left_ref[...] = first_ref[...].T

    @pl.when(step == steps)
    def _():
        left_ref[...] = second_ref[...].T

    @pl.when(step < steps)
    def _():
        store(dot(left_ref[...], wide_ref[...]))

    @pl.when(step >= steps)
    def _():
        store(dot(left_ref[...], narrow_ref[...]))


def shared_grads(core, first, wide, second, narrow, unit):
    tokens, rows = first.shape
    tile = 512
    steps, more = wide.shape[1] // tile, narrow.shape[1] // tile
    whole = once((tokens, rows))
    early = (steps + more) * 5 // 8
    low = pl.BlockSpec((rows // 2, tile), lambda i: (0, jnp.minimum(i, early - 1)))
    high = pl.BlockSpec((rows // 2, tile), lambda i: (0, jnp.maximum(i - early, 0)))
    shapes = [jax.ShapeDtypeStruct((rows // 2, n * tile), jnp.bfloat16) for n in (early, steps + more - early)]
    return pl.pallas_call(
        lambda *refs: shared_kernel(*refs, steps=steps, early=early, unit=unit),
        grid=(steps + more,),
        in_specs=[
            pl.BlockSpec(memory_space=pltpu.SMEM),
            whole,
            pl.BlockSpec((tokens, tile), lambda i: (0, jnp.minimum(i, steps - 1))),
            whole,
            pl.BlockSpec((tokens, tile), lambda i: (0, jnp.maximum(i - steps, 0))),
        ],
        out_specs=[low, low, high, high],
        out_shape=[shapes[0], shapes[0], shapes[1], shapes[1]],
        scratch_shapes=[pltpu.VMEM((rows, tokens), jnp.bfloat16)],
        cost_estimate=SMALL,
        name="shared_grads",
    )(core, first, wide, second, narrow)


def after(value, *before):
    return lax.optimization_barrier((value,) + before)[0]


def swap(value, axis, step):
    size = lax.axis_size(axis)
    return lax.ppermute(value, axis, [(k, k ^ step) for k in range(size)])


def parted(value, bit):
    return [lax.dynamic_index_in_dim(value, place, 0, keepdims=False) for place in (bit, 1 - bit)]


def added(first, second):
    return (first.astype(jnp.float32) + second.astype(jnp.float32)).astype(jnp.bfloat16)


def dp_halves(parts, unit):
    copies, chips = lax.axis_size("dp"), lax.axis_size("expert") // 2
    parts = [part.reshape(copies // 2, 2, chips * unit, -1) for part in parts]
    place = lax.axis_index("dp")
    cut = parts[0].shape[-1] // 2
    low = [jnp.swapaxes(part[..., :cut], 0, 1) for part in parts]
    high = [part[..., cut:] for part in parts]
    halves = []
    for pair, bit in ((low, place % 2), (high, place // 2)):
        stay, leave = zip(*(parted(part, bit) for part in pair))
        halves.append((added(*stay), added(*leave)))
    return halves


def dp_sums(halves, unit, *work):
    place = lax.axis_index("dp")
    came = [swap(leave, "dp", step) for (_, leave), step in zip(halves, (1, 2))]
    *came, _ = lax.optimization_barrier((*came, work))
    total = []
    for (stay, _), other, bit, step in zip(halves, came, (place // 2, place % 2), (2, 1)):
        mine, mine_too = (parted(part, bit) for part in (stay, other))
        leave = swap(added(mine[1], mine_too[1]), "dp", step)
        total.append(mine[0].astype(jnp.float32) + mine_too[0].astype(jnp.float32) + leave.astype(jnp.float32))
    chips = lax.axis_size("expert") // 2
    total = jnp.concatenate(total, axis=1).astype(jnp.bfloat16).reshape(chips, unit, -1)
    place = lax.axis_index("expert") // 2
    return [lax.dynamic_index_in_dim(total, place ^ step, 0, keepdims=False) for step in range(chips)]


def total_of(parts):
    return sum(part.astype(jnp.float32) for part in parts)


def chip_parts(parts, unit):
    copies, chips = lax.axis_size("dp"), lax.axis_size("expert") // 2
    place = lax.axis_index("expert") // 2
    parts = [part.reshape(copies, chips, unit, -1) for part in parts]
    return [
        added(*(lax.dynamic_index_in_dim(part, place ^ step, 1, keepdims=False) for part in parts))
        for step in range(chips)
    ]


def sent(parts, axis, stride):
    return [swap(part, axis, stride * step) if step else part for step, part in enumerate(parts)]


def on_device(
    block_input,
    routes,
    item_lengths,
    w_qkv,
    w_attn_out,
    rel_table,
    gain_attn,
    gain_moe,
    w_router,
    w_gate,
    w_up,
    w_down,
    cotangent,
):
    tokens, width = block_input.shape
    experts = w_router.shape[1]
    capacity = TOK_DEV * TOP * 5 // (4 * experts)
    slots = experts * capacity
    buckets = rel_table.shape[0]
    copies, ways = lax.axis_size("dp"), lax.axis_size("expert")
    place = lax.axis_index("expert").astype(jnp.int32)
    own = place.reshape(1)
    labels = jnp.arange(experts, dtype=jnp.int32)
    picks = [routes[:, rank : rank + 1] == labels[None, :] for rank in range(TOP)]
    places = jnp.arange(slots, dtype=jnp.int32)

    half = ways // 2
    groups = [list(range(k * half, (k + 1) * half)) for k in range(2)]

    def near(block):
        parts = block.reshape(half, -1, block.shape[1])
        parts = lax.all_to_all(parts, "expert", split_axis=0, concat_axis=0, axis_index_groups=groups, tiled=True)
        return parts.reshape(block.shape)

    def exchange(blocks, *before):
        far = [swap(block, "expert", half + step) for step, block in enumerate(blocks[1:])]
        return [near(after(blocks[0], *before))] + far

    packed, target_rows = pack_first(own, routes.T, cotangent, experts, capacity)
    target = target_rows.T
    block_input = after(block_input, *packed)
    inputs = block_input.astype(jnp.float32)
    normed, unit_one, scale_one = normalize_forward(inputs, gain_attn)
    raw = exchange(packed, scale_one)
    attn_in = normed.astype(jnp.bfloat16)
    bias = bias_rows(rel_table)
    proj = dot(attn_in, w_qkv).astype(jnp.bfloat16)
    mixed, stat = attention_forward(item_lengths, bias, proj)
    attn = dot(mixed, w_attn_out)
    resid = inputs + attn
    second, unit_two, scale_two = normalize_forward(resid, gain_moe)
    moe_in = second.astype(jnp.bfloat16)
    *packed, _ = lax.optimization_barrier((*pack(target_rows, moe_in, experts, capacity), raw))
    logits = dot(moe_in, w_router)
    chosen = jnp.stack([jnp.sum(jnp.where(pick, logits, 0.0), axis=1) for pick in picks], axis=1)
    highest = jnp.max(chosen, axis=1, keepdims=True)
    exps = jnp.exp(chosen - highest)
    gates = exps / jnp.sum(exps, axis=1, keepdims=True)
    rows = exchange(packed, gates)
    gate_weight, up_weight, down_weight = w_gate[0], w_up[0], w_down[0]
    router_rows = jnp.pad(w_router.T, ((0, TILE - experts), (0, 0)))
    slope, other = slope_rows(raw, down_weight, experts, capacity)
    weights = (gate_weight, up_weight, router_rows, other)
    kept, near_share, near_router, near_pairs = expert_rows(own, rows[:1], slope, *weights, 0, ())
    back = [near(near_pairs[0])]
    rows[1:] = [after(block, near_pairs[0]) for block in rows[1:]]
    kept, far_share, far_router, far_pairs = expert_rows(own, rows[1:], slope, *weights, 1, kept)
    back += [swap(block, "expert", half + step) for step, block in enumerate(far_pairs)]
    hidden, gate_pre_grad, up_pre_grad = kept
    shares = (near_share, far_share)
    hidden = after(hidden, back[0])
    weight_grad = weight_grads(hidden, gate_pre_grad, up_pre_grad, shares, rows, raw, copies, capacity)
    weight_sum = lax.psum_scatter(weight_grad, "dp", scatter_dimension=0, tiled=True)
    result = result_rows(after(hidden, weight_grad), down_weight, [block.shape for block in rows])
    *back, held = lax.optimization_barrier((*back, result[0]))
    result = [after(block, *back) for block in (held, *result[1:])]
    returned = exchange(result)
    resid_grad, attn_grad, gain_moe_grad = combine(
        target, gates, resid, scale_two, gain_moe.reshape(1, width), cotangent, back
    )
    mixed_grad = dot(attn_grad, w_attn_out, NT).astype(jnp.bfloat16)
    proj_grad, tiles = attention_backward(item_lengths, bias, stat, proj, mixed, mixed_grad)
    unit = width // (copies * ways)
    low, low_away, high, high_away = shared_grads(own % 2, attn_in, proj_grad, mixed, attn_grad, unit)
    dp_parts = dp_halves((low, swap(after(low_away, *returned), "expert", 1)), unit)
    z_parts = chip_parts((high, swap(after(high_away, *returned), "expert", 1)), unit)
    proj_grad, _ = lax.optimization_barrier((proj_grad, (dp_parts, z_parts)))
    table_grad = table_sums(tiles, buckets)
    router_grad = (near_router + far_router)[:experts].T
    attn_in_grad = dot(proj_grad, w_qkv, NT)
    input_norm_grad, gain_attn_grad = normalize_backward(attn_in_grad, unit_one, scale_one, gain_attn)
    input_grad = resid_grad + input_norm_grad
    output = combine_output(target, gates, after(resid, dp_parts[0][1]), returned)
    small = (table_grad.reshape(-1), gain_attn_grad, gain_moe_grad, router_grad)
    sizes = [part.size // (copies * ways) for part in small]
    together = jnp.concatenate([part.reshape(copies * ways, -1) for part in small], axis=1)
    *z_came, _ = lax.optimization_barrier((*sent(z_parts, "expert", 2), (input_grad, output, together)))
    halves = dp_sums(dp_parts, unit, input_grad, output, together, z_came)
    z_sum = total_of(z_came).astype(jnp.bfloat16)
    dp_place = lax.axis_index("dp")
    z_sum = [lax.dynamic_index_in_dim(z_sum, dp_place ^ step, 0, keepdims=False) for step in range(copies)]
    together = lax.all_to_all(together, ("dp", "expert"), split_axis=0, concat_axis=0, tiled=True)
    piece = width // copies
    down_sum = jnp.concatenate(
        [weight_sum[:, 2 * width + k * piece : 2 * width + (k + 1) * piece] for k in range(copies)], axis=0
    )
    experts_out = (
        weight_sum[:, :width].astype(jnp.float32).T[None],
        weight_sum[:, width : 2 * width].astype(jnp.float32).T[None],
        down_sum.astype(jnp.float32)[None],
    )
    low, high = sent(halves, "expert", 2), sent(z_sum, "dp", 1)
    (low, high), together, _ = lax.optimization_barrier(((low, high), together, experts_out))
    together = jnp.sum(together, axis=0)
    at = [sum(sizes[:k]) for k in range(5)]
    table_sum, attn_sum, moe_sum, router_sum = [together[at[k] : at[k + 1]] for k in range(4)]
    sums = jnp.concatenate([total_of(low), total_of(high)], axis=1)
    return (
        output,
        input_grad,
        sums[:, : 3 * width],
        sums[:, 3 * width :],
        table_sum,
        attn_sum,
        moe_sum,
        router_sum.reshape(-1, experts),
        *experts_out,
    )


def solution(mesh):
    return jax.shard_map(
        on_device,
        mesh=mesh,
        in_specs=(
            P(("dp", "expert"), None),
            P(("dp", "expert"), None),
            P(("dp", "expert"), None),
            P(),
            P(),
            P(),
            P(),
            P(),
            P(),
            P("expert", None, None),
            P("expert", None, None),
            P("expert", None, None),
            P(("dp", "expert"), None),
        ),
        out_specs=(
            P(("dp", "expert"), None),
            P(("dp", "expert"), None),
            P(("dp", "expert"), None),
            P(("dp", "expert"), None),
            P(("dp", "expert")),
            P(("dp", "expert")),
            P(("dp", "expert")),
            P(("dp", "expert"), None),
            P("expert", None, "dp"),
            P("expert", None, "dp"),
            P("expert", None, "dp"),
        ),
        check_vma=False,
    )
```

```python
import jax
import jax.numpy as jnp
from jax import lax
from jax.experimental import pallas as pl
from jax.experimental.pallas import tpu as pltpu
from jax.sharding import PartitionSpec as P

TOP = 2
LONG_LEN = 512
SHORT_LEN = 128
TOK_DEV = 640
BOUNDS = (12, 16, 23, 32, 46, 64, 91)
EPSILON = 1e-06
HIGHEST = lax.Precision.HIGHEST
TILE = 128
FT = 256
NEG = -1e30
NN = (((1,), (0,)), ((), ()))
NT = (((1,), (1,)), ((), ()))
TN = (((0,), (0,)), ((), ()))
CURVE = 0.7978845608028654
CUBE = 0.044715
EXTRA = 8
SHORT = pl.CostEstimate(flops=23_000_000_000, bytes_accessed=1 << 16, transcendentals=0)
SMALL = pl.CostEstimate(flops=1 << 20, bytes_accessed=1 << 16, transcendentals=0)
MEDIUM = pl.CostEstimate(flops=265_650_000_000, bytes_accessed=1 << 16, transcendentals=0)
LARGE = pl.CostEstimate(flops=1 << 38, bytes_accessed=1 << 28, transcendentals=0)


def dot(a, b, dims=NN):
    return lax.dot_general(a, b, dims, preferred_element_type=jnp.float32)


def normalize_forward(value, gain):
    scale = lax.rsqrt(jnp.mean(value * value, axis=-1, keepdims=True) + EPSILON)
    unit = value * scale
    return (unit * gain, unit, scale)


def normalize_backward(grad, unit, scale, gain):
    gain_grad = jnp.sum(grad * unit, axis=0)
    along = grad * gain
    inner = jnp.mean(along * unit, axis=-1, keepdims=True)
    return (scale * (along - unit * inner), gain_grad)


def bias_strip(bias_row):
    wide = jnp.broadcast_to(bias_row, (TILE, bias_row.shape[1]))
    return pltpu.roll(wide, 0, 1, stride=1, stride_axis=0)


def bias_tile(strip, bias_row, step):
    if abs(step) <= 1:
        start = 2 * TILE - step * TILE
        return strip[:, start : start + TILE]
    last = bias_row.shape[1] - 1
    return bias_row[:, 0:1] if step > 0 else bias_row[:, last : last + 1]


def items_of(tokens, lengths_ref):
    return ((0, LONG_LEN, lengths_ref[0, 0], LONG_LEN // 2), (LONG_LEN, tokens, lengths_ref[0, 1], SHORT_LEN // 2))


def attention_forward_kernel(lengths_ref, bias_ref, q_ref, k_ref, v_ref, mixed_ref, stat_ref, score_ref, exp_ref):
    tokens, lanes = q_ref.shape
    size = lanes // 2
    lane = lax.broadcasted_iota(jnp.int32, (1, lanes), 1)
    values_t = v_ref[...].T
    for start, stop, visible, sure in items_of(tokens, lengths_ref):
        length = stop - start
        count = length // TILE
        outs = []
        for head in range(2):
            bias_row = bias_ref[0, head : head + 1, :]
            strip = bias_strip(bias_row)
            own = (lane >= head * size) & (lane < (head + 1) * size)
            query = jnp.where(own, q_ref[start:stop, :] * 0.125, 0.0).astype(jnp.bfloat16)
            score_ref[0:length, 0:length] = dot(k_ref[start:stop, :], query, NT)
            totals = []
            for col in range(count):
                cols = slice(col * TILE, (col + 1) * TILE)
                top = None
                for row in range(count):
                    rows = slice(row * TILE, (row + 1) * TILE)
                    tile = score_ref[rows, cols] + bias_tile(strip, bias_row, row - col)
                    if (row + 1) * TILE > sure:
                        place = lax.broadcasted_iota(jnp.int32, (TILE, 1), 0) + row * TILE
                        tile = jnp.where(place < visible, tile, NEG)
                    score_ref[rows, cols] = tile
                    peak = jnp.max(tile, axis=0, keepdims=True)
                    top = peak if top is None else jnp.maximum(top, peak)
                total = jnp.zeros((1, TILE), jnp.float32)
                for row in range(count):
                    rows = slice(row * TILE, (row + 1) * TILE)
                    tile = jnp.exp(score_ref[rows, cols] - top)
                    total = total + jnp.sum(tile, axis=0, keepdims=True)
                    exp_ref[rows, cols] = tile.astype(jnp.bfloat16)
                totals.append(total)
                stat_ref[0, head : head + 1, start + col * TILE : start + (col + 1) * TILE] = top + jnp.log(total)
            total = jnp.concatenate(totals, axis=1)
            out = dot(values_t[head * size : (head + 1) * size, start:stop], exp_ref[0:length, 0:length])
            outs.append(out / total)
        mixed_ref[start:stop, :] = jnp.concatenate(outs, axis=0).T.astype(jnp.bfloat16)


def attention_forward(lengths, bias, proj):
    tokens, width = proj.shape[0], proj.shape[1] // 3
    lanes = TILE
    pairs = width // lanes
    return pl.pallas_call(
        attention_forward_kernel,
        grid=(pairs,),
        in_specs=[
            pl.BlockSpec(memory_space=pltpu.SMEM),
            pl.BlockSpec((1, 2, bias.shape[2]), lambda p: (p, 0, 0)),
            pl.BlockSpec((tokens, lanes), lambda p: (0, p)),
            pl.BlockSpec((tokens, lanes), lambda p: (0, pairs + p)),
            pl.BlockSpec((tokens, lanes), lambda p: (0, 2 * pairs + p)),
        ],
        out_specs=[
            pl.BlockSpec((tokens, lanes), lambda p: (0, p)),
            pl.BlockSpec((1, 2, tokens), lambda p: (p, 0, 0)),
        ],
        out_shape=[
            jax.ShapeDtypeStruct((tokens, width), jnp.bfloat16),
            jax.ShapeDtypeStruct((pairs, 2, tokens), jnp.float32),
        ],
        scratch_shapes=[pltpu.VMEM((LONG_LEN, LONG_LEN), jnp.float32), pltpu.VMEM((LONG_LEN, LONG_LEN), jnp.bfloat16)],
        cost_estimate=SMALL,
        name="attention_forward",
    )(lengths, bias, proj, proj, proj)


def attention_backward_kernel(
    lengths_ref, bias_ref, stat_ref, q_ref, k_ref, v_ref, mixed_ref, grad_ref, proj_ref, table_ref,
    score_ref, slope_ref, weight_ref, change_ref, stage_ref, done_ref,
):
    pair = pl.program_id(0)
    pairs = pl.num_programs(0)
    slot = pair % 2

    def copy(part, step):
        at = pl.multiple_of((part * pairs + step) * TILE, TILE)
        return pltpu.make_async_copy(
            stage_ref.at[step % 2, part], proj_ref.at[:, pl.ds(at, TILE)], done_ref.at[step % 2, part]
        )

    @pl.when(pair >= 2)
    def _():
        for part in range(3):
            copy(part, pair - 2).wait()

    tokens, lanes = q_ref.shape
    size = lanes // 2
    lane = lax.broadcasted_iota(jnp.int32, (1, lanes), 1)
    keys_t = k_ref[...].T
    product = (grad_ref[...].astype(jnp.float32) * mixed_ref[...].astype(jnp.float32)).T
    table_ref[...] = jnp.zeros_like(table_ref)
    for start, stop, visible, sure in items_of(tokens, lengths_ref):
        length = stop - start
        count = length // TILE
        query_grads, key_grads, value_grads = [], [], []
        for head in range(2):
            bias_row = bias_ref[0, head : head + 1, :]
            strip = bias_strip(bias_row)
            own = (lane >= head * size) & (lane < (head + 1) * size)
            query = jnp.where(own, q_ref[start:stop, :] * 0.125, 0.0).astype(jnp.bfloat16)
            grad = jnp.where(own, grad_ref[start:stop, :], 0.0).astype(jnp.bfloat16)
            score_ref[0:length, 0:length] = dot(k_ref[start:stop, :], query, NT)
            slope_ref[0:length, 0:length] = dot(v_ref[start:stop, :], grad, NT)
            inner = jnp.sum(product[head * size : (head + 1) * size, start:stop], axis=0, keepdims=True)
            sums = {-1: None, 0: None, 1: None}
            far = {-1: None, 1: None}
            for col in range(count):
                cols = slice(col * TILE, (col + 1) * TILE)
                base = stat_ref[0, head : head + 1, start + col * TILE : start + (col + 1) * TILE]
                middle = inner[:, cols]
                for row in range(count):
                    rows = slice(row * TILE, (row + 1) * TILE)
                    step = row - col
                    tile = score_ref[rows, cols] + (bias_tile(strip, bias_row, step) - base)
                    if (row + 1) * TILE > sure:
                        place = lax.broadcasted_iota(jnp.int32, (TILE, 1), 0) + row * TILE
                        tile = jnp.where(place < visible, tile, NEG)
                    tile = jnp.exp(tile)
                    weight_ref[rows, cols] = tile.astype(jnp.bfloat16)
                    tile = tile * (slope_ref[rows, cols] - middle)
                    change_ref[rows, cols] = tile.astype(jnp.bfloat16)
                    if abs(step) <= 1:
                        sums[step] = tile if sums[step] is None else sums[step] + tile
                    else:
                        side = 1 if step > 0 else -1
                        part = jnp.sum(tile, axis=0, keepdims=True)
                        far[side] = part if far[side] is None else far[side] + part
            for step, value in sums.items():
                if value is not None:
                    at = TILE - step * TILE
                    table_ref[0, head, 0:TILE, at : at + TILE] += value
            for side, value in far.items():
                if value is not None:
                    at = TILE - side * TILE
                    table_ref[0, head, TILE : TILE + 1, at : at + TILE] = value
            value_grads.append(dot(weight_ref[0:length, 0:length], grad))
            key_grads.append(dot(change_ref[0:length, 0:length], query))
            query_grads.append(dot(keys_t[head * size : (head + 1) * size, start:stop], change_ref[0:length, 0:length]))
        stage_ref[slot, 0, start:stop, :] = (jnp.concatenate(query_grads, axis=0).T * 0.125).astype(jnp.bfloat16)
        stage_ref[slot, 1, start:stop, :] = (key_grads[0] + key_grads[1]).astype(jnp.bfloat16)
        stage_ref[slot, 2, start:stop, :] = (value_grads[0] + value_grads[1]).astype(jnp.bfloat16)
    for part in range(3):
        copy(part, pair).start()

    @pl.when(pair == pairs - 1)
    def _():
        for part in range(3):
            copy(part, pair - 1).wait()
            copy(part, pair).wait()


def attention_backward(lengths, bias, stat, proj, mixed, grad):
    tokens, width = mixed.shape
    lanes = TILE
    pairs = width // lanes
    return pl.pallas_call(
        attention_backward_kernel,
        grid=(pairs,),
        in_specs=[
            pl.BlockSpec(memory_space=pltpu.SMEM),
            pl.BlockSpec((1, 2, bias.shape[2]), lambda p: (p, 0, 0)),
            pl.BlockSpec((1, 2, tokens), lambda p: (p, 0, 0)),
            pl.BlockSpec((tokens, lanes), lambda p: (0, p)),
            pl.BlockSpec((tokens, lanes), lambda p: (0, pairs + p)),
            pl.BlockSpec((tokens, lanes), lambda p: (0, 2 * pairs + p)),
            pl.BlockSpec((tokens, lanes), lambda p: (0, p)),
            pl.BlockSpec((tokens, lanes), lambda p: (0, p)),
        ],
        out_specs=[
            pl.BlockSpec(memory_space=pl.ANY),
            pl.BlockSpec((1, 2, TILE + 8, 3 * TILE), lambda p: (p, 0, 0, 0)),
        ],
        out_shape=[
            jax.ShapeDtypeStruct((tokens, 3 * width), jnp.bfloat16),
            jax.ShapeDtypeStruct((pairs, 2, TILE + 8, 3 * TILE), jnp.float32),
        ],
        scratch_shapes=[
            pltpu.VMEM((LONG_LEN, LONG_LEN), jnp.float32),
            pltpu.VMEM((LONG_LEN, LONG_LEN), jnp.float32),
            pltpu.VMEM((LONG_LEN, LONG_LEN), jnp.bfloat16),
            pltpu.VMEM((LONG_LEN, LONG_LEN), jnp.bfloat16),
            pltpu.VMEM((2, 3, tokens, lanes), jnp.bfloat16),
            pltpu.SemaphoreType.DMA((2, 3)),
        ],
        cost_estimate=SMALL,
        name="attention_backward",
    )(lengths, bias, stat, proj, proj, proj, mixed, grad)


def bucket_of(offset):
    distance = jnp.abs(offset)
    far = 8 + sum(((distance >= bound).astype(jnp.int32) for bound in BOUNDS))
    return jnp.where(distance < 8, distance, far) + 16 * (offset > 0).astype(jnp.int32)


def bias_rows(rel_table):
    bucket = bucket_of(2 * TILE - jnp.arange(4 * TILE, dtype=jnp.int32))
    onehot = (bucket[:, None] == jnp.arange(rel_table.shape[0], dtype=jnp.int32)[None, :]).astype(jnp.float32)
    return jnp.einsum("xb,bh->hx", onehot, rel_table, precision=HIGHEST).reshape(-1, 2, 4 * TILE)


def table_sums(tiles, buckets):
    row = jnp.arange(TILE + 8, dtype=jnp.int32)[:, None]
    col = jnp.arange(3 * TILE, dtype=jnp.int32)[None, :]
    near = bucket_of(row - col + TILE)
    far = jnp.where(col < TILE, buckets - 1, buckets // 2 - 1)
    bucket = jnp.where(row < TILE, near, far)
    onehot = (bucket[:, :, None] == jnp.arange(buckets, dtype=jnp.int32)).astype(jnp.float32)
    return jnp.einsum("ghrc,rcb->bgh", tiles, onehot, precision=HIGHEST).reshape(buckets, -1)


def pack_first_kernel(place_ref, routes_ref, rows_ref, *out_refs, experts, capacity):
    target_ref = out_refs[-1]
    tokens = routes_ref.shape[1]
    routes = [routes_ref[rank : rank + 1, :] for rank in range(TOP)]
    label = lax.broadcasted_iota(jnp.int32, (experts, 1), 0)
    picks = [label == route for route in routes]
    named = jnp.where(picks[0] | picks[1], 1.0, 0.0).astype(jnp.bfloat16)
    later = lax.broadcasted_iota(jnp.int32, (1, tokens), 1)
    earlier = lax.broadcasted_iota(jnp.int32, (tokens, 1), 0)
    count = dot(named, jnp.where(earlier < later, 1.0, 0.0).astype(jnp.bfloat16))
    for rank in range(TOP):
        position = jnp.sum(jnp.where(picks[rank], count, 0.0), axis=0, keepdims=True).astype(jnp.int32)
        apart = routes[rank] ^ place_ref[0]
        apart = jnp.where(apart < experts // 2, routes[rank] & (experts // 2 - 1), apart)
        target_ref[rank : rank + 1, :] = apart * capacity + position
    other = jnp.concatenate([routes[1], routes[0]], axis=0).astype(jnp.float32) + 1.0
    pack_kernel(target_ref, rows_ref, *out_refs[:-1], other=other, capacity=capacity)


def pack_kernel(target_ref, rows_ref, *out_refs, other=None, capacity):
    rows = rows_ref[...]
    base = 0
    for out_ref in out_refs:
        stride = capacity + (0 if other is None else EXTRA)
        for at in range(0, out_ref.shape[0], stride):
            slot = lax.broadcasted_iota(jnp.int32, (capacity, 1), 0) + base
            hits = [slot == target_ref[rank : rank + 1, :] for rank in range(TOP)]
            hit = jnp.where(hits[0] | hits[1], 1.0, 0.0).astype(jnp.bfloat16)
            out_ref[at : at + capacity, :] = dot(hit, rows).astype(jnp.bfloat16)
            if other is not None:
                named = sum(jnp.where(hits[rank], other[rank : rank + 1, :], 0.0) for rank in range(TOP))
                ones = jnp.ones((EXTRA, named.shape[1]), jnp.bfloat16)
                out_ref[at + capacity : at + stride, :] = jnp.zeros((EXTRA, out_ref.shape[1]), jnp.bfloat16)
                out_ref[at + capacity : at + stride, 0:capacity] = dot(ones, named.astype(jnp.bfloat16), NT).astype(jnp.bfloat16)
            base += capacity


def block_shapes(experts, rows, width):
    half = experts // 2
    return [jax.ShapeDtypeStruct((n * rows, width), jnp.bfloat16) for n in [half] + [1] * half]


def pack_first(place, routes, rows, experts, capacity):
    blocks = block_shapes(experts, capacity + EXTRA, rows.shape[1])
    *blocks, target = pl.pallas_call(
        lambda *refs: pack_first_kernel(*refs, experts=experts, capacity=capacity),
        in_specs=[pl.BlockSpec(memory_space=pltpu.SMEM), pl.BlockSpec(), pl.BlockSpec()],
        out_shape=blocks + [jax.ShapeDtypeStruct(routes.shape, jnp.int32)],
        cost_estimate=SMALL,
        name="pack_first",
    )(place, routes, rows)
    return blocks, target


def pack(target, rows, experts, capacity):
    return pl.pallas_call(
        lambda *refs: pack_kernel(*refs, capacity=capacity),
        out_shape=block_shapes(experts, capacity, rows.shape[1]),
        cost_estimate=SMALL,
        name="pack_rows",
    )(target, rows)


def gather_rows(target_ref, gates_ref, blocks):
    total = None
    base = 0
    for block in blocks:
        slot = lax.broadcasted_iota(jnp.int32, (1, block.shape[0]), 1) + base
        share = sum(
            jnp.where(target_ref[:, rank : rank + 1] == slot, gates_ref[:, rank : rank + 1], 0.0) for rank in range(TOP)
        )
        part = dot(share.astype(jnp.bfloat16), block[...])
        total = part if total is None else total + part
        base += block.shape[0]
    return total


def output_kernel(target_ref, gates_ref, resid_ref, *refs):
    refs[-1][...] = (resid_ref[...] + gather_rows(target_ref, gates_ref, refs[:-1])).astype(jnp.bfloat16)


def combine_output(target, gates, resid, blocks):
    return pl.pallas_call(
        output_kernel,
        out_shape=jax.ShapeDtypeStruct(resid.shape, jnp.bfloat16),
        cost_estimate=MEDIUM,
        name="combine_output",
    )(target, gates, resid, *blocks)


def combine_kernel(target_ref, gates_ref, resid_ref, scale_ref, gain_ref, upstream_ref, *refs):
    blocks, (grad_ref, low_ref, gain_grad_ref) = refs[:-3], refs[-3:]
    total = gather_rows(target_ref, gates_ref, blocks)
    scale = scale_ref[...]
    unit = resid_ref[...] * scale
    gain_grad_ref[...] = jnp.sum(total * unit, axis=0, keepdims=True)
    along = total * gain_ref[...]
    inner = jnp.mean(along * unit, axis=1, keepdims=True)
    grad = upstream_ref[...].astype(jnp.float32) + scale * (along - unit * inner)
    grad_ref[...] = grad
    low_ref[...] = grad.astype(jnp.bfloat16)


def combine(target, gates, resid, scale, gain, upstream, blocks):
    tokens, width = resid.shape
    return pl.pallas_call(
        combine_kernel,
        out_shape=[
            jax.ShapeDtypeStruct((tokens, width), jnp.float32),
            jax.ShapeDtypeStruct((tokens, width), jnp.bfloat16),
            jax.ShapeDtypeStruct((1, width), jnp.float32),
        ],
        cost_estimate=SMALL,
        name="combine_back",
    )(target, gates, resid, scale, gain, upstream, *blocks)


def spans(blocks, capacity, extra=0):
    base = 0
    for block in blocks:
        for at in range(0, block.shape[0], capacity + extra):
            yield block, at, base
            base += capacity


def expert_kernel(own_ref, slope_ref, wg_ref, wu_ref, wr_ref, other_ref, *refs, ways, parts):
    blocks, refs = refs[:ways], refs[-(8 + ways) :]
    hidden_ref, gate_ref, up_ref, share_ref, router_ref = refs[:5]
    pairs, (x_ref, acc_ref, dots_ref) = refs[5 : 5 + ways], refs[5 + ways :]
    step = pl.program_id(0)
    rows = x_ref.shape[0] // parts

    @pl.when(step == 0)
    def _():
        acc_ref[...] = jnp.zeros_like(acc_ref)
        dots_ref[...] = jnp.zeros_like(dots_ref)
        base = 0
        for block in blocks:
            x_ref[base : base + block.shape[0], :] = block[...]
            base += block.shape[0]

    for part in range(parts):
        span = slice(part * rows, (part + 1) * rows)
        x = x_ref[span, :]
        gate = dot(x, wg_ref[...])
        up = dot(x, wu_ref[...])
        slope = slope_ref[span, :].astype(jnp.float32)
        square = gate * gate
        rise = 0.5 + 0.5 * jnp.tanh(gate * (CURVE + (CURVE * CUBE) * square))
        unit = gate * rise
        bend = rise + (unit - unit * rise) * (2 * CURVE + (6 * CURVE * CUBE) * square)
        hidden = (unit * up).astype(jnp.bfloat16)
        hidden_ref[span, :] = hidden
        both = hidden.astype(jnp.float32) * slope
        dots_ref[span, :] += both[:, 0:TILE] + both[:, TILE : 2 * TILE]
        gate_grad = (slope * up * bend).astype(jnp.bfloat16)
        up_grad = (slope * unit).astype(jnp.bfloat16)
        gate_ref[span, :] = gate_grad
        up_ref[span, :] = up_grad
        acc_ref[span, :] += dot(gate_grad, wg_ref[...], NT) + dot(up_grad, wu_ref[...], NT)

    @pl.when(step == pl.num_programs(0) - 1)
    def _():
        logits = dot(x_ref[...], wr_ref[...], NT)
        label = lax.broadcasted_iota(jnp.int32, (1, TILE), 1)
        mine = label == own_ref[0]
        theirs = label == other_ref[:, 0:1].astype(jnp.int32) - 1
        first = jnp.sum(jnp.where(mine, logits, 0.0), axis=1, keepdims=True)
        second = jnp.sum(jnp.where(theirs, logits, 0.0), axis=1, keepdims=True)
        top = jnp.maximum(first, second)
        first = jnp.exp(first - top)
        second = jnp.exp(second - top)
        total = first + second
        first = first / total
        second = second / total
        inner = jnp.sum(dots_ref[...], axis=1, keepdims=True)
        coef = inner * second * (jnp.where(mine, 1.0, 0.0) - jnp.where(theirs, 1.0, 0.0))
        share_ref[...] = jnp.broadcast_to(first, share_ref.shape)
        router_ref[...] = dot((first * coef).astype(jnp.bfloat16), x_ref[...], TN)
        acc_ref[...] += dot(coef.astype(jnp.bfloat16), wr_ref[...])
        base = 0
        for pair in pairs:
            pair[...] = acc_ref[base : base + pair.shape[0], :].astype(jnp.bfloat16)
            base += pair.shape[0]


def once(shape):
    return pl.BlockSpec(shape, lambda i: (0, 0), pipeline_mode=pl.Buffered(1))


def expert_rows(own, blocks, slope, wg, wu, wr, other, chunk, kept, parts=2):
    n = slope.shape[0] // 2
    d, f = wg.shape
    ways = len(blocks)
    tile = pl.BlockSpec((n, FT), lambda i: (chunk, i))
    weight = pl.BlockSpec((d, FT), lambda i: (0, i))
    fixed = lambda shape: pl.BlockSpec(shape, lambda i: (0, 0))
    hidden, gate, up, share, router, *pairs = pl.pallas_call(
        lambda *refs: expert_kernel(*refs, ways=ways, parts=parts),
        grid=(f // FT,),
        in_specs=[
            pl.BlockSpec(memory_space=pltpu.SMEM),
            tile,
            weight,
            weight,
            once((TILE, d)),
            pl.BlockSpec((n, TILE), lambda i: (chunk, 0), pipeline_mode=pl.Buffered(1)),
        ]
        + [once(block.shape) for block in blocks]
        + [pl.BlockSpec(memory_space=pl.ANY) for _ in kept],
        out_specs=[tile, tile, tile, fixed((n, TILE)), fixed((TILE, d))] + [fixed(block.shape) for block in blocks],
        out_shape=[jax.ShapeDtypeStruct((2 * n, f), jnp.bfloat16)] * 3
        + [jax.ShapeDtypeStruct((n, TILE), jnp.float32), jax.ShapeDtypeStruct((TILE, d), jnp.float32)]
        + [jax.ShapeDtypeStruct(block.shape, jnp.bfloat16) for block in blocks],
        scratch_shapes=[
            pltpu.VMEM((n, d), jnp.bfloat16),
            pltpu.VMEM((n, d), jnp.float32),
            pltpu.VMEM((n, TILE), jnp.float32),
        ],
        input_output_aliases={6 + ways + k: k for k in range(len(kept))},
        cost_estimate=SHORT if chunk else SMALL,
        name="expert_rows",
    )(own, slope, wg, wu, wr, other, *blocks, *kept)
    return (hidden, gate, up), share, router, pairs


def slope_kernel(wd_ref, *refs, capacity):
    blocks, (out_ref, other_ref, u_ref) = refs[:-3], refs[-3:]

    @pl.when(pl.program_id(0) == 0)
    def _():
        reach = -(-capacity // TILE) * TILE
        for block, at, base in spans(blocks, capacity, EXTRA):
            u_ref[base : base + capacity, :] = block[at : at + capacity, :]
            named = block[at + capacity : at + capacity + EXTRA, 0:reach].astype(jnp.float32).T
            other_ref[base : base + capacity, :] = jnp.broadcast_to(named[0:capacity, 0:1], (capacity, TILE))

    out_ref[...] = dot(u_ref[...], wd_ref[...], NT).astype(jnp.bfloat16)


def slope_rows(blocks, wd, experts, capacity):
    f, d = wd.shape
    n = experts * capacity
    return pl.pallas_call(
        lambda *refs: slope_kernel(*refs, capacity=capacity),
        grid=(f // FT,),
        in_specs=[pl.BlockSpec((FT, d), lambda i: (i, 0))] + [once(block.shape) for block in blocks],
        out_specs=[pl.BlockSpec((n, FT), lambda i: (0, i)), pl.BlockSpec((n, TILE), lambda i: (0, 0))],
        out_shape=[jax.ShapeDtypeStruct((n, f), jnp.bfloat16), jax.ShapeDtypeStruct((n, TILE), jnp.float32)],
        scratch_shapes=[pltpu.VMEM((n, d), jnp.bfloat16)],
        cost_estimate=LARGE,
        name="slope_rows",
    )(wd, *blocks)


def gate_slots(target_ref, blocks, near_ref, far_ref, capacity, extra):
    for block, at, base in spans(blocks, capacity, extra):
        share_ref, start = (near_ref, base) if base < near_ref.shape[0] else (far_ref, base - near_ref.shape[0])
        value = block[at : at + capacity, :].astype(jnp.float32) * share_ref[start : start + capacity, 0:1]
        target_ref[base : base + capacity, :] = value.astype(jnp.bfloat16)


def weight_kernel(hidden, gate, up, near_ref, far_ref, *refs, ways, copies, capacity):
    rows, raw, refs = refs[:ways], refs[ways : 2 * ways], refs[2 * ways :]
    out_ref, rows_ref, raw_ref, stage_ref, down_ref, done_ref, sent_ref = refs
    step = pl.program_id(0)
    steps = pl.num_programs(0)
    d = stage_ref.shape[2] // 2
    piece = d // copies
    part_of = out_ref.shape[0] // copies

    def whole(at):
        return pltpu.make_async_copy(
            stage_ref.at[at % 2], out_ref.at[pl.ds(pl.multiple_of(at * FT, FT), FT), 0 : 2 * d], done_ref.at[at % 2]
        )

    def small(at, part, copy):
        row = at * FT + part * 64
        column = pl.multiple_of(2 * d + row // part_of * piece, piece)
        return pltpu.make_async_copy(
            down_ref.at[at % 2, part * 64 : (part + 1) * 64, copy * piece : (copy + 1) * piece],
            out_ref.at[pl.ds(pl.multiple_of(copy * part_of + row % part_of, 64), 64), pl.ds(column, piece)],
            sent_ref.at[at % 2, part, copy],
        )

    def finish(at):
        whole(at).wait()
        for part in range(FT // 64):
            for copy in range(copies):
                small(at, part, copy).wait()

    @pl.when(step == 0)
    def _():
        gate_slots(rows_ref, rows, near_ref, far_ref, capacity, 0)
        gate_slots(raw_ref, raw, near_ref, far_ref, capacity, EXTRA)

    @pl.when(step >= 2)
    def _():
        finish(step - 2)

    slot = step % 2
    stage_ref[slot, :, 0:d] = dot(gate[...], rows_ref[...], TN).astype(jnp.bfloat16)
    stage_ref[slot, :, d : 2 * d] = dot(up[...], rows_ref[...], TN).astype(jnp.bfloat16)
    down_ref[slot] = dot(hidden[...], raw_ref[...], TN).astype(jnp.bfloat16)
    whole(step).start()
    for part in range(FT // 64):
        for copy in range(copies):
            small(step, part, copy).start()

    @pl.when(step == steps - 1)
    def _():
        finish(step - 1)
        finish(step)


def weight_grads(hidden, gate, up, shares, rows, raw, copies, capacity):
    n, f = hidden.shape
    d = rows[0].shape[1]
    ways = len(rows)
    narrow = pl.BlockSpec((n, FT), lambda i: (0, i))
    return pl.pallas_call(
        lambda *refs: weight_kernel(*refs, ways=ways, copies=copies, capacity=capacity),
        grid=(f // FT,),
        in_specs=[narrow] * 3 + [once(part.shape) for part in (*shares, *rows, *raw)],
        out_specs=pl.BlockSpec(memory_space=pl.ANY),
        out_shape=jax.ShapeDtypeStruct((f, 3 * d), jnp.bfloat16),
        scratch_shapes=[
            pltpu.VMEM((n, d), jnp.bfloat16),
            pltpu.VMEM((n, d), jnp.bfloat16),
            pltpu.VMEM((2, FT, 2 * d), jnp.bfloat16),
            pltpu.VMEM((2, FT, d), jnp.bfloat16),
            pltpu.SemaphoreType.DMA((2,)),
            pltpu.SemaphoreType.DMA((2, FT // 64, copies)),
        ],
        cost_estimate=SMALL,
        name="weight_grads",
    )(hidden, gate, up, *shares, *rows, *raw)


def result_kernel(hidden_ref, wd_ref, *refs):
    results, acc_ref = refs[:-1], refs[-1]
    step = pl.program_id(0)
    part = dot(hidden_ref[...], wd_ref[...])

    @pl.when(step == 0)
    def _():
        acc_ref[...] = part

    @pl.when(step > 0)
    def _():
        acc_ref[...] += part

    @pl.when(step == pl.num_programs(0) - 1)
    def _():
        base = 0
        for result in results:
            result[...] = acc_ref[base : base + result.shape[0], :].astype(jnp.bfloat16)
            base += result.shape[0]


def result_rows(hidden, wd, shapes):
    n, f = hidden.shape
    d = wd.shape[1]
    tile = FT * 2 if f % (FT * 2) == 0 else FT
    return pl.pallas_call(
        result_kernel,
        grid=(f // tile,),
        in_specs=[pl.BlockSpec((n, tile), lambda i: (0, i)), pl.BlockSpec((tile, d), lambda i: (i, 0))],
        out_specs=[pl.BlockSpec(shape, lambda i: (0, 0)) for shape in shapes],
        out_shape=[jax.ShapeDtypeStruct(shape, jnp.bfloat16) for shape in shapes],
        scratch_shapes=[pltpu.VMEM((n, d), jnp.float32)],
        cost_estimate=SMALL,
        name="result_rows",
    )(hidden, wd)


def shared_kernel(core_ref, first_ref, wide_ref, second_ref, narrow_ref, *refs, steps, early, unit):
    low_refs, high_refs, left_ref = refs[:2], refs[2:4], refs[4]
    step = pl.program_id(0)

    def store(value):
        own = core_ref[0] == 0

        def fill(mine_ref, away_ref):
            for group in range(mine_ref.shape[0] // unit):
                low = value[2 * group * unit : (2 * group + 1) * unit, :]
                high = value[(2 * group + 1) * unit : (2 * group + 2) * unit, :]
                span = slice(group * unit, (group + 1) * unit)
                mine_ref[span, :] = jnp.where(own, low, high).astype(jnp.bfloat16)
                away_ref[span, :] = jnp.where(own, high, low).astype(jnp.bfloat16)

        pl.when(step < early)(lambda: fill(*low_refs))
        pl.when(step >= early)(lambda: fill(*high_refs))

    @pl.when(step == 0)
    def _():
        left_ref[...] = first_ref[...].T

    @pl.when(step == steps)
    def _():
        left_ref[...] = second_ref[...].T

    @pl.when(step < steps)
    def _():
        store(dot(left_ref[...], wide_ref[...]))

    @pl.when(step >= steps)
    def _():
        store(dot(left_ref[...], narrow_ref[...]))


def shared_grads(core, first, wide, second, narrow, unit):
    tokens, rows = first.shape
    tile = 512
    steps, more = wide.shape[1] // tile, narrow.shape[1] // tile
    whole = once((tokens, rows))
    early = (steps + more) // 2
    low = pl.BlockSpec((rows // 2, tile), lambda i: (0, jnp.minimum(i, early - 1)))
    high = pl.BlockSpec((rows // 2, tile), lambda i: (0, jnp.maximum(i - early, 0)))
    shapes = [jax.ShapeDtypeStruct((rows // 2, n * tile), jnp.bfloat16) for n in (early, steps + more - early)]
    return pl.pallas_call(
        lambda *refs: shared_kernel(*refs, steps=steps, early=early, unit=unit),
        grid=(steps + more,),
        in_specs=[
            pl.BlockSpec(memory_space=pltpu.SMEM),
            whole,
            pl.BlockSpec((tokens, tile), lambda i: (0, jnp.minimum(i, steps - 1))),
            whole,
            pl.BlockSpec((tokens, tile), lambda i: (0, jnp.maximum(i - steps, 0))),
        ],
        out_specs=[low, low, high, high],
        out_shape=[shapes[0], shapes[0], shapes[1], shapes[1]],
        scratch_shapes=[pltpu.VMEM((rows, tokens), jnp.bfloat16)],
        cost_estimate=SMALL,
        name="shared_grads",
    )(core, first, wide, second, narrow)


def after(value, *before):
    return lax.optimization_barrier((value,) + before)[0]


def swap(value, axis, step):
    size = lax.axis_size(axis)
    return lax.ppermute(value, axis, [(k, k ^ step) for k in range(size)])


def parted(value, bit):
    return [lax.dynamic_index_in_dim(value, place, 0, keepdims=False) for place in (bit, 1 - bit)]


def added(first, second):
    return (first.astype(jnp.float32) + second.astype(jnp.float32)).astype(jnp.bfloat16)


def dp_halves(parts, unit):
    copies, chips = lax.axis_size("dp"), lax.axis_size("expert") // 2
    parts = [part.reshape(copies // 2, 2, chips * unit, -1) for part in parts]
    place = lax.axis_index("dp")
    cut = parts[0].shape[-1] // 2
    low = [jnp.swapaxes(part[..., :cut], 0, 1) for part in parts]
    high = [part[..., cut:] for part in parts]
    halves = []
    for pair, bit in ((low, place % 2), (high, place // 2)):
        stay, leave = zip(*(parted(part, bit) for part in pair))
        halves.append((added(*stay), added(*leave)))
    return halves


def dp_sums(halves, unit, *work):
    place = lax.axis_index("dp")
    came = [swap(leave, "dp", step) for (_, leave), step in zip(halves, (1, 2))]
    *came, _ = lax.optimization_barrier((*came, work))
    total = []
    for (stay, _), other, bit, step in zip(halves, came, (place // 2, place % 2), (2, 1)):
        mine, mine_too = (parted(part, bit) for part in (stay, other))
        leave = swap(added(mine[1], mine_too[1]), "dp", step)
        total.append(mine[0].astype(jnp.float32) + mine_too[0].astype(jnp.float32) + leave.astype(jnp.float32))
    chips = lax.axis_size("expert") // 2
    total = jnp.concatenate(total, axis=1).astype(jnp.bfloat16).reshape(chips, unit, -1)
    place = lax.axis_index("expert") // 2
    return [lax.dynamic_index_in_dim(total, place ^ step, 0, keepdims=False) for step in range(chips)]


def total_of(parts):
    return sum(part.astype(jnp.float32) for part in parts)


def chip_parts(parts, unit):
    copies, chips = lax.axis_size("dp"), lax.axis_size("expert") // 2
    place = lax.axis_index("expert") // 2
    parts = [part.reshape(copies, chips, unit, -1) for part in parts]
    return [
        added(*(lax.dynamic_index_in_dim(part, place ^ step, 1, keepdims=False) for part in parts))
        for step in range(chips)
    ]


def sent(parts, axis, stride):
    return [swap(part, axis, stride * step) if step else part for step, part in enumerate(parts)]


def on_device(
    block_input,
    routes,
    item_lengths,
    w_qkv,
    w_attn_out,
    rel_table,
    gain_attn,
    gain_moe,
    w_router,
    w_gate,
    w_up,
    w_down,
    cotangent,
):
    tokens, width = block_input.shape
    experts = w_router.shape[1]
    capacity = TOK_DEV * TOP * 5 // (4 * experts)
    slots = experts * capacity
    buckets = rel_table.shape[0]
    copies, ways = lax.axis_size("dp"), lax.axis_size("expert")
    place = lax.axis_index("expert").astype(jnp.int32)
    own = place.reshape(1)
    labels = jnp.arange(experts, dtype=jnp.int32)
    picks = [routes[:, rank : rank + 1] == labels[None, :] for rank in range(TOP)]
    places = jnp.arange(slots, dtype=jnp.int32)

    half = ways // 2
    groups = [list(range(k * half, (k + 1) * half)) for k in range(2)]

    def near(block):
        parts = block.reshape(half, -1, block.shape[1])
        parts = lax.all_to_all(parts, "expert", split_axis=0, concat_axis=0, axis_index_groups=groups, tiled=True)
        return parts.reshape(block.shape)

    def exchange(blocks, *before):
        far = [swap(block, "expert", half + step) for step, block in enumerate(blocks[1:])]
        return [near(after(blocks[0], *before))] + far

    packed, target_rows = pack_first(own, routes.T, cotangent, experts, capacity)
    target = target_rows.T
    block_input = after(block_input, *packed)
    inputs = block_input.astype(jnp.float32)
    normed, unit_one, scale_one = normalize_forward(inputs, gain_attn)
    raw = exchange(packed, scale_one)
    attn_in = normed.astype(jnp.bfloat16)
    bias = bias_rows(rel_table)
    proj = dot(attn_in, w_qkv).astype(jnp.bfloat16)
    mixed, stat = attention_forward(item_lengths, bias, proj)
    attn = dot(mixed, w_attn_out)
    resid = inputs + attn
    second, unit_two, scale_two = normalize_forward(resid, gain_moe)
    moe_in = second.astype(jnp.bfloat16)
    *packed, _ = lax.optimization_barrier((*pack(target_rows, moe_in, experts, capacity), raw))
    logits = dot(moe_in, w_router)
    chosen = jnp.stack([jnp.sum(jnp.where(pick, logits, 0.0), axis=1) for pick in picks], axis=1)
    highest = jnp.max(chosen, axis=1, keepdims=True)
    exps = jnp.exp(chosen - highest)
    gates = exps / jnp.sum(exps, axis=1, keepdims=True)
    rows = exchange(packed, gates)
    gate_weight, up_weight, down_weight = w_gate[0], w_up[0], w_down[0]
    router_rows = jnp.pad(w_router.T, ((0, TILE - experts), (0, 0)))
    slope, other = slope_rows(raw, down_weight, experts, capacity)
    weights = (gate_weight, up_weight, router_rows, other)
    kept, near_share, near_router, near_pairs = expert_rows(own, rows[:1], slope, *weights, 0, ())
    back = [near(near_pairs[0])]
    rows[1:] = [after(block, near_pairs[0]) for block in rows[1:]]
    kept, far_share, far_router, far_pairs = expert_rows(own, rows[1:], slope, *weights, 1, kept)
    back += [swap(block, "expert", half + step) for step, block in enumerate(far_pairs)]
    hidden, gate_pre_grad, up_pre_grad = kept
    shares = (near_share, far_share)
    hidden = after(hidden, back[0])
    weight_grad = weight_grads(hidden, gate_pre_grad, up_pre_grad, shares, rows, raw, copies, capacity)
    weight_sum = lax.psum_scatter(weight_grad, "dp", scatter_dimension=0, tiled=True)
    result = result_rows(after(hidden, weight_grad), down_weight, [block.shape for block in rows])
    *back, held = lax.optimization_barrier((*back, result[0]))
    result = [after(block, *back) for block in (held, *result[1:])]
    returned = exchange(result)
    resid_grad, attn_grad, gain_moe_grad = combine(
        target, gates, resid, scale_two, gain_moe.reshape(1, width), cotangent, back
    )
    mixed_grad = dot(attn_grad, w_attn_out, NT).astype(jnp.bfloat16)
    proj_grad, tiles = attention_backward(item_lengths, bias, stat, proj, mixed, mixed_grad)
    unit = width // (copies * ways)
    low, low_away, high, high_away = shared_grads(own % 2, attn_in, proj_grad, mixed, attn_grad, unit)
    dp_parts = dp_halves((low, swap(after(low_away, *returned), "expert", 1)), unit)
    z_parts = chip_parts((high, swap(after(high_away, *returned), "expert", 1)), unit)
    proj_grad, _ = lax.optimization_barrier((proj_grad, (dp_parts, z_parts)))
    table_grad = table_sums(tiles, buckets)
    router_grad = (near_router + far_router)[:experts].T
    attn_in_grad = dot(proj_grad, w_qkv, NT)
    input_norm_grad, gain_attn_grad = normalize_backward(attn_in_grad, unit_one, scale_one, gain_attn)
    input_grad = resid_grad + input_norm_grad
    output = combine_output(target, gates, after(resid, dp_parts[0][1]), returned)
    small = (table_grad.reshape(-1), gain_attn_grad, gain_moe_grad, router_grad)
    sizes = [part.size // (copies * ways) for part in small]
    together = jnp.concatenate([part.reshape(copies * ways, -1) for part in small], axis=1)
    *z_came, _ = lax.optimization_barrier((*sent(z_parts, "expert", 2), (input_grad, output, together)))
    halves = dp_sums(dp_parts, unit, input_grad, output, together, z_came)
    z_sum = total_of(z_came).astype(jnp.bfloat16)
    dp_place = lax.axis_index("dp")
    z_sum = [lax.dynamic_index_in_dim(z_sum, dp_place ^ step, 0, keepdims=False) for step in range(copies)]
    together = lax.all_to_all(together, ("dp", "expert"), split_axis=0, concat_axis=0, tiled=True)
    piece = width // copies
    down_sum = jnp.concatenate(
        [weight_sum[:, 2 * width + k * piece : 2 * width + (k + 1) * piece] for k in range(copies)], axis=0
    )
    experts_out = (
        weight_sum[:, :width].astype(jnp.float32).T[None],
        weight_sum[:, width : 2 * width].astype(jnp.float32).T[None],
        down_sum.astype(jnp.float32)[None],
    )
    low, high = sent(halves, "expert", 2), sent(z_sum, "dp", 1)
    (low, high), together, _ = lax.optimization_barrier(((low, high), together, experts_out))
    together = jnp.sum(together, axis=0)
    at = [sum(sizes[:k]) for k in range(5)]
    table_sum, attn_sum, moe_sum, router_sum = [together[at[k] : at[k + 1]] for k in range(4)]
    sums = jnp.concatenate([total_of(low), total_of(high)], axis=1)
    return (
        output,
        input_grad,
        sums[:, : 3 * width],
        sums[:, 3 * width :],
        table_sum,
        attn_sum,
        moe_sum,
        router_sum.reshape(-1, experts),
        *experts_out,
    )


def solution(mesh):
    return jax.shard_map(
        on_device,
        mesh=mesh,
        in_specs=(
            P(("dp", "expert"), None),
            P(("dp", "expert"), None),
            P(("dp", "expert"), None),
            P(),
            P(),
            P(),
            P(),
            P(),
            P(),
            P("expert", None, None),
            P("expert", None, None),
            P("expert", None, None),
            P(("dp", "expert"), None),
        ),
        out_specs=(
            P(("dp", "expert"), None),
            P(("dp", "expert"), None),
            P(("dp", "expert"), None),
            P(("dp", "expert"), None),
            P(("dp", "expert")),
            P(("dp", "expert")),
            P(("dp", "expert")),
            P(("dp", "expert"), None),
            P("expert", None, "dp"),
            P("expert", None, "dp"),
            P("expert", None, "dp"),
        ),
        check_vma=False,
    )
```
